128 devices in a mesh: tok: 16 (over z, x), head: 8 (over y, core).
Axes of the slice: x: 4, y: 4, z: 4, core: 2. Of those that a mesh axis runs over, the one named last changes fastest.
Arguments:
- tokens: bfloat16 [4096, 2048], P('tok', 'head'), may hold values from -6 to 6
- input_weight: bfloat16 [2048, 6144], P(None, 'head'), may hold values from -0.125 to 0.125
- output_weight: bfloat16 [2048, 2048], P('head'), may hold values from -0.5 to 0.5
- head_gain: float32 [2048], P('head'), may hold values from 0.1 to 1.9
- query_lambda_one: float32 [128], replicated, may hold values from -1.2 to 1.2
- key_lambda_one: float32 [128], replicated, may hold values from -1.2 to 1.2
- query_lambda_two: float32 [128], replicated, may hold values from -1.2 to 1.2
- key_lambda_two: float32 [128], replicated, may hold values from -1.2 to 1.2
- cache_pool: bfloat16 [1024, 8, 128, 512], P('tok', 'head'), may hold values from -160 to 160
- page_table: int32 [4096, 8], P('tok'), may hold values from 0 to 63, as said below
- cache_length: int32 [4096], P('tok'), may hold values from 1 to 1024, as said below
- cache_owner: int32 [4096, 1], P('tok'), may hold values from 0 to 15, as said below
Outputs:
- mixed: bfloat16 [4096, 2048], P('tok', 'head')
The draws below stay inside these ranges and needn't reach their ends.
Inputs may be any that keep to these rules, and one draw needn't show every extreme that they name: `page_table`: entries index the pool pages of the request's cache owner, counted from that owner's first page. A request's first entry is one of that owner's first 8 pages and may be shared with other requests of the same owner (a common prompt); every other entry that covers a cached position belongs to that request alone; entries past the cached length are read by nobody. `cache_length`: some request has exactly 1024 cached tokens in every draw. `cache_owner`: among the 256 requests of one index of tok, at most 32 name the same owner; some owner is named by exactly 32 requests of every index.
All inputs are finite; a program needn't handle non-finite values.
Results may differ from the reference program's by a relative error of at most 0.025.
Values may be sent and summed in bfloat16 or wider, within the bound.
A program may use at most 128 MiB of HBM per device.

```python
import math
import jax
import jax.numpy as jnp
from jax import lax

D = 2048
HEADS = 8
QK = 128
VDIM = 256
PAGE = 128
R_DEV = 256
LEN_MAX = 1024
PAGES_DEV = 64
CAP = 32
MAXP = 8
REQS = 4096
POOL = 1024
N_TOK = 16


def draw_cache_pool(key, part):
    base_key = jax.random.fold_in(jax.random.fold_in(key, 11), 0)
    layout = (POOL, HEADS, PAGE, 2 * QK + VDIM)
    is_key = jnp.arange(2 * QK + VDIM) < 2 * QK
    column_scale = jnp.where(is_key, 1.0, 1.0 / 32.0).astype(jnp.float32)
    values = jnp.clip(jax.random.normal(base_key, layout, jnp.float32), -4.0, 4.0)
    values = values * column_scale
    return values.astype(jnp.bfloat16)


def cache_layout(key):
    owner_key, length_key, group_key, fill_key, order_key = jax.random.split(jax.random.fold_in(key, 37), 5)
    level_key, favored_key, noise_key, shuffle_key = jax.random.split(owner_key, 4)
    count_of_slots = N_TOK * CAP
    priority_levels = jax.random.randint(level_key, (N_TOK,), 0, 4).astype(jnp.int32)
    preferred_owner = jax.random.randint(favored_key, (), 0, N_TOK).astype(jnp.int32)
    owner_per_slot = (jnp.arange(count_of_slots) // CAP).astype(jnp.int32)
    extra_credit = priority_levels[owner_per_slot] * 32768 + jnp.where(owner_per_slot == preferred_owner, 524288, 0).astype(jnp.int32)
    random_jitter = jax.random.randint(noise_key, (N_TOK, count_of_slots), 0, 65536).astype(jnp.int32)
    owner_scores = (random_jitter + extra_credit[None, :]) * count_of_slots + jnp.arange(count_of_slots).astype(jnp.int32)[None, :]
    picked = lax.top_k(owner_scores, R_DEV)[1]
    block_owners = owner_per_slot[picked]
    shuffles = jax.vmap(lambda one_key: jax.random.permutation(one_key, R_DEV))(jax.random.split(shuffle_key, N_TOK))
    block_owners = jnp.take_along_axis(block_owners, shuffles.astype(jnp.int32), axis=1)
    owners = block_owners.reshape(REQS).astype(jnp.int32)
    desired = jax.random.randint(length_key, (REQS,), 1, LEN_MAX + 1).astype(jnp.int32)
    desired = desired.at[0].set(LEN_MAX)
    rest = 1 + jax.random.permutation(order_key, REQS - 1).astype(jnp.int32)
    visit = jnp.concatenate([jnp.zeros((1,), jnp.int32), rest])
    shared_pages = PAGES_DEV // 8
    private_pages = PAGES_DEV - shared_pages

    def allot(used, row):
        owner = owners[row]
        wanted = desired[row]
        extra = (wanted + PAGE - 1) // PAGE - 1
        extra = jnp.minimum(extra, private_pages - used[owner])
        length = jnp.minimum(wanted, (extra + 1) * PAGE)
        first_free = shared_pages + used[owner]
        return (used.at[owner].add(extra), (length, first_free, extra))
    _, (lengths_seen, firsts_seen, extras_seen) = lax.scan(allot, jnp.zeros((N_TOK,), jnp.int32), visit)
    lengths = jnp.zeros((REQS,), jnp.int32).at[visit].set(lengths_seen)
    firsts = jnp.zeros((REQS,), jnp.int32).at[visit].set(firsts_seen)
    extras = jnp.zeros((REQS,), jnp.int32).at[visit].set(extras_seen)
    prompt_page = jax.random.randint(group_key, (REQS,), 0, shared_pages).astype(jnp.int32)
    filler = jax.random.randint(fill_key, (REQS, MAXP), 0, PAGES_DEV).astype(jnp.int32)
    column = jnp.arange(MAXP).astype(jnp.int32)[None, :]
    private_entry = firsts[:, None] + column - 1
    table = jnp.where(column == 0, prompt_page[:, None], jnp.where(column - 1 < extras[:, None], private_entry, filler))
    return (owners, lengths, table.astype(jnp.int32))


def draw_cache_owner(key, part):
    owners, lengths, table = cache_layout(key)
    return owners[:, None]


def draw_cache_length(key, part):
    owners, lengths, table = cache_layout(key)
    return lengths


def draw_page_table(key, part):
    owners, lengths, table = cache_layout(key)
    return table


def block_levels(rng, extent, pieces, low, top_value):
    loudness, own = 1.0, jax.random.fold_in(rng, 6)
    for axis_at, shards_of in pieces:
        draws = jnp.exp(jax.random.uniform(jax.random.fold_in(own, axis_at), (shards_of,), jnp.float32, low / len(pieces), top_value / len(pieces)))
        loudness = loudness * jnp.repeat(draws, extent[axis_at] // shards_of).reshape([-1 if axis == axis_at else 1 for axis in range(len(extent))])
    return loudness


def scatter_about(rng, extent, width, limit, pieces=(), dtype=jnp.bfloat16):
    level = block_levels(rng, extent, pieces, -0.22, 0.18) if pieces else 1.0
    entries = jax.random.normal(rng, extent, jnp.float32) * width * level
    return jnp.minimum(jnp.maximum(entries, -limit), limit).astype(dtype)


def setup_inputs(seed: int = 0) -> dict:
    keys = jax.random.split(jax.random.key(seed), 13)
    tokens = scatter_about(keys[0], (REQS, D), 1.0, 6.0, ((0, 16), (1, 8)))
    input_weight = scatter_about(keys[1], (D, HEADS * (4 * QK + VDIM)), D ** -0.5, 0.125, ((1, 8),))
    output_weight = scatter_about(keys[2], (HEADS * VDIM, D), (HEADS * VDIM // 16) ** -0.5, 0.5, ((0, 8),))
    head_gain = jnp.clip(1.0 + 0.18 * jax.random.normal(keys[3], (HEADS * VDIM,), jnp.float32), 0.1, 1.9)
    query_lambda_one = scatter_about(keys[4], (QK,), 0.3, 1.2, (), jnp.float32)
    key_lambda_one = scatter_about(keys[5], (QK,), 0.3, 1.2, (), jnp.float32)
    query_lambda_two = scatter_about(keys[6], (QK,), 0.3, 1.2, (), jnp.float32)
    key_lambda_two = scatter_about(keys[7], (QK,), 0.3, 1.2, (), jnp.float32)
    cache_pool = draw_cache_pool(jax.random.fold_in(keys[12], 71), 0)
    page_table = draw_page_table(jax.random.fold_in(keys[12], 71), 0)
    cache_length = draw_cache_length(jax.random.fold_in(keys[12], 71), 0)
    cache_owner = draw_cache_owner(jax.random.fold_in(keys[12], 71), 0)
    return dict(tokens=tokens, input_weight=input_weight, output_weight=output_weight, head_gain=head_gain, query_lambda_one=query_lambda_one, key_lambda_one=key_lambda_one, query_lambda_two=query_lambda_two, key_lambda_two=key_lambda_two, cache_pool=cache_pool, page_table=page_table, cache_length=cache_length, cache_owner=cache_owner)


lambda_init = 0.8
norm_eps = 1e-05

def softmax_mix(self_score, owner_scores, value_new, values, is_valid):
    joined = jnp.concatenate([self_score[:, None], jnp.where(is_valid[None, :], owner_scores, -jnp.inf)], axis=1)
    top_score = lax.optimization_barrier(jnp.max(joined, axis=1, keepdims=True))
    weights = jnp.exp(joined - top_score)
    total_sum = lax.optimization_barrier(jnp.sum(weights, axis=1))
    rounded_counts = lax.optimization_barrier(weights.astype(jnp.bfloat16))
    stacked_rows = jnp.concatenate([value_new[:, None, :], values], axis=1).astype(jnp.float32)
    summed_scores = jnp.einsum('nu,nus->ns', rounded_counts.astype(jnp.float32), stacked_rows)
    return summed_scores / total_sum[:, None]

def reference(tokens, input_weight, output_weight, head_gain, query_lambda_one, key_lambda_one, query_lambda_two, key_lambda_two, cache_pool, page_table, cache_length, cache_owner):
    projected = jnp.dot(tokens, input_weight, preferred_element_type=jnp.float32).astype(jnp.bfloat16)
    projected = projected.reshape(REQS, HEADS, 4 * QK + VDIM)
    lambda_mix = jnp.exp(jnp.sum(query_lambda_one * key_lambda_one)) - jnp.exp(jnp.sum(query_lambda_two * key_lambda_two)) + lambda_init
    gain_rows = head_gain.reshape(HEADS, VDIM)
    scale_qk = 1.0 / math.sqrt(QK)
    positions = jnp.arange(LEN_MAX).astype(jnp.int32)

    def per_request(request_items):
        request_row, page_numbers, length, owner_id = request_items
        query_one = request_row[:, 0:QK].astype(jnp.float32)
        query_two = request_row[:, QK:2 * QK].astype(jnp.float32)
        key_one = request_row[:, 2 * QK:3 * QK].astype(jnp.float32)
        key_two = request_row[:, 3 * QK:4 * QK].astype(jnp.float32)
        value_new = request_row[:, 4 * QK:]
        page_ids = (owner_id * PAGES_DEV + page_numbers).astype(jnp.int32)
        cached_keys = cache_pool[page_ids]
        cached_keys = jnp.transpose(cached_keys, (1, 0, 2, 3)).reshape(HEADS, LEN_MAX, 2 * QK + VDIM)
        key_floats = cached_keys[:, :, 0:2 * QK].astype(jnp.float32)
        is_valid = positions < length
        score_one = jnp.einsum('hd,hkd->hk', query_one, key_floats[:, :, 0:QK]) * scale_qk
        score_two = jnp.einsum('hd,hkd->hk', query_two, key_floats[:, :, QK:2 * QK]) * scale_qk
        self_one = lax.optimization_barrier(jnp.sum(query_one * key_one, axis=1)) * scale_qk
        self_two = lax.optimization_barrier(jnp.sum(query_two * key_two, axis=1)) * scale_qk
        values = cached_keys[:, :, 2 * QK:]
        attn_one = softmax_mix(self_one, score_one, value_new, values, is_valid)
        attn_two = softmax_mix(self_two, score_two, value_new, values, is_valid)
        mixed = attn_one - lambda_mix * attn_two
        scale_rms = lax.rsqrt(lax.optimization_barrier(jnp.mean(mixed * mixed, axis=-1, keepdims=True)) + norm_eps)
        normed = mixed * scale_rms * gain_rows * (1.0 - lambda_init)
        return normed.reshape(HEADS * VDIM).astype(jnp.bfloat16)
    head_out = lax.map(per_request, (projected, page_table, cache_length, cache_owner[:, 0]))
    return jnp.dot(head_out, output_weight, preferred_element_type=jnp.float32).astype(jnp.bfloat16)
```

```python
import functools
import math

import jax
import jax.numpy as jnp
from jax import lax
from jax.experimental import pallas as pl
from jax.experimental.pallas import tpu as pltpu
from jax.sharding import PartitionSpec as P

QK = 128
VDIM = 256
PAGE = 128
CAP = 32
SHARED = 8
MAXP = 8
GROUP = 16
LANES = 128
ROW = 2 * QK + LANES

lambda_init = 0.8
norm_eps = 1e-05
NEG = -1e30
SCALE = math.log2(math.e) / math.sqrt(QK)
MESH = pl.DeviceIdType.MESH
F32 = jnp.float32
BF16 = jnp.bfloat16


def iota(shape, dim):
    return lax.broadcasted_iota(jnp.int32, shape, dim)


def iota_f(shape, dim):
    return iota(shape, dim).astype(F32)


def dot(a, b):
    return jnp.dot(a, b, preferred_element_type=F32)


def dot_nt(a, b):
    return lax.dot_general(a, b, (((1,), (1,)), ((), ())), preferred_element_type=F32)


def dot_tn(a, b):
    return lax.dot_general(a, b, (((0,), (0,)), ((), ())), preferred_element_type=F32)


def to_row(column, count):
    eye = iota((count, LANES), 0) == iota((count, LANES), 1)
    return jnp.sum(jnp.where(eye, column, 0.0), axis=0, keepdims=True)


def to_column(row, count):
    eye = iota((count, LANES), 0) == iota((count, LANES), 1)
    return jnp.sum(jnp.where(eye, row, 0.0), axis=1, keepdims=True)


def split3(value):
    high = value.astype(BF16).astype(F32)
    rest = value - high
    middle = rest.astype(BF16).astype(F32)
    return high, middle, rest - middle


def step_kernel(
    sizes,
    tokens,
    w_in,
    w_out,
    pool,
    gain,
    lq1,
    lk1,
    lq2,
    lk2,
    table,
    length,
    owner,
    out,
    x,
    win_v,
    wout_v,
    pool_v,
    place,
    place_t,
    meta0,
    rows_v,
    proj,
    v_new,
    sendq,
    recvq,
    sendr,
    recvr,
    match,
    full,
    part,
    first_a,
    first_b,
    page0,
    priv_a,
    priv_b,
    u_first,
    acc,
    mix_send,
    mix_recv,
    mix_own,
    ring_send,
    ring_recv,
    local_sem,
    ag_send,
    ag_recv,
    q_send,
    q_recv,
    r_send,
    r_recv,
    m_send,
    m_recv,
    g_send,
    g_recv,
):
    n_tok, n_head, count, features = sizes
    slots = n_tok * CAP
    pages = pool.shape[0]
    half = count // 2
    ny = n_head // 2
    me_t = lax.axis_index("tok")
    me_h = lax.axis_index("head")
    y, core = me_h // 2, me_h % 2
    up, down, far = (y + 1) % ny, (y + ny - 1) % ny, (y + 2) % ny

    def head_id(yy, cc):
        return yy * 2 + cc

    sib = head_id(y, 1 - core)
    h_up, h_down, h_far = head_id(up, core), head_id(down, core), head_id(far, core)

    barrier = pltpu.get_barrier_semaphore()
    for peer in (sib, h_up, h_down):
        pl.semaphore_signal(barrier, inc=1, device_id=(me_t, peer), device_id_type=MESH)
    for k in range(1, n_tok):
        pl.semaphore_signal(
            barrier, inc=1, device_id=((me_t + k) % n_tok, me_h), device_id_type=MESH
        )

    local_x = pltpu.make_async_copy(tokens, x.at[me_h], local_sem.at[0])
    local_x.start()
    load_win = pltpu.make_async_copy(w_in, win_v, local_sem.at[1])
    load_win.start()
    load_pool = pltpu.make_async_copy(pool, pool_v, local_sem.at[2])
    load_pool.start()
    load_wout = []
    for h in range(n_head):
        load = pltpu.make_async_copy(
            w_out.at[:, pl.ds(h * features, features)], wout_v.at[h], local_sem.at[3 + h]
        )
        load.start()
        load_wout.append(load)

    own = owner[...]
    named = own == iota((count, LANES), 1)
    earlier = (iota((count, count), 0) > iota((count, count), 1)).astype(F32).astype(BF16)
    before = dot(earlier, named.astype(F32).astype(BF16))
    rank = jnp.sum(jnp.where(named, before, 0.0), axis=1, keepdims=True)
    slot = own * CAP + rank.astype(jnp.int32)
    eye = iota((count, count), 0) == iota((count, count), 1)
    slot_row = jnp.sum(jnp.where(eye, slot, 0), axis=0, keepdims=True)
    place[...] = (iota((slots, count), 0) == slot_row).astype(F32).astype(BF16)
    place_t[...] = (iota((count, slots), 1) == slot).astype(F32).astype(BF16)
    length_c = jnp.sum(jnp.where(eye, length[...], 0), axis=1, keepdims=True)
    lane = iota((count, LANES), 1)
    spread = (iota((MAXP, LANES), 0) == iota((MAXP, LANES), 1)).astype(F32).astype(BF16)
    meta = dot(table[...].astype(F32).astype(BF16), spread)
    high = (length_c // 8).astype(F32)
    low = (length_c % 8).astype(F32)
    meta0[...] = meta + jnp.where(lane == 8, high, 0.0) + jnp.where(lane == 9, low, 0.0)

    pl.semaphore_wait(barrier, 3 + n_tok - 1)

    first, second = pl.ds(0, half), pl.ds(half, half)

    def share(index, source, part_rows, target):
        return pltpu.make_async_remote_copy(
            src_ref=x.at[source, part_rows],
            dst_ref=x.at[source, part_rows],
            send_sem=ag_send.at[index],
            recv_sem=ag_recv.at[index],
            device_id=(me_t, target),
            device_id_type=MESH,
        )

    local_x.wait()
    copies = {}

    def go(index, source, part_rows, target):
        copies[index] = share(index, source, part_rows, target)
        copies[index].start()

    go(0, me_h, first, h_up)
    go(2, me_h, second, h_down)
    go(1, me_h, second, h_up)
    go(3, me_h, first, h_down)
    go(6, me_h, pl.ds(0, count), sib)

    def add_chunk(source, start=False):
        rows = pl.ds(pl.multiple_of(source * features, features), features)
        update = dot(x[source], win_v[rows, 0 : 4 * QK])
        proj[...] = update if start else proj[...] + update

    load_win.wait()
    add_chunk(me_h, True)
    copies[0].wait_recv()
    go(4, h_down, first, h_up)
    go(7, h_down, first, sib)
    copies[2].wait_recv()
    go(5, h_up, second, h_down)
    go(10, h_up, second, sib)
    copies[6].wait_recv()
    add_chunk(sib)
    copies[1].wait_recv()
    go(8, h_down, second, sib)
    add_chunk(h_down)
    copies[3].wait_recv()
    go(9, h_up, first, sib)
    add_chunk(h_up)
    copies[4].wait_recv()
    go(11, h_far, first, sib)
    copies[5].wait_recv()
    go(12, h_far, second, sib)
    add_chunk(h_far)
    copies[7].wait_recv()
    copies[8].wait_recv()
    add_chunk(head_id(down, 1 - core))
    copies[9].wait_recv()
    copies[10].wait_recv()
    add_chunk(head_id(up, 1 - core))
    copies[11].wait_recv()
    copies[12].wait_recv()
    add_chunk(head_id(far, 1 - core))

    qk = proj[...].astype(BF16)
    qf = qk.astype(F32)
    self_a = jnp.sum(qf[:, 0:QK] * qf[:, 2 * QK : 3 * QK], axis=1, keepdims=True) * SCALE
    self_b = jnp.sum(qf[:, QK : 2 * QK] * qf[:, 3 * QK :], axis=1, keepdims=True) * SCALE
    meta = meta0[...]
    for index, term in enumerate(split3(self_a) + split3(self_b)):
        meta = meta + jnp.where(lane == 10 + index, term, 0.0)
    rows_v[:, 0 : 2 * QK] = qk[:, 0 : 2 * QK]
    rows_v[:, 2 * QK :] = meta.astype(BF16)
    sendq[...] = dot(place[...], rows_v[...]).astype(BF16).reshape(n_tok, CAP, ROW)
    q_copies = []
    for k in range(1, n_tok):
        target = (me_t + k) % n_tok
        copy = pltpu.make_async_remote_copy(
            src_ref=sendq.at[target],
            dst_ref=recvq.at[me_t],
            send_sem=q_send.at[k],
            recv_sem=q_recv.at[k],
            device_id=(target, me_h),
            device_id_type=MESH,
        )
        copy.start()
        q_copies.append(copy)
    recvq[me_t] = sendq[me_t]

    value = jnp.zeros((count, VDIM), F32)
    for h in range(n_head):
        value = value + dot(x[h], win_v[h * features : (h + 1) * features, 4 * QK :])
    v_new[...] = value.astype(BF16)
    lam = (
        jnp.exp(jnp.sum(lq1[...] * lk1[...], axis=1, keepdims=True))
        - jnp.exp(jnp.sum(lq2[...] * lk2[...], axis=1, keepdims=True))
        + lambda_init
    )
    load_pool.wait()
    for copy in q_copies:
        copy.wait_recv()

    blocks = slots // PAGE
    per = PAGE // CAP
    lane_f = iota_f((PAGE, LANES), 1)

    def block_rows(ref, i):
        return ref[pl.ds(i * per, per)].reshape(PAGE, ROW)

    def cut(i):
        return pl.ds(i * PAGE, PAGE)

    lengths, selfs = [], []
    for i in range(blocks):
        info = block_rows(recvq, i)[:, 2 * QK :].astype(F32)
        cached = info[:, 8:9] * 8.0 + info[:, 9:10]
        hit_any = jnp.zeros((PAGE, LANES), F32)
        hit_full = jnp.zeros((PAGE, LANES), F32)
        hit_part = jnp.zeros((PAGE, LANES), F32)
        for j in range(1, MAXP):
            left = cached - float(PAGE * j)
            number = jnp.where(left > 0.0, info[:, j : j + 1], -1.0)
            hit = number == lane_f
            whole = jnp.where(left >= float(PAGE), 1.0, 0.0)
            rest = jnp.where(left >= float(PAGE), 0.0, left)
            hit_any = jnp.where(hit, 1.0, hit_any)
            hit_full = jnp.where(hit, hit_full + whole, hit_full)
            hit_part = jnp.where(hit, hit_part + rest, hit_part)
        match[cut(i)] = hit_any.astype(BF16)
        full[cut(i)] = hit_full.astype(BF16)
        part[cut(i)] = hit_part.astype(BF16)
        page0[cut(i)] = jnp.broadcast_to(info[:, 0:1], (PAGE, LANES))
        lengths.append(cached)
        selfs.append(
            (
                info[:, 10:11] + info[:, 11:12] + info[:, 12:13],
                info[:, 13:14] + info[:, 14:15] + info[:, 15:16],
            )
        )

    queries = recvq[...].reshape(slots, ROW)[:, 0 : 2 * QK]
    ones = jnp.ones((slots, LANES), F32).astype(BF16)
    page_q = dot_tn(match[...], queries)[0:pages].astype(BF16)
    page_full = dot_tn(full[...], ones)[0:pages]
    page_part = dot_tn(part[...], ones)[0:pages]
    times = page_full + jnp.where(iota_f((pages, LANES), 1) < page_part, 1.0, 0.0)

    for g in range(0, SHARED, 2):
        keys = pool_v[g : g + 2].reshape(2 * PAGE, 2 * QK + VDIM)
        for first_ref, lo in ((first_a, 0), (first_b, QK)):
            score = dot_nt(queries[:, lo : lo + QK], keys[:, lo : lo + QK])
            chosen = jnp.where(page0[...] == float(g), score[:, 0:PAGE], score[:, PAGE:])
            if g == 0:
                first_ref[...] = chosen
            else:
                first_ref[...] = jnp.where(page0[...] >= float(g), chosen, first_ref[...])

    row = iota((GROUP, LANES), 0)

    def private_scores(g, carry):
        keys = pool_v[pl.ds(g * GROUP, GROUP)].reshape(GROUP * PAGE, 2 * QK + VDIM)
        mine = pl.ds(pl.multiple_of(g * GROUP, GROUP), GROUP)
        for ref, lo in ((priv_a, 0), (priv_b, QK)):
            score = dot_nt(acc_q[mine, lo : lo + QK], keys[:, lo : lo + QK])
            chosen = score[:, 0:PAGE]
            for i in range(1, GROUP):
                chosen = jnp.where(row == i, score[:, i * PAGE : (i + 1) * PAGE], chosen)
            ref[mine] = chosen
        return carry

    acc_q = rows_v
    rows_v[0:pages, 0 : 2 * QK] = page_q
    lax.fori_loop(0, pages // GROUP, private_scores, 0)

    priv = []
    for ref in (priv_a, priv_b):
        score = jnp.where(times > 0.0, ref[...] * SCALE, NEG)
        priv.append((score, to_row(jnp.max(score, axis=1, keepdims=True), pages)))

    tops = []
    page_top = [jnp.zeros((1, LANES), F32) for _ in range(2)]
    for i in range(blocks):
        hit = match[cut(i)].astype(F32) > 0.0
        for m, ref in enumerate((first_a, first_b)):
            score = jnp.where(lane_f < lengths[i], ref[cut(i)] * SCALE, NEG)
            ref[cut(i)] = score
            best = jnp.maximum(score, jnp.where(hit, priv[m][1], NEG))
            top = jnp.maximum(jnp.max(best, axis=1, keepdims=True), selfs[i][m])
            page_top[m] = page_top[m] + jnp.sum(
                jnp.where(hit, top, 0.0), axis=0, keepdims=True
            )
            tops.append(top)

    page_weight, page_sum = [], []
    for m in range(2):
        top = to_column(page_top[m], pages)
        weight = jnp.where(times > 0.0, jnp.exp2(priv[m][0] - top) * times, 0.0)
        page_weight.append(weight)
        page_sum.append(to_row(jnp.sum(weight, axis=1, keepdims=True), pages))

    page_coef = [jnp.zeros((1, LANES), F32) for _ in range(2)]
    for i in range(blocks):
        hit = match[cut(i)].astype(F32) > 0.0
        mixed, own_coef = None, None
        for m, ref in enumerate((first_a, first_b)):
            top = tops[2 * i + m]
            weight = jnp.exp2(ref[cut(i)] - top)
            new = jnp.exp2(selfs[i][m] - top)
            total = new + jnp.sum(
                weight + jnp.where(hit, page_sum[m], 0.0), axis=1, keepdims=True
            )
            coef = 1.0 / total if m == 0 else -lam / total
            page_coef[m] = page_coef[m] + jnp.sum(
                jnp.where(hit, coef, 0.0), axis=0, keepdims=True
            )
            mixed = weight * coef if m == 0 else mixed + weight * coef
            own_coef = new * coef if m == 0 else own_coef + new * coef
        u_first[cut(i)] = mixed.astype(BF16)
        coef_high = own_coef.astype(BF16).astype(F32)
        coefs = jnp.where(lane_f == 0.0, coef_high, 0.0) + jnp.where(
            lane_f == 1.0, own_coef - coef_high, 0.0
        )
        sendr[pl.ds(i * per, per), :, VDIM:] = coefs.astype(BF16).reshape(per, CAP, LANES)

    page_mix = page_weight[0] * to_column(page_coef[0], pages) + page_weight[1] * to_column(
        page_coef[1], pages
    )
    priv_a[...] = page_mix
    for g in range(0, SHARED, 2):
        values = pool_v[g : g + 2].reshape(2 * PAGE, 2 * QK + VDIM)[:, 2 * QK :]
        weight = u_first[...].astype(F32)
        pair = jnp.concatenate(
            [jnp.where(page0[...] == float(g + i), weight, 0.0) for i in range(2)], axis=1
        ).astype(BF16)
        update = dot(pair, values)
        acc[...] = update if g == 0 else acc[...] + update

    def private_values(g, carry):
        values = pool_v[pl.ds(g * GROUP, GROUP)].reshape(GROUP * PAGE, 2 * QK + VDIM)[:, 2 * QK :]
        mine = pl.ds(pl.multiple_of(g * GROUP, GROUP), GROUP)
        weight = priv_a[mine]
        wide = jnp.concatenate(
            [jnp.where(row == i, weight, 0.0) for i in range(GROUP)], axis=1
        ).astype(BF16)
        mix_own[0, mine] = dot(wide, values)
        return carry

    lax.fori_loop(0, pages // GROUP, private_values, 0)
    page_out = mix_own[0, 0:pages]
    page_high = page_out.astype(BF16)
    page_low = (page_out - page_high.astype(F32)).astype(BF16)
    chosen_pages = match[...][:, 0:pages]
    result = acc[...] + dot(chosen_pages, page_high) + dot(chosen_pages, page_low)
    sendr[:, :, 0:VDIM] = result.astype(BF16).reshape(n_tok, CAP, VDIM)

    r_copies = []
    for k in range(1, n_tok):
        target = (me_t + k) % n_tok
        copy = pltpu.make_async_remote_copy(
            src_ref=sendr.at[target],
            dst_ref=recvr.at[me_t],
            send_sem=r_send.at[k],
            recv_sem=r_recv.at[k],
            device_id=(target, me_h),
            device_id_type=MESH,
        )
        copy.start()
        r_copies.append(copy)
    recvr[me_t] = sendr[me_t]
    for load in load_wout:
        load.wait()
    for copy in r_copies:
        copy.wait_recv()

    got = dot(place_t[...], recvr[...].reshape(slots, ROW))
    coef = got[:, VDIM : VDIM + 1] + got[:, VDIM + 1 : VDIM + 2]
    mixed = got[:, 0:VDIM] + coef * v_new[...].astype(F32)
    scale = lax.rsqrt(jnp.mean(mixed * mixed, axis=1, keepdims=True) + norm_eps)
    head_out = (mixed * scale * gain[...] * (1.0 - lambda_init)).astype(BF16)

    order = (far, up, down, y)
    mixes = []
    for k, yy in enumerate(order):
        mix_send[k] = dot(head_out, wout_v[head_id(yy, 1 - core)]).astype(BF16)
        copy = pltpu.make_async_remote_copy(
            src_ref=mix_send.at[k],
            dst_ref=mix_recv.at[k],
            send_sem=m_send.at[k],
            recv_sem=m_recv.at[k],
            device_id=(me_t, sib),
            device_id_type=MESH,
        )
        copy.start()
        mixes.append(copy)
    for k, yy in enumerate(order):
        mix_own[k] = dot(head_out, wout_v[head_id(yy, core)])

    rings = {}

    def ring(index, value, target):
        ring_send[index] = value.astype(BF16)
        rings[index] = pltpu.make_async_remote_copy(
            src_ref=ring_send.at[index],
            dst_ref=ring_recv.at[index],
            send_sem=g_send.at[index],
            recv_sem=g_recv.at[index],
            device_id=(me_t, target),
            device_id_type=MESH,
        )
        rings[index].start()

    def chip_sum(k):
        mixes[k].wait_recv()
        return mix_own[k] + mix_recv[k].astype(F32)

    total = chip_sum(0)
    ring(0, total[0:half], h_up)
    ring(1, total[half:], h_down)
    to_up = chip_sum(1)
    ring(2, to_up[half:], h_up)
    to_down = chip_sum(2)
    ring(3, to_down[0:half], h_down)
    rings[0].wait_recv()
    ring(4, to_up[0:half] + ring_recv[0].astype(F32), h_up)
    rings[1].wait_recv()
    ring(5, to_down[half:] + ring_recv[1].astype(F32), h_down)
    total = chip_sum(3)
    for index in (2, 3, 4, 5):
        rings[index].wait_recv()
    out[0:half] = (
        total[0:half] + ring_recv[4].astype(F32) + ring_recv[3].astype(F32)
    ).astype(BF16)
    out[half:] = (total[half:] + ring_recv[2].astype(F32) + ring_recv[5].astype(F32)).astype(BF16)

    for index in range(13):
        copies[index].wait_send()
    for copy in q_copies + r_copies + mixes:
        copy.wait_send()
    for index in range(6):
        rings[index].wait_send()


def on_device(sizes, tokens, w_in, w_out, gain, lq1, lk1, lq2, lk2, pool, table, length, owner):
    n_tok, n_head, count, features = sizes
    slots = n_tok * CAP
    pages = pool.shape[0]
    half = count // 2
    vmem = pl.BlockSpec(memory_space=pltpu.VMEM)
    hbm = pl.BlockSpec(memory_space=pl.ANY)
    dma = pltpu.SemaphoreType.DMA
    return pl.pallas_call(
        functools.partial(step_kernel, sizes),
        out_shape=jax.ShapeDtypeStruct((count, features), BF16),
        in_specs=[hbm] * 4 + [vmem] * 8,
        out_specs=vmem,
        scratch_shapes=[
            pltpu.VMEM((n_head, count, features), BF16),
            pltpu.VMEM(w_in.shape, BF16),
            pltpu.VMEM((n_head, VDIM, features), BF16),
            pltpu.VMEM((pages, PAGE, 2 * QK + VDIM), BF16),
            pltpu.VMEM((slots, count), BF16),
            pltpu.VMEM((count, slots), BF16),
            pltpu.VMEM((count, LANES), F32),
            pltpu.VMEM((count, ROW), BF16),
            pltpu.VMEM((count, 4 * QK), F32),
            pltpu.VMEM((count, VDIM), BF16),
            pltpu.VMEM((n_tok, CAP, ROW), BF16),
            pltpu.VMEM((n_tok, CAP, ROW), BF16),
            pltpu.VMEM((n_tok, CAP, ROW), BF16),
            pltpu.VMEM((n_tok, CAP, ROW), BF16),
            pltpu.VMEM((slots, LANES), BF16),
            pltpu.VMEM((slots, LANES), BF16),
            pltpu.VMEM((slots, LANES), BF16),
            pltpu.VMEM((slots, PAGE), F32),
            pltpu.VMEM((slots, PAGE), F32),
            pltpu.VMEM((slots, LANES), F32),
            pltpu.VMEM((pages, PAGE), F32),
            pltpu.VMEM((pages, PAGE), F32),
            pltpu.VMEM((slots, PAGE), BF16),
            pltpu.VMEM((slots, VDIM), F32),
            pltpu.VMEM((4, count, features), BF16),
            pltpu.VMEM((4, count, features), BF16),
            pltpu.VMEM((4, count, features), F32),
            pltpu.VMEM((6, half, features), BF16),
            pltpu.VMEM((6, half, features), BF16),
            dma((3 + n_head,)),
            dma((13,)),
            dma((13,)),
            dma((n_tok,)),
            dma((n_tok,)),
            dma((n_tok,)),
            dma((n_tok,)),
            dma((4,)),
            dma((4,)),
            dma((6,)),
            dma((6,)),
        ],
        compiler_params=pltpu.CompilerParams(
            collective_id=0, has_side_effects=True, vmem_limit_bytes=60 * 1024 * 1024
        ),
        name="decode_step",
    )(
        tokens,
        w_in,
        w_out,
        pool.reshape(pages, PAGE, 2 * QK + VDIM),
        gain.reshape(1, VDIM),
        lq1.reshape(1, QK),
        lk1.reshape(1, QK),
        lq2.reshape(1, QK),
        lk2.reshape(1, QK),
        table,
        length.reshape(1, count),
        owner,
    )


def solution(mesh):
    n_tok, n_head = mesh.shape["tok"], mesh.shape["head"]

    def run(
        tokens,
        input_weight,
        output_weight,
        head_gain,
        query_lambda_one,
        key_lambda_one,
        query_lambda_two,
        key_lambda_two,
        cache_pool,
        page_table,
        cache_length,
        cache_owner,
    ):
        sizes = (n_tok, n_head, tokens.shape[0] // n_tok, tokens.shape[1] // n_head)
        placed = (
            P("tok", "head"),
            P(None, "head"),
            P("head", None),
            P("head"),
            P(),
            P(),
            P(),
            P(),
            P("tok", "head", None, None),
            P("tok", None),
            P("tok"),
            P("tok", None),
        )
        return jax.shard_map(
            functools.partial(on_device, sizes),
            mesh=mesh,
            in_specs=placed,
            out_specs=P("tok", "head"),
            check_vma=False,
        )(
            tokens,
            input_weight,
            output_weight,
            head_gain,
            query_lambda_one,
            key_lambda_one,
            query_lambda_two,
            key_lambda_two,
            cache_pool,
            page_table,
            cache_length,
            cache_owner,
        )

    return run
```

```python
import functools
import math

import jax
import jax.numpy as jnp
from jax import lax
from jax.experimental import pallas as pl
from jax.experimental.pallas import tpu as pltpu
from jax.sharding import PartitionSpec as P

QK = 128
VDIM = 256
PAGE = 128
CAP = 32
SHARED = 8
MAXP = 8
GROUP = 16
LANES = 128
FIELDS = 16
TILE = 8
PER = LANES // CAP
WIDE = 2 * QK + VDIM

lambda_init = 0.8
norm_eps = 1e-05
NEG = -1e30
SCALE = math.log2(math.e) / math.sqrt(QK)
MESH = pl.DeviceIdType.MESH
F32 = jnp.float32
BF16 = jnp.bfloat16


def iota(shape, dim):
    return lax.broadcasted_iota(jnp.int32, shape, dim)


def one_hot(condition):
    return condition.astype(F32).astype(BF16)


def dot(a, b):
    return jnp.dot(a, b, preferred_element_type=F32)


def dot_nt(a, b):
    return lax.dot_general(a, b, (((1,), (1,)), ((), ())), preferred_element_type=F32)


def split(value, terms):
    parts = []
    for _ in range(terms - 1):
        high = value.astype(BF16).astype(F32)
        parts.append(high)
        value = value - high
    return parts + [value]


def stack_rows(rows, height):
    row = iota((height, rows[0].shape[1]), 0)
    stacked = jnp.where(row == 0, rows[0], 0.0)
    for index in range(1, len(rows)):
        stacked = jnp.where(row == index, rows[index], stacked)
    return stacked


def step_kernel(
    sizes,
    tokens,
    w_in,
    w_out,
    pool,
    gain,
    lq1,
    lk1,
    lq2,
    lk2,
    table,
    length,
    owner,
    out,
    x,
    win_v,
    wcol_v,
    pool_v,
    heads,
    place,
    place_t,
    turn,
    proj,
    v_new,
    send_m,
    recv_m,
    send_q,
    recv_q,
    send_s,
    recv_s,
    send_r,
    recv_r,
    send_c,
    recv_c,
    info,
    match,
    match_t,
    times,
    page0,
    first_a,
    first_b,
    page_q,
    priv_a,
    priv_b,
    page_out,
    wide,
    local_sem,
    x_send,
    x_recv,
    m_send,
    m_recv,
    q_send,
    q_recv,
    s_send,
    s_recv,
    w_send,
    w_recv,
    c_send,
    c_recv,
    r_send,
    r_recv,
    h_send,
    h_recv,
):
    n_tok, n_head, count, features = sizes
    slots = n_tok * CAP
    blocks = slots // LANES
    pages = pool.shape[0]
    ny = n_head // 2
    nx = 4
    nz = n_tok // nx
    me_t = lax.axis_index("tok")
    me_h = lax.axis_index("head")
    y, core = me_h // 2, me_h % 2
    z_at, x_at = me_t // nx, me_t % nx
    up, down, far = (y + 1) % ny, (y + ny - 1) % ny, (y + 2) % ny
    sib = y * 2 + 1 - core
    near = (up * 2 + core, down * 2 + core, far * 2 + core)
    across = (up * 2 + 1 - core, down * 2 + 1 - core, far * 2 + 1 - core)

    offsets = [(dz, dx) for dz in range(nz) for dx in range(nx) if dz + dx > 0]
    offsets.sort(key=lambda o: -(min(o[0], nz - o[0]) + min(o[1], nx - o[1])))
    peers = [((z_at + dz) % nz) * nx + (x_at + dx) % nx for dz, dx in offsets]

    barrier = pltpu.get_barrier_semaphore()
    for peer in (sib,) + near + across:
        pl.semaphore_signal(barrier, inc=1, device_id=(me_t, peer), device_id_type=MESH)
    for peer in peers:
        pl.semaphore_signal(barrier, inc=1, device_id=(peer, me_h), device_id_type=MESH)

    sent = []

    def remote(source, target, send_sem, recv_sem, device):
        copy = pltpu.make_async_remote_copy(
            src_ref=source,
            dst_ref=target,
            send_sem=send_sem,
            recv_sem=recv_sem,
            device_id=device,
            device_id_type=MESH,
        )
        copy.start()
        sent.append(copy)
        return copy

    def exchange(source, target, send_sem, recv_sem):
        copies = [
            remote(source.at[p], target.at[me_t], send_sem.at[k], recv_sem.at[k], (p, me_h))
            for k, p in enumerate(peers)
        ]
        target[me_t] = source[me_t]
        return copies

    local_x = pltpu.make_async_copy(tokens, x.at[me_h], local_sem.at[0])
    local_x.start()
    load_win = pltpu.make_async_copy(w_in, win_v, local_sem.at[1])
    load_win.start()

    own = owner[...]
    named = own == iota((n_tok, count), 0)
    earlier = one_hot(iota((count, count), 0) < iota((count, count), 1))
    before = dot(one_hot(named), earlier)
    rank = jnp.sum(jnp.where(named, before, 0.0), axis=0, keepdims=True)
    slot = own * CAP + rank.astype(jnp.int32)
    eye = iota((count, count), 0) == iota((count, count), 1)
    slot_c = jnp.sum(jnp.where(eye, slot, 0), axis=1, keepdims=True)
    place[...] = one_hot(iota((slots, count), 0) == slot)
    place_t[...] = one_hot(iota((count, slots), 1) == slot_c)
    shift = (me_t % PER) * CAP
    for b in range(PER):
        source_lane = iota((LANES, LANES), 0)
        moved = source_lane - b * CAP + shift == iota((LANES, LANES), 1)
        turn[b] = one_hot(moved & (source_lane // CAP == b))

    def tiles(rows, height, target):
        groups = jnp.concatenate(
            [rows[:, g * LANES : (g + 1) * LANES] for g in range(blocks)], axis=0
        ).astype(BF16)
        for b in range(PER):
            moved = dot(groups, turn[b]).astype(BF16)
            for g in range(blocks):
                target[g * PER + b] = moved[g * height : (g + 1) * height]

    def gather_tiles(source, g):
        total = source[g * PER].astype(F32)
        for b in range(1, PER):
            total = total + source[g * PER + b].astype(F32)
        return total

    lengths = length[...]
    ends = stack_rows([(lengths // 8).astype(F32), (lengths % 8).astype(F32)], 8)
    fields = jnp.concatenate([table[...].astype(F32), ends], axis=0).astype(BF16)
    tiles(dot(fields, place_t[...]), FIELDS, send_m)

    pl.semaphore_wait(barrier, 1 + 2 * len(near) + len(peers))

    def gather_start(buffer, send_sem, recv_sem):
        def share(index, source, target):
            return remote(
                buffer.at[source],
                buffer.at[source],
                send_sem.at[index],
                recv_sem.at[index],
                (me_t, target),
            )

        direct = [share(k, me_h, target) for k, target in enumerate(near)]
        return share, direct, share(3, me_h, sib)

    def gather_rest(started, add):
        share, direct, twin = started
        add(me_h)
        twin.wait_recv()
        add(sib)
        passed = []
        for k, turned in enumerate((1, 0, 2)):
            direct[k].wait_recv()
            passed.append(share(4 + k, near[turned], sib))
            add(near[turned])
            if k > 0:
                passed[k - 1].wait_recv()
                add(across[(1, 0, 2)[k - 1]])
        passed[2].wait_recv()
        add(across[2])

    local_x.wait()
    started = gather_start(x, x_send, x_recv)
    m_copies = exchange(send_m, recv_m, m_send, m_recv)
    load_win.wait()
    load_pool = pltpu.make_async_copy(pool, pool_v, local_sem.at[2])
    load_pool.start()

    def add_proj(source):
        rows = pl.ds(pl.multiple_of(source * features, features), features)
        update = dot(x[source], win_v[rows, 0 : 4 * QK])
        proj[...] = proj[...] + update

    proj[...] = jnp.zeros(proj.shape, F32)
    gather_rest(started, add_proj)

    qk = proj[...].astype(BF16)
    send_q[...] = dot(place[...], qk[:, 0 : 2 * QK]).astype(BF16).reshape(n_tok, CAP, 2 * QK)
    q_copies = exchange(send_q, recv_q, q_send, q_recv)
    qf = qk.astype(F32)
    ones = jnp.ones((8, QK), F32).astype(BF16)
    terms = []
    for m in range(2):
        product = qf[:, m * QK : (m + 1) * QK] * qf[:, (m + 2) * QK : (m + 3) * QK]
        high, low = split(product, 2)
        total = dot_nt(ones, high.astype(BF16)) + dot_nt(ones, low.astype(BF16))
        terms += split(total[0:1] * SCALE, 3)
    tiles(dot(stack_rows(terms, TILE).astype(BF16), place_t[...]), TILE, send_s)
    s_copies = exchange(send_s, recv_s, s_send, s_recv)

    def columns(h):
        return w_out.at[:, pl.ds(pl.multiple_of(h * features, features), features)]

    own_w = pltpu.make_async_copy(columns(me_h), wcol_v.at[me_h], local_sem.at[3])
    own_w.start()
    w_copies = [
        remote(columns(h), wcol_v.at[me_h], w_send.at[k], w_recv.at[k], (me_t, h))
        for k, h in enumerate(near + across + (sib,))
    ]

    value = jnp.zeros((count, VDIM), F32)
    for h in range(n_head):
        value = value + dot(x[h], win_v[h * features : (h + 1) * features, 4 * QK :])
    v_new[...] = value.astype(BF16)
    lam = (
        jnp.exp(jnp.sum(lq1[...] * lk1[...], axis=1, keepdims=True))
        - jnp.exp(jnp.sum(lq2[...] * lk2[...], axis=1, keepdims=True))
        + lambda_init
    )

    for copy in m_copies:
        copy.wait_recv()
    whole = jnp.zeros((pages, LANES), F32)
    rest = jnp.zeros((pages, LANES), F32)
    page = iota((pages, LANES), 0).astype(F32)
    for g in range(blocks):
        cut = slice(g * LANES, (g + 1) * LANES)
        got = gather_tiles(recv_m, g)
        cached = got[8:9] * 8.0 + got[9:10]
        info[0:1, cut] = got[0:1]
        info[1:2, cut] = cached
        hit_any = jnp.zeros((pages, LANES), F32)
        for j in range(1, MAXP):
            left = cached - float(PAGE * j)
            number = jnp.where(left > 0.0, got[j : j + 1], -1.0)
            hit = number == page
            hit_any = jnp.where(hit, 1.0, hit_any)
            whole = whole + jnp.where(hit, jnp.where(left >= float(PAGE), 1.0, 0.0), 0.0)
            rest = rest + jnp.where(hit, jnp.where(left >= float(PAGE), 0.0, left), 0.0)
        match[:, cut] = hit_any.astype(BF16)
        match_t[cut] = jnp.transpose(jnp.concatenate([hit_any, hit_any], axis=0)).astype(BF16)
        chosen = jnp.transpose(jnp.broadcast_to(got[0:1], (LANES, LANES)))
        for p in range(SHARED):
            page0[p, cut] = one_hot(chosen == float(p))
    whole = jnp.sum(whole, axis=1, keepdims=True)
    rest = jnp.sum(rest, axis=1, keepdims=True)
    position = iota((pages, PAGE), 1).astype(F32)
    times[...] = whole + jnp.where(position < rest, 1.0, 0.0)
    load_pool.wait()
    for copy in q_copies:
        copy.wait_recv()

    queries = recv_q[...].reshape(slots, 2 * QK)
    page_q[...] = dot(match[...], queries).astype(BF16)
    half = slots // 2
    for h in range(2):
        cut = slice(h * half, (h + 1) * half)
        at = info[0:1, cut]
        for ref, lo in ((first_a, 0), (first_b, QK)):
            kept = None
            for p in range(0, SHARED, 2):
                keys = pool_v[p : p + 2].reshape(2 * PAGE, WIDE)[:, lo : lo + QK]
                score = dot_nt(keys, queries[cut, lo : lo + QK])
                chosen = jnp.where(at == float(p), score[0:PAGE], score[PAGE:])
                kept = chosen if p == 0 else jnp.where(at >= float(p), chosen, kept)
            ref[:, cut] = kept

    row = iota((GROUP, LANES), 0)

    def private_scores(g, carry):
        mine = pl.ds(pl.multiple_of(g * GROUP, GROUP), GROUP)
        keys = pool_v[mine].reshape(GROUP * PAGE, WIDE)
        for ref, lo in ((priv_a, 0), (priv_b, QK)):
            score = dot_nt(page_q[mine, lo : lo + QK], keys[:, lo : lo + QK])
            chosen = score[:, 0:PAGE]
            for i in range(1, GROUP):
                chosen = jnp.where(row == i, score[:, i * PAGE : (i + 1) * PAGE], chosen)
            ref[mine] = chosen
        return carry

    lax.fori_loop(0, pages // GROUP, private_scores, 0)

    for copy in s_copies:
        copy.wait_recv()
    page_best = []
    for ref in (priv_a, priv_b):
        score = jnp.where(times[...] > 0.0, ref[...] * SCALE, NEG)
        ref[...] = score
        page_best.append(jnp.max(score, axis=1, keepdims=True))
    tops, selfs = [], []
    page_top = [jnp.zeros((pages, LANES), F32) for _ in range(2)]
    depth = iota((PAGE, LANES), 0).astype(F32)
    for g in range(blocks):
        cut = slice(g * LANES, (g + 1) * LANES)
        hit = match[:, cut].astype(F32) > 0.0
        got = gather_tiles(recv_s, g)
        valid = depth < info[1:2, cut]
        for m, ref in enumerate((first_a, first_b)):
            score = jnp.where(valid, ref[:, cut] * SCALE, NEG)
            ref[:, cut] = score
            mine = got[3 * m : 3 * m + 1] + got[3 * m + 1 : 3 * m + 2] + got[3 * m + 2 : 3 * m + 3]
            best = jnp.max(jnp.where(hit, page_best[m], NEG), axis=0, keepdims=True)
            top = jnp.maximum(jnp.maximum(jnp.max(score, axis=0, keepdims=True), best), mine)
            page_top[m] = page_top[m] + jnp.where(hit, top, 0.0)
            tops.append(top)
            selfs.append(mine)

    page_sum = []
    for m, ref in enumerate((priv_a, priv_b)):
        top = jnp.sum(page_top[m], axis=1, keepdims=True)
        weight = jnp.where(times[...] > 0.0, jnp.exp2(ref[...] - top) * times[...], 0.0)
        ref[...] = weight
        page_sum.append(jnp.sum(weight, axis=1, keepdims=True))
    page_coef = [jnp.zeros((pages, LANES), F32) for _ in range(2)]
    own_rows = []
    for g in range(blocks):
        cut = slice(g * LANES, (g + 1) * LANES)
        hit = match[:, cut].astype(F32) > 0.0
        mixed, own_coef = None, None
        for m, ref in enumerate((first_a, first_b)):
            top = tops[2 * g + m]
            weight = jnp.exp2(ref[:, cut] - top)
            new = jnp.exp2(selfs[2 * g + m] - top)
            total = (
                new
                + jnp.sum(weight, axis=0, keepdims=True)
                + jnp.sum(jnp.where(hit, page_sum[m], 0.0), axis=0, keepdims=True)
            )
            coef = 1.0 / total if m == 0 else -lam / total
            page_coef[m] = page_coef[m] + jnp.where(hit, coef, 0.0)
            mixed = weight * coef if m == 0 else mixed + weight * coef
            own_coef = new * coef if m == 0 else own_coef + new * coef
        mixed = jnp.transpose(mixed).astype(BF16)
        for p in range(SHARED):
            wide[cut, p * PAGE : (p + 1) * PAGE] = mixed * page0[p, cut]
        own_rows.append(stack_rows(split(own_coef, 2), TILE))
    tiles(jnp.concatenate(own_rows, axis=1), TILE, send_c)
    c_copies = exchange(send_c, recv_c, c_send, c_recv)

    priv_a[...] = priv_a[...] * jnp.sum(page_coef[0], axis=1, keepdims=True) + priv_b[
        ...
    ] * jnp.sum(page_coef[1], axis=1, keepdims=True)

    def private_values(g, carry):
        mine = pl.ds(pl.multiple_of(g * GROUP, GROUP), GROUP)
        values = pool_v[mine].reshape(GROUP * PAGE, WIDE)[:, 2 * QK :]
        weight = priv_a[mine]
        spread = jnp.concatenate(
            [jnp.where(row == i, weight, 0.0) for i in range(GROUP)], axis=1
        ).astype(BF16)
        page_out[mine] = dot(spread, values)
        return carry

    lax.fori_loop(0, pages // GROUP, private_values, 0)
    high, low = split(page_out[...], 2)
    pair = jnp.concatenate([high, low], axis=0).astype(BF16)
    values = pool_v[0:SHARED].reshape(SHARED * PAGE, WIDE)[:, 2 * QK :]
    result = dot(wide[...], values) + dot(match_t[...], pair)
    send_r[...] = result.astype(BF16).reshape(n_tok, CAP, VDIM)

    r_copies = exchange(send_r, recv_r, r_send, r_recv)
    own_w.wait()
    for copy in c_copies:
        copy.wait_recv()
    rows = jnp.concatenate([gather_tiles(recv_c, g) for g in range(blocks)], axis=1)
    coefs = dot_nt(place_t[...], rows.astype(BF16))
    addend = (coefs[:, 0:1] + coefs[:, 1:2]) * v_new[...].astype(F32)
    for copy in r_copies:
        copy.wait_recv()
    mixed = dot(place_t[...], recv_r[...].reshape(slots, VDIM)) + addend
    scale = lax.rsqrt(jnp.mean(mixed * mixed, axis=1, keepdims=True) + norm_eps)
    heads[me_h] = (mixed * scale * gain[...] * (1.0 - lambda_init)).astype(BF16)

    started = gather_start(heads, h_send, h_recv)
    for copy in w_copies:
        copy.wait_recv()
    mix = proj.at[:, 0:features]
    mix[...] = jnp.zeros(mix.shape, F32)

    def add_out(source):
        mix[...] = mix[...] + dot(heads[source], wcol_v[source])

    gather_rest(started, add_out)
    out[...] = mix[...].astype(BF16)
    for copy in sent:
        copy.wait_send()


def on_device(sizes, tokens, w_in, w_out, gain, lq1, lk1, lq2, lk2, pool, table, length, owner):
    n_tok, n_head, count, features = sizes
    slots = n_tok * CAP
    pages = pool.shape[0]
    vmem = pl.BlockSpec(memory_space=pltpu.VMEM)
    hbm = pl.BlockSpec(memory_space=pl.ANY)
    dma = pltpu.SemaphoreType.DMA
    return pl.pallas_call(
        functools.partial(step_kernel, sizes),
        out_shape=jax.ShapeDtypeStruct((count, features), BF16),
        in_specs=[hbm] * 4 + [vmem] * 8,
        out_specs=vmem,
        scratch_shapes=[
            pltpu.VMEM((n_head, count, features), BF16),
            pltpu.VMEM(w_in.shape, BF16),
            pltpu.VMEM((n_head, VDIM, features), BF16),
            pltpu.VMEM((pages, PAGE, WIDE), BF16),
            pltpu.VMEM((n_head, count, VDIM), BF16),
            pltpu.VMEM((slots, count), BF16),
            pltpu.VMEM((count, slots), BF16),
            pltpu.VMEM((PER, LANES, LANES), BF16),
            pltpu.VMEM((count, 4 * QK), F32),
            pltpu.VMEM((count, VDIM), BF16),
            pltpu.VMEM((n_tok, FIELDS, LANES), BF16),
            pltpu.VMEM((n_tok, FIELDS, LANES), BF16),
            pltpu.VMEM((n_tok, CAP, 2 * QK), BF16),
            pltpu.VMEM((n_tok, CAP, 2 * QK), BF16),
            pltpu.VMEM((n_tok, TILE, LANES), BF16),
            pltpu.VMEM((n_tok, TILE, LANES), BF16),
            pltpu.VMEM((n_tok, CAP, VDIM), BF16),
            pltpu.VMEM((n_tok, CAP, VDIM), BF16),
            pltpu.VMEM((n_tok, TILE, LANES), BF16),
            pltpu.VMEM((n_tok, TILE, LANES), BF16),
            pltpu.VMEM((8, slots), F32),
            pltpu.VMEM((pages, slots), BF16),
            pltpu.VMEM((slots, 2 * pages), BF16),
            pltpu.VMEM((pages, PAGE), F32),
            pltpu.VMEM((SHARED, slots, PAGE), BF16),
            pltpu.VMEM((PAGE, slots), F32),
            pltpu.VMEM((PAGE, slots), F32),
            pltpu.VMEM((pages, 2 * QK), BF16),
            pltpu.VMEM((pages, PAGE), F32),
            pltpu.VMEM((pages, PAGE), F32),
            pltpu.VMEM((pages, VDIM), F32),
            pltpu.VMEM((slots, SHARED * PAGE), BF16),
            dma((4,)),
        ]
        + [dma((count_of,)) for count_of in (7,) * 2 + (n_tok,) * 6 + (7,) * 2 + (n_tok,) * 4 + (7,) * 2],
        compiler_params=pltpu.CompilerParams(
            collective_id=0, has_side_effects=True, vmem_limit_bytes=60 * 1024 * 1024
        ),
        name="decode_step",
    )(
        tokens,
        w_in,
        w_out,
        pool.reshape(pages, PAGE, WIDE),
        gain.reshape(1, VDIM),
        lq1.reshape(1, QK),
        lk1.reshape(1, QK),
        lq2.reshape(1, QK),
        lk2.reshape(1, QK),
        jnp.transpose(table),
        length.reshape(1, count),
        owner.reshape(1, count),
    )


def solution(mesh):
    n_tok, n_head = mesh.shape["tok"], mesh.shape["head"]

    def run(
        tokens,
        input_weight,
        output_weight,
        head_gain,
        query_lambda_one,
        key_lambda_one,
        query_lambda_two,
        key_lambda_two,
        cache_pool,
        page_table,
        cache_length,
        cache_owner,
    ):
        sizes = (n_tok, n_head, tokens.shape[0] // n_tok, tokens.shape[1] // n_head)
        placed = (
            P("tok", "head"),
            P(None, "head"),
            P("head", None),
            P("head"),
            P(),
            P(),
            P(),
            P(),
            P("tok", "head", None, None),
            P("tok", None),
            P("tok"),
            P("tok", None),
        )
        return jax.shard_map(
            functools.partial(on_device, sizes),
            mesh=mesh,
            in_specs=placed,
            out_specs=P("tok", "head"),
            check_vma=False,
        )(
            tokens,
            input_weight,
            output_weight,
            head_gain,
            query_lambda_one,
            key_lambda_one,
            query_lambda_two,
            key_lambda_two,
            cache_pool,
            page_table,
            cache_length,
            cache_owner,
        )

    return run
```

```python
import functools
import math

import jax
import jax.numpy as jnp
from jax import lax
from jax.experimental import pallas as pl
from jax.experimental.pallas import tpu as pltpu
from jax.sharding import PartitionSpec as P

QK = 128
VDIM = 256
PAGE = 128
CAP = 32
SHARED = 8
MAXP = 8
GROUP = 16
LANES = 128
FIELDS = 16
TILE = 8
PER = LANES // CAP
WIDE = 2 * QK + VDIM

lambda_init = 0.8
norm_eps = 1e-05
NEG = -1e30
SCALE = math.log2(math.e) / math.sqrt(QK)
MESH = pl.DeviceIdType.MESH
F32 = jnp.float32
BF16 = jnp.bfloat16


def iota(shape, dim):
    return lax.broadcasted_iota(jnp.int32, shape, dim)


def one_hot(condition):
    return condition.astype(F32).astype(BF16)


def dot(a, b):
    return jnp.dot(a, b, preferred_element_type=F32)


def dot_nt(a, b):
    return lax.dot_general(a, b, (((1,), (1,)), ((), ())), preferred_element_type=F32)


def split(value, terms):
    parts = []
    for _ in range(terms - 1):
        high = value.astype(BF16).astype(F32)
        parts.append(high)
        value = value - high
    return parts + [value]


def stack_rows(rows, height):
    row = iota((height, rows[0].shape[1]), 0)
    stacked = jnp.where(row == 0, rows[0], 0.0)
    for index in range(1, len(rows)):
        stacked = jnp.where(row == index, rows[index], stacked)
    return stacked


def step_kernel(
    sizes,
    tokens,
    w_in,
    w_out,
    pool,
    gain,
    lq1,
    lk1,
    lq2,
    lk2,
    table,
    length,
    owner,
    out,
    x,
    win_v,
    wcol_v,
    pool_v,
    heads,
    place,
    place_t,
    turn,
    proj,
    v_new,
    send_m,
    recv_m,
    send_q,
    recv_q,
    send_s,
    recv_s,
    send_r,
    recv_r,
    send_c,
    recv_c,
    info,
    match,
    match_t,
    times,
    page0,
    first_a,
    first_b,
    page_q,
    priv_a,
    priv_b,
    page_out,
    wide,
    local_sem,
    x_send,
    x_recv,
    m_sem,
    q_sem,
    s_sem,
    w_sem,
    c_sem,
    r_sem,
    h_send,
    h_recv,
):
    n_tok, n_head, count, features = sizes
    slots = n_tok * CAP
    blocks = slots // LANES
    pages = pool.shape[0]
    ny = n_head // 2
    nx = 4
    nz = n_tok // nx
    me_t = lax.axis_index("tok")
    me_h = lax.axis_index("head")
    y, core = me_h // 2, me_h % 2
    z_at, x_at = me_t // nx, me_t % nx
    up, down, far = (y + 1) % ny, (y + ny - 1) % ny, (y + 2) % ny
    sib = y * 2 + 1 - core
    h_up, h_down, h_far = up * 2 + core, down * 2 + core, far * 2 + core
    a_up, a_down, a_far = up * 2 + 1 - core, down * 2 + 1 - core, far * 2 + 1 - core
    others = (sib, h_up, h_down, h_far, a_up, a_down, a_far)

    offsets = [(dz, dx) for dz in range(nz) for dx in range(nx) if dz + dx > 0]
    offsets.sort(key=lambda o: -(min(o[0], nz - o[0]) + min(o[1], nx - o[1])))
    peers = [((z_at + dz) % nz) * nx + (x_at + dx) % nx for dz, dx in offsets]

    barrier = pltpu.get_barrier_semaphore()
    for peer in others:
        pl.semaphore_signal(barrier, inc=1, device_id=(me_t, peer), device_id_type=MESH)
    for peer in peers:
        pl.semaphore_signal(barrier, inc=1, device_id=(peer, me_h), device_id_type=MESH)

    sent = []

    def remote(source, target, send_sem, recv_sem, device):
        copy = pltpu.make_async_remote_copy(
            src_ref=source,
            dst_ref=target,
            send_sem=send_sem,
            recv_sem=recv_sem,
            device_id=device,
            device_id_type=MESH,
        )
        copy.start()
        return copy

    def bulk(source, target, blocks_of, send_sem, recv_sem):
        some = pl.ds(0, blocks_of)
        copy = pltpu.make_async_remote_copy(
            src_ref=source.at[some],
            dst_ref=target.at[some],
            send_sem=send_sem,
            recv_sem=recv_sem,
            device_id=(me_t, sib),
            device_id_type=MESH,
        )
        sent.append(copy)
        return copy

    def exchange(source, target, sems):
        for p in peers:
            remote(source.at[p], target.at[me_t], sems.at[0], sems.at[1], (p, me_h))
        target[me_t] = source[me_t]
        return bulk(source, target, len(peers), sems.at[0], sems.at[1])

    local_x = pltpu.make_async_copy(tokens, x.at[me_h], local_sem.at[0])
    local_x.start()
    load_win = pltpu.make_async_copy(w_in, win_v, local_sem.at[1])
    load_win.start()

    own = owner[...]
    named = own == iota((n_tok, count), 0)
    earlier = one_hot(iota((count, count), 0) < iota((count, count), 1))
    before = dot(one_hot(named), earlier)
    rank = jnp.sum(jnp.where(named, before, 0.0), axis=0, keepdims=True)
    slot = own * CAP + rank.astype(jnp.int32)
    eye = iota((count, count), 0) == iota((count, count), 1)
    slot_c = jnp.sum(jnp.where(eye, slot, 0), axis=1, keepdims=True)
    place[...] = one_hot(iota((slots, count), 0) == slot)
    place_t[...] = one_hot(iota((count, slots), 1) == slot_c)
    shift = (me_t % PER) * CAP
    for b in range(PER):
        source_lane = iota((LANES, LANES), 0)
        moved = source_lane - b * CAP + shift == iota((LANES, LANES), 1)
        turn[b] = one_hot(moved & (source_lane // CAP == b))

    def tiles(rows, height, target):
        groups = jnp.concatenate(
            [rows[:, g * LANES : (g + 1) * LANES] for g in range(blocks)], axis=0
        ).astype(BF16)
        for b in range(PER):
            moved = dot(groups, turn[b]).astype(BF16)
            for g in range(blocks):
                target[g * PER + b] = moved[g * height : (g + 1) * height]

    def gather_tiles(source, g):
        total = source[g * PER].astype(F32)
        for b in range(1, PER):
            total = total + source[g * PER + b].astype(F32)
        return total

    lengths = length[...]
    ends = stack_rows([(lengths // 8).astype(F32), (lengths % 8).astype(F32)], 8)
    fields = jnp.concatenate([table[...].astype(F32), ends], axis=0).astype(BF16)
    tiles(dot(fields, place_t[...]), FIELDS, send_m)

    pl.semaphore_wait(barrier, len(others) + len(peers))

    quarter = count // 4

    def gather_start(buffer, send_sem, recv_sem):
        def go(index, source, start, quarters, target):
            part = buffer.at[source, pl.ds(start * quarter, quarters * quarter)]
            return remote(part, part, send_sem.at[0], recv_sem.at[index], (me_t, target))

        copies = [
            go(0, me_h, 0, 1, h_up),
            go(1, me_h, 3, 1, h_down),
            go(2, me_h, 1, 1, h_up),
            go(3, me_h, 2, 1, h_down),
            go(4, me_h, 2, 2, h_up),
            go(5, me_h, 0, 2, h_down),
            go(6, me_h, 0, 4, sib),
        ]
        bulk(buffer, buffer, n_head - 1, send_sem.at[0], recv_sem.at[0])
        return go, copies

    def gather_rest(started, add):
        go, copies = started
        add(me_h)
        for k, (source, start, target) in enumerate(
            ((h_down, 0, h_up), (h_up, 3, h_down), (h_down, 1, h_up), (h_up, 2, h_down))
        ):
            copies[k].wait_recv()
            copies.append(go(7 + k, source, start, 1, target))
        copies.append(go(11, h_down, 0, 2, sib))
        copies.append(go(12, h_up, 2, 2, sib))
        copies[6].wait_recv()
        add(sib)
        copies[4].wait_recv()
        copies.append(go(13, h_down, 2, 2, sib))
        add(h_down)
        copies[5].wait_recv()
        copies.append(go(14, h_up, 0, 2, sib))
        add(h_up)
        copies[11].wait_recv()
        copies[13].wait_recv()
        add(a_down)
        copies[12].wait_recv()
        copies[14].wait_recv()
        add(a_up)
        for k, start in enumerate((0, 3, 1, 2)):
            copies[7 + k].wait_recv()
            copies.append(go(15 + k, h_far, start, 1, sib))
        add(h_far)
        for k in range(4):
            copies[15 + k].wait_recv()
        add(a_far)

    local_x.wait()
    started = gather_start(x, x_send, x_recv)
    meta_in = exchange(send_m, recv_m, m_sem)
    load_win.wait()
    load_pool = pltpu.make_async_copy(pool, pool_v, local_sem.at[2])
    load_pool.start()

    def add_query(source):
        rows = pl.ds(pl.multiple_of(source * features, features), features)
        proj[...] = proj[...] + dot(x[source], win_v[rows, 0 : 2 * QK])

    proj[...] = jnp.zeros(proj.shape, F32)
    gather_rest(started, add_query)

    query = proj[...].astype(BF16)
    send_q[...] = dot(place[...], query).astype(BF16).reshape(n_tok, CAP, 2 * QK)
    query_in = exchange(send_q, recv_q, q_sem)

    fresh = jnp.zeros((count, 2 * QK + VDIM), F32)
    for h in range(n_head):
        fresh = fresh + dot(x[h], win_v[h * features : (h + 1) * features, 2 * QK :])
    fresh = fresh.astype(BF16)
    v_new[...] = fresh[:, 2 * QK :]
    product = query.astype(F32) * fresh[:, 0 : 2 * QK].astype(F32)
    high, low = split(product, 2)
    ones = jnp.ones((8, QK), F32).astype(BF16)
    terms = []
    for m in range(2):
        part = slice(m * QK, (m + 1) * QK)
        total = dot_nt(ones, high[:, part].astype(BF16)) + dot_nt(ones, low[:, part].astype(BF16))
        terms += split(total[0:1] * SCALE, 3)
    tiles(dot(stack_rows(terms, TILE).astype(BF16), place_t[...]), TILE, send_s)
    self_in = exchange(send_s, recv_s, s_sem)

    def columns(h):
        return w_out.at[:, pl.ds(pl.multiple_of(h * features, features), features)]

    own_w = pltpu.make_async_copy(columns(me_h), wcol_v.at[me_h], local_sem.at[3])
    own_w.start()
    for h in (h_up, h_down, h_far, a_up, a_down, a_far, sib):
        remote(columns(h), wcol_v.at[me_h], w_sem.at[0], w_sem.at[1], (me_t, h))
    weights_in = bulk(wcol_v, wcol_v, n_head - 1, w_sem.at[0], w_sem.at[1])
    lam = (
        jnp.exp(jnp.sum(lq1[...] * lk1[...], axis=1, keepdims=True))
        - jnp.exp(jnp.sum(lq2[...] * lk2[...], axis=1, keepdims=True))
        + lambda_init
    )

    meta_in.wait_recv()
    whole = jnp.zeros((pages, LANES), F32)
    rest = jnp.zeros((pages, LANES), F32)
    page = iota((pages, LANES), 0).astype(F32)
    for g in range(blocks):
        cut = slice(g * LANES, (g + 1) * LANES)
        got = gather_tiles(recv_m, g)
        cached = got[8:9] * 8.0 + got[9:10]
        info[0:1, cut] = got[0:1]
        info[1:2, cut] = cached
        hit_any = jnp.zeros((pages, LANES), F32)
        for j in range(1, MAXP):
            left = cached - float(PAGE * j)
            number = jnp.where(left > 0.0, got[j : j + 1], -1.0)
            hit = number == page
            hit_any = jnp.where(hit, 1.0, hit_any)
            whole = whole + jnp.where(hit, jnp.where(left >= float(PAGE), 1.0, 0.0), 0.0)
            rest = rest + jnp.where(hit, jnp.where(left >= float(PAGE), 0.0, left), 0.0)
        match[:, cut] = hit_any.astype(BF16)
        match_t[cut] = jnp.transpose(jnp.concatenate([hit_any, hit_any], axis=0)).astype(BF16)
        chosen = jnp.transpose(jnp.broadcast_to(got[0:1], (LANES, LANES)))
        for p in range(SHARED):
            page0[p, cut] = one_hot(chosen == float(p))
    whole = jnp.sum(whole, axis=1, keepdims=True)
    rest = jnp.sum(rest, axis=1, keepdims=True)
    position = iota((pages, PAGE), 1).astype(F32)
    times[...] = whole + jnp.where(position < rest, 1.0, 0.0)
    load_pool.wait()
    query_in.wait_recv()

    queries = recv_q[...].reshape(slots, 2 * QK)
    page_q[...] = dot(match[...], queries).astype(BF16)
    half = slots // 2
    for h in range(2):
        cut = slice(h * half, (h + 1) * half)
        at = info[0:1, cut]
        for ref, lo in ((first_a, 0), (first_b, QK)):
            kept = None
            for p in range(0, SHARED, 2):
                keys = pool_v[p : p + 2].reshape(2 * PAGE, WIDE)[:, lo : lo + QK]
                score = dot_nt(keys, queries[cut, lo : lo + QK])
                chosen = jnp.where(at == float(p), score[0:PAGE], score[PAGE:])
                kept = chosen if p == 0 else jnp.where(at >= float(p), chosen, kept)
            ref[:, cut] = kept

    row = iota((GROUP, LANES), 0)

    def private_scores(g, carry):
        mine = pl.ds(pl.multiple_of(g * GROUP, GROUP), GROUP)
        keys = pool_v[mine].reshape(GROUP * PAGE, WIDE)
        for ref, lo in ((priv_a, 0), (priv_b, QK)):
            score = dot_nt(page_q[mine, lo : lo + QK], keys[:, lo : lo + QK])
            chosen = score[:, 0:PAGE]
            for i in range(1, GROUP):
                chosen = jnp.where(row == i, score[:, i * PAGE : (i + 1) * PAGE], chosen)
            ref[mine] = chosen
        return carry

    lax.fori_loop(0, pages // GROUP, private_scores, 0)

    self_in.wait_recv()
    page_best = []
    for ref in (priv_a, priv_b):
        score = jnp.where(times[...] > 0.0, ref[...] * SCALE, NEG)
        ref[...] = score
        page_best.append(jnp.max(score, axis=1, keepdims=True))
    tops, selfs = [], []
    page_top = [jnp.zeros((pages, LANES), F32) for _ in range(2)]
    depth = iota((PAGE, LANES), 0).astype(F32)
    for g in range(blocks):
        cut = slice(g * LANES, (g + 1) * LANES)
        hit = match[:, cut].astype(F32) > 0.0
        got = gather_tiles(recv_s, g)
        valid = depth < info[1:2, cut]
        for m, ref in enumerate((first_a, first_b)):
            score = jnp.where(valid, ref[:, cut] * SCALE, NEG)
            ref[:, cut] = score
            mine = got[3 * m : 3 * m + 1] + got[3 * m + 1 : 3 * m + 2] + got[3 * m + 2 : 3 * m + 3]
            best = jnp.max(jnp.where(hit, page_best[m], NEG), axis=0, keepdims=True)
            top = jnp.maximum(jnp.maximum(jnp.max(score, axis=0, keepdims=True), best), mine)
            page_top[m] = page_top[m] + jnp.where(hit, top, 0.0)
            tops.append(top)
            selfs.append(mine)

    page_sum = []
    for m, ref in enumerate((priv_a, priv_b)):
        top = jnp.sum(page_top[m], axis=1, keepdims=True)
        weight = jnp.where(times[...] > 0.0, jnp.exp2(ref[...] - top) * times[...], 0.0)
        ref[...] = weight
        page_sum.append(jnp.sum(weight, axis=1, keepdims=True))
    page_coef = [jnp.zeros((pages, LANES), F32) for _ in range(2)]
    own_rows = []
    for g in range(blocks):
        cut = slice(g * LANES, (g + 1) * LANES)
        hit = match[:, cut].astype(F32) > 0.0
        mixed, own_coef = None, None
        for m, ref in enumerate((first_a, first_b)):
            top = tops[2 * g + m]
            weight = jnp.exp2(ref[:, cut] - top)
            new = jnp.exp2(selfs[2 * g + m] - top)
            total = (
                new
                + jnp.sum(weight, axis=0, keepdims=True)
                + jnp.sum(jnp.where(hit, page_sum[m], 0.0), axis=0, keepdims=True)
            )
            coef = 1.0 / total if m == 0 else -lam / total
            page_coef[m] = page_coef[m] + jnp.where(hit, coef, 0.0)
            mixed = weight * coef if m == 0 else mixed + weight * coef
            own_coef = new * coef if m == 0 else own_coef + new * coef
        mixed = jnp.transpose(mixed).astype(BF16)
        for p in range(SHARED):
            wide[cut, p * PAGE : (p + 1) * PAGE] = mixed * page0[p, cut]
        own_rows.append(stack_rows(split(own_coef, 2), TILE))
    tiles(jnp.concatenate(own_rows, axis=1), TILE, send_c)
    coef_in = exchange(send_c, recv_c, c_sem)

    priv_a[...] = priv_a[...] * jnp.sum(page_coef[0], axis=1, keepdims=True) + priv_b[
        ...
    ] * jnp.sum(page_coef[1], axis=1, keepdims=True)

    def private_values(g, carry):
        mine = pl.ds(pl.multiple_of(g * GROUP, GROUP), GROUP)
        values = pool_v[mine].reshape(GROUP * PAGE, WIDE)[:, 2 * QK :]
        weight = priv_a[mine]
        spread = jnp.concatenate(
            [jnp.where(row == i, weight, 0.0) for i in range(GROUP)], axis=1
        ).astype(BF16)
        page_out[mine] = dot(spread, values)
        return carry

    lax.fori_loop(0, pages // GROUP, private_values, 0)
    high, low = split(page_out[...], 2)
    pair = jnp.concatenate([high, low], axis=0).astype(BF16)
    values = pool_v[0:SHARED].reshape(SHARED * PAGE, WIDE)[:, 2 * QK :]
    result = dot(wide[...], values) + dot(match_t[...], pair)
    send_r[...] = result.astype(BF16).reshape(n_tok, CAP, VDIM)

    mixed_in = exchange(send_r, recv_r, r_sem)
    own_w.wait()
    coef_in.wait_recv()
    rows = jnp.concatenate([gather_tiles(recv_c, g) for g in range(blocks)], axis=1)
    coefs = dot_nt(place_t[...], rows.astype(BF16))
    addend = (coefs[:, 0:1] + coefs[:, 1:2]) * v_new[...].astype(F32)
    mixed_in.wait_recv()
    mixed = dot(place_t[...], recv_r[...].reshape(slots, VDIM)) + addend
    scale = lax.rsqrt(jnp.mean(mixed * mixed, axis=1, keepdims=True) + norm_eps)
    heads[me_h] = (mixed * scale * gain[...] * (1.0 - lambda_init)).astype(BF16)

    started = gather_start(heads, h_send, h_recv)
    weights_in.wait_recv()
    proj[...] = jnp.zeros(proj.shape, F32)

    def add_out(source):
        proj[...] = proj[...] + dot(heads[source], wcol_v[source])

    gather_rest(started, add_out)
    out[...] = proj[...].astype(BF16)
    for copy in sent:
        copy.wait_send()


def on_device(sizes, tokens, w_in, w_out, gain, lq1, lk1, lq2, lk2, pool, table, length, owner):
    n_tok, n_head, count, features = sizes
    slots = n_tok * CAP
    pages = pool.shape[0]
    vmem = pl.BlockSpec(memory_space=pltpu.VMEM)
    hbm = pl.BlockSpec(memory_space=pl.ANY)
    dma = pltpu.SemaphoreType.DMA
    return pl.pallas_call(
        functools.partial(step_kernel, sizes),
        out_shape=jax.ShapeDtypeStruct((count, features), BF16),
        in_specs=[hbm] * 4 + [vmem] * 8,
        out_specs=vmem,
        scratch_shapes=[
            pltpu.VMEM((n_head, count, features), BF16),
            pltpu.VMEM(w_in.shape, BF16),
            pltpu.VMEM((n_head, VDIM, features), BF16),
            pltpu.VMEM((pages, PAGE, WIDE), BF16),
            pltpu.VMEM((n_head, count, VDIM), BF16),
            pltpu.VMEM((slots, count), BF16),
            pltpu.VMEM((count, slots), BF16),
            pltpu.VMEM((PER, LANES, LANES), BF16),
            pltpu.VMEM((count, 2 * QK), F32),
            pltpu.VMEM((count, VDIM), BF16),
            pltpu.VMEM((n_tok, FIELDS, LANES), BF16),
            pltpu.VMEM((n_tok, FIELDS, LANES), BF16),
            pltpu.VMEM((n_tok, CAP, 2 * QK), BF16),
            pltpu.VMEM((n_tok, CAP, 2 * QK), BF16),
            pltpu.VMEM((n_tok, TILE, LANES), BF16),
            pltpu.VMEM((n_tok, TILE, LANES), BF16),
            pltpu.VMEM((n_tok, CAP, VDIM), BF16),
            pltpu.VMEM((n_tok, CAP, VDIM), BF16),
            pltpu.VMEM((n_tok, TILE, LANES), BF16),
            pltpu.VMEM((n_tok, TILE, LANES), BF16),
            pltpu.VMEM((8, slots), F32),
            pltpu.VMEM((pages, slots), BF16),
            pltpu.VMEM((slots, 2 * pages), BF16),
            pltpu.VMEM((pages, PAGE), F32),
            pltpu.VMEM((SHARED, slots, PAGE), BF16),
            pltpu.VMEM((PAGE, slots), F32),
            pltpu.VMEM((PAGE, slots), F32),
            pltpu.VMEM((pages, 2 * QK), BF16),
            pltpu.VMEM((pages, PAGE), F32),
            pltpu.VMEM((pages, PAGE), F32),
            pltpu.VMEM((pages, VDIM), F32),
            pltpu.VMEM((slots, SHARED * PAGE), BF16),
            dma((4,)),
        ]
        + [dma((number,)) for number in (1, 19, 2, 2, 2, 2, 2, 2, 1, 19)],
        compiler_params=pltpu.CompilerParams(
            collective_id=0, has_side_effects=True, vmem_limit_bytes=60 * 1024 * 1024
        ),
        name="decode_step",
    )(
        tokens,
        w_in,
        w_out,
        pool.reshape(pages, PAGE, WIDE),
        gain.reshape(1, VDIM),
        lq1.reshape(1, QK),
        lk1.reshape(1, QK),
        lq2.reshape(1, QK),
        lk2.reshape(1, QK),
        jnp.transpose(table),
        length.reshape(1, count),
        owner.reshape(1, count),
    )


def solution(mesh):
    n_tok, n_head = mesh.shape["tok"], mesh.shape["head"]

    def run(
        tokens,
        input_weight,
        output_weight,
        head_gain,
        query_lambda_one,
        key_lambda_one,
        query_lambda_two,
        key_lambda_two,
        cache_pool,
        page_table,
        cache_length,
        cache_owner,
    ):
        sizes = (n_tok, n_head, tokens.shape[0] // n_tok, tokens.shape[1] // n_head)
        placed = (
            P("tok", "head"),
            P(None, "head"),
            P("head", None),
            P("head"),
            P(),
            P(),
            P(),
            P(),
            P("tok", "head", None, None),
            P("tok", None),
            P("tok"),
            P("tok", None),
        )
        return jax.shard_map(
            functools.partial(on_device, sizes),
            mesh=mesh,
            in_specs=placed,
            out_specs=P("tok", "head"),
            check_vma=False,
        )(
            tokens,
            input_weight,
            output_weight,
            head_gain,
            query_lambda_one,
            key_lambda_one,
            query_lambda_two,
            key_lambda_two,
            cache_pool,
            page_table,
            cache_length,
            cache_owner,
        )

    return run
```

```python
import functools
import math

import jax
import jax.numpy as jnp
from jax import lax
from jax.experimental import pallas as pl
from jax.experimental.pallas import tpu as pltpu
from jax.sharding import PartitionSpec as P

QK = 128
VDIM = 256
PAGE = 128
CAP = 32
SHARED = 8
MAXP = 8
GROUP = 16
LANES = 128
FIELDS = 16
TILE = 8
PER = LANES // CAP
WIDE = 2 * QK + VDIM

lambda_init = 0.8
norm_eps = 1e-05
NEG = -1e30
SCALE = math.log2(math.e) / math.sqrt(QK)
MESH = pl.DeviceIdType.MESH
F32 = jnp.float32
BF16 = jnp.bfloat16


def iota(shape, dim):
    return lax.broadcasted_iota(jnp.int32, shape, dim)


def one_hot(condition):
    return condition.astype(F32).astype(BF16)


def dot(a, b):
    return jnp.dot(a, b, preferred_element_type=F32)


def dot_nt(a, b):
    return lax.dot_general(a, b, (((1,), (1,)), ((), ())), preferred_element_type=F32)


def split(value, terms):
    parts = []
    for _ in range(terms - 1):
        high = value.astype(BF16).astype(F32)
        parts.append(high)
        value = value - high
    return parts + [value]


def stack_rows(rows, height):
    row = iota((height, rows[0].shape[1]), 0)
    stacked = jnp.where(row == 0, rows[0], 0.0)
    for index in range(1, len(rows)):
        stacked = jnp.where(row == index, rows[index], stacked)
    return stacked


def step_kernel(
    sizes,
    tokens,
    w_in,
    w_out,
    pool,
    gain_h,
    lq1_h,
    lk1_h,
    lq2_h,
    lk2_h,
    table_h,
    length_h,
    owner_h,
    out,
    gain,
    lq1,
    lk1,
    lq2,
    lk2,
    table,
    length,
    owner,
    x,
    win_v,
    wcol_v,
    pool_v,
    heads,
    place,
    place_t,
    turn,
    proj,
    v_new,
    send_m,
    recv_m,
    send_q,
    recv_q,
    send_s,
    recv_s,
    send_r,
    recv_r,
    send_c,
    recv_c,
    info,
    match,
    match_t,
    times,
    page0,
    first_a,
    first_b,
    page_q,
    priv_a,
    priv_b,
    page_out,
    wide,
    local_sem,
    x_send,
    x_recv,
    m_sem,
    q_sem,
    s_sem,
    w_sem,
    c_sem,
    r_sem,
    h_send,
    h_recv,
):
    n_tok, n_head, count, features = sizes
    slots = n_tok * CAP
    blocks = slots // LANES
    pages = pool.shape[0]
    ny = n_head // 2
    nx = 4
    nz = n_tok // nx
    me_t = lax.axis_index("tok")
    me_h = lax.axis_index("head")
    y, core = me_h // 2, me_h % 2
    z_at, x_at = me_t // nx, me_t % nx
    up, down, far = (y + 1) % ny, (y + ny - 1) % ny, (y + 2) % ny
    sib = y * 2 + 1 - core
    h_up, h_down, h_far = up * 2 + core, down * 2 + core, far * 2 + core
    a_up, a_down, a_far = up * 2 + 1 - core, down * 2 + 1 - core, far * 2 + 1 - core
    others = (sib, h_up, h_down, h_far, a_up, a_down, a_far)

    offsets = [(dz, dx) for dz in range(nz) for dx in range(nx) if dz + dx > 0]
    offsets.sort(key=lambda o: -(min(o[0], nz - o[0]) + min(o[1], nx - o[1])))
    peers = [((z_at + dz) % nz) * nx + (x_at + dx) % nx for dz, dx in offsets]

    barrier = pltpu.get_barrier_semaphore()
    for peer in others:
        pl.semaphore_signal(barrier, inc=1, device_id=(me_t, peer), device_id_type=MESH)
    for peer in peers:
        pl.semaphore_signal(barrier, inc=1, device_id=(peer, me_h), device_id_type=MESH)

    sent = []

    def remote(source, target, send_sem, recv_sem, device):
        copy = pltpu.make_async_remote_copy(
            src_ref=source,
            dst_ref=target,
            send_sem=send_sem,
            recv_sem=recv_sem,
            device_id=device,
            device_id_type=MESH,
        )
        copy.start()
        return copy

    def bulk(source, target, blocks_of, send_sem, recv_sem):
        some = pl.ds(0, blocks_of)
        copy = pltpu.make_async_remote_copy(
            src_ref=source.at[some],
            dst_ref=target.at[some],
            send_sem=send_sem,
            recv_sem=recv_sem,
            device_id=(me_t, sib),
            device_id_type=MESH,
        )
        sent.append(copy)
        return copy

    def exchange(source, target, sems):
        for p in peers:
            remote(source.at[p], target.at[me_t], sems.at[0], sems.at[1], (p, me_h))
        target[me_t] = source[me_t]
        return bulk(source, target, len(peers), sems.at[0], sems.at[1])

    local_x = pltpu.make_async_copy(tokens, x.at[me_h], local_sem.at[0])
    local_x.start()
    load_win = pltpu.make_async_copy(w_in, win_v, local_sem.at[1])
    load_win.start()

    small = [
        pltpu.make_async_copy(source, target, local_sem.at[4 + k])
        for k, (source, target) in enumerate(
            (
                (owner_h, owner),
                (table_h, table),
                (length_h, length),
                (gain_h, gain),
                (lq1_h, lq1),
                (lk1_h, lk1),
                (lq2_h, lq2),
                (lk2_h, lk2),
            )
        )
    ]
    for load in small:
        load.start()
    for load in small:
        load.wait()

    own = owner[...]
    named = own == iota((n_tok, count), 0)
    earlier = one_hot(iota((count, count), 0) < iota((count, count), 1))
    before = dot(one_hot(named), earlier)
    rank = jnp.sum(jnp.where(named, before, 0.0), axis=0, keepdims=True)
    slot = own * CAP + rank.astype(jnp.int32)
    eye = iota((count, count), 0) == iota((count, count), 1)
    slot_c = jnp.sum(jnp.where(eye, slot, 0), axis=1, keepdims=True)
    place[...] = one_hot(iota((slots, count), 0) == slot)
    place_t[...] = one_hot(iota((count, slots), 1) == slot_c)
    shift = (me_t % PER) * CAP
    for b in range(PER):
        source_lane = iota((LANES, LANES), 0)
        moved = source_lane - b * CAP + shift == iota((LANES, LANES), 1)
        turn[b] = one_hot(moved & (source_lane // CAP == b))

    def tiles(rows, height, target):
        groups = jnp.concatenate(
            [rows[:, g * LANES : (g + 1) * LANES] for g in range(blocks)], axis=0
        ).astype(BF16)
        for b in range(PER):
            moved = dot(groups, turn[b]).astype(BF16)
            for g in range(blocks):
                target[g * PER + b] = moved[g * height : (g + 1) * height]

    def gather_tiles(source, g):
        total = source[g * PER].astype(F32)
        for b in range(1, PER):
            total = total + source[g * PER + b].astype(F32)
        return total

    lengths = length[...]
    ends = stack_rows([(lengths // 8).astype(F32), (lengths % 8).astype(F32)], 8)
    fields = jnp.concatenate([table[...].astype(F32), ends], axis=0).astype(BF16)
    tiles(dot(fields, place_t[...]), FIELDS, send_m)

    pl.semaphore_wait(barrier, len(others) + len(peers))

    quarter = count // 4

    def gather_start(buffer, send_sem, recv_sem):
        def go(index, source, start, quarters, target):
            part = buffer.at[source, pl.ds(start * quarter, quarters * quarter)]
            return remote(part, part, send_sem.at[0], recv_sem.at[index], (me_t, target))

        copies = [
            go(0, me_h, 0, 1, h_up),
            go(1, me_h, 3, 1, h_down),
            go(2, me_h, 1, 1, h_up),
            go(3, me_h, 2, 1, h_down),
            go(4, me_h, 2, 2, h_up),
            go(5, me_h, 0, 2, h_down),
            go(6, me_h, 0, 4, sib),
        ]
        bulk(buffer, buffer, n_head - 1, send_sem.at[0], recv_sem.at[0])
        return go, copies

    def gather_rest(started, add):
        go, copies = started
        add(me_h)
        for k, (source, start, target) in enumerate(
            ((h_down, 0, h_up), (h_up, 3, h_down), (h_down, 1, h_up), (h_up, 2, h_down))
        ):
            copies[k].wait_recv()
            copies.append(go(7 + k, source, start, 1, target))
        copies.append(go(11, h_down, 0, 2, sib))
        copies.append(go(12, h_up, 2, 2, sib))
        copies[6].wait_recv()
        add(sib)
        copies[4].wait_recv()
        copies.append(go(13, h_down, 2, 2, sib))
        add(h_down)
        copies[5].wait_recv()
        copies.append(go(14, h_up, 0, 2, sib))
        add(h_up)
        copies[11].wait_recv()
        copies[13].wait_recv()
        add(a_down)
        copies[12].wait_recv()
        copies[14].wait_recv()
        add(a_up)
        for k, start in enumerate((0, 3, 1, 2)):
            copies[7 + k].wait_recv()
            copies.append(go(15 + k, h_far, start, 1, sib))
        add(h_far)
        for k in range(4):
            copies[15 + k].wait_recv()
        add(a_far)

    local_x.wait()
    started = gather_start(x, x_send, x_recv)
    meta_in = exchange(send_m, recv_m, m_sem)
    load_win.wait()
    load_pool = pltpu.make_async_copy(pool, pool_v, local_sem.at[2])
    load_pool.start()

    def add_query(source):
        rows = pl.ds(pl.multiple_of(source * features, features), features)
        proj[...] = proj[...] + dot(x[source], win_v[rows, 0 : 2 * QK])

    proj[...] = jnp.zeros(proj.shape, F32)
    gather_rest(started, add_query)

    query = proj[...].astype(BF16)
    send_q[...] = dot(place[...], query).astype(BF16).reshape(n_tok, CAP, 2 * QK)
    query_in = exchange(send_q, recv_q, q_sem)

    fresh = jnp.zeros((count, 2 * QK + VDIM), F32)
    for h in range(n_head):
        fresh = fresh + dot(x[h], win_v[h * features : (h + 1) * features, 2 * QK :])
    fresh = fresh.astype(BF16)
    v_new[...] = fresh[:, 2 * QK :]
    product = query.astype(F32) * fresh[:, 0 : 2 * QK].astype(F32)
    high, low = split(product, 2)
    ones = jnp.ones((8, QK), F32).astype(BF16)
    terms = []
    for m in range(2):
        part = slice(m * QK, (m + 1) * QK)
        total = dot_nt(ones, high[:, part].astype(BF16)) + dot_nt(ones, low[:, part].astype(BF16))
        terms += split(total[0:1] * SCALE, 3)
    tiles(dot(stack_rows(terms, TILE).astype(BF16), place_t[...]), TILE, send_s)
    self_in = exchange(send_s, recv_s, s_sem)

    def columns(h):
        return w_out.at[:, pl.ds(pl.multiple_of(h * features, features), features)]

    own_w = pltpu.make_async_copy(columns(me_h), wcol_v.at[me_h], local_sem.at[3])
    own_w.start()
    for h in (h_up, h_down, h_far, a_up, a_down, a_far, sib):
        remote(columns(h), wcol_v.at[me_h], w_sem.at[0], w_sem.at[1], (me_t, h))
    weights_in = bulk(wcol_v, wcol_v, n_head - 1, w_sem.at[0], w_sem.at[1])
    lam = (
        jnp.exp(jnp.sum(lq1[...] * lk1[...], axis=1, keepdims=True))
        - jnp.exp(jnp.sum(lq2[...] * lk2[...], axis=1, keepdims=True))
        + lambda_init
    )

    meta_in.wait_recv()
    whole = jnp.zeros((pages, LANES), F32)
    rest = jnp.zeros((pages, LANES), F32)
    page = iota((pages, LANES), 0).astype(F32)
    for g in range(blocks):
        cut = slice(g * LANES, (g + 1) * LANES)
        got = gather_tiles(recv_m, g)
        cached = got[8:9] * 8.0 + got[9:10]
        info[0:1, cut] = got[0:1]
        info[1:2, cut] = cached
        hit_any = jnp.zeros((pages, LANES), F32)
        for j in range(1, MAXP):
            left = cached - float(PAGE * j)
            number = jnp.where(left > 0.0, got[j : j + 1], -1.0)
            hit = number == page
            hit_any = jnp.where(hit, 1.0, hit_any)
            whole = whole + jnp.where(hit, jnp.where(left >= float(PAGE), 1.0, 0.0), 0.0)
            rest = rest + jnp.where(hit, jnp.where(left >= float(PAGE), 0.0, left), 0.0)
        match[:, cut] = hit_any.astype(BF16)
        match_t[cut] = jnp.transpose(jnp.concatenate([hit_any, hit_any], axis=0)).astype(BF16)
        chosen = jnp.transpose(jnp.broadcast_to(got[0:1], (LANES, LANES)))
        for p in range(SHARED):
            page0[p, cut] = one_hot(chosen == float(p))
    whole = jnp.sum(whole, axis=1, keepdims=True)
    rest = jnp.sum(rest, axis=1, keepdims=True)
    position = iota((pages, PAGE), 1).astype(F32)
    times[...] = whole + jnp.where(position < rest, 1.0, 0.0)
    load_pool.wait()
    query_in.wait_recv()

    queries = recv_q[...].reshape(slots, 2 * QK)
    found = dot(match[...], queries)
    side = iota((GROUP, 2 * QK), 1) < QK
    for g in range(pages // GROUP):
        mine = found[g * GROUP : (g + 1) * GROUP]
        both = [jnp.where(side, mine, 0.0), jnp.where(side, 0.0, mine)]
        page_q[2 * g * GROUP : 2 * (g + 1) * GROUP] = jnp.concatenate(both, axis=0).astype(BF16)
    half = slots // 2
    for h in range(2):
        cut = slice(h * half, (h + 1) * half)
        at = info[0:1, cut]
        for ref, lo in ((first_a, 0), (first_b, QK)):
            kept = None
            for p in range(0, SHARED, 2):
                keys = pool_v[p : p + 2].reshape(2 * PAGE, WIDE)[:, lo : lo + QK]
                score = dot_nt(keys, queries[cut, lo : lo + QK])
                chosen = jnp.where(at == float(p), score[0:PAGE], score[PAGE:])
                kept = chosen if p == 0 else jnp.where(at >= float(p), chosen, kept)
            ref[:, cut] = kept

    row = iota((2 * GROUP, LANES), 0) % GROUP
    for g in range(pages // GROUP):
        mine = slice(g * GROUP, (g + 1) * GROUP)
        keys = pool_v[mine].reshape(GROUP * PAGE, WIDE)[:, 0 : 2 * QK]
        score = dot_nt(page_q[2 * g * GROUP : 2 * (g + 1) * GROUP], keys)
        chosen = score[:, 0:PAGE]
        for i in range(1, GROUP):
            chosen = jnp.where(row == i, score[:, i * PAGE : (i + 1) * PAGE], chosen)
        priv_a[mine] = chosen[0:GROUP]
        priv_b[mine] = chosen[GROUP:]

    self_in.wait_recv()
    page_best = []
    for ref in (priv_a, priv_b):
        score = jnp.where(times[...] > 0.0, ref[...] * SCALE, NEG)
        ref[...] = score
        page_best.append(jnp.max(score, axis=1, keepdims=True))
    tops, selfs = [], []
    page_top = [jnp.zeros((pages, LANES), F32) for _ in range(2)]
    depth = iota((PAGE, LANES), 0).astype(F32)
    for g in range(blocks):
        cut = slice(g * LANES, (g + 1) * LANES)
        hit = match[:, cut].astype(F32) > 0.0
        got = gather_tiles(recv_s, g)
        valid = depth < info[1:2, cut]
        for m, ref in enumerate((first_a, first_b)):
            score = jnp.where(valid, ref[:, cut] * SCALE, NEG)
            ref[:, cut] = score
            mine = got[3 * m : 3 * m + 1] + got[3 * m + 1 : 3 * m + 2] + got[3 * m + 2 : 3 * m + 3]
            best = jnp.max(jnp.where(hit, page_best[m], NEG), axis=0, keepdims=True)
            top = jnp.maximum(jnp.maximum(jnp.max(score, axis=0, keepdims=True), best), mine)
            page_top[m] = page_top[m] + jnp.where(hit, top, 0.0)
            tops.append(top)
            selfs.append(mine)

    page_sum = []
    for m, ref in enumerate((priv_a, priv_b)):
        top = jnp.sum(page_top[m], axis=1, keepdims=True)
        weight = jnp.where(times[...] > 0.0, jnp.exp2(ref[...] - top) * times[...], 0.0)
        ref[...] = weight
        page_sum.append(jnp.sum(weight, axis=1, keepdims=True))
    page_coef = [jnp.zeros((pages, LANES), F32) for _ in range(2)]
    own_rows = []
    for g in range(blocks):
        cut = slice(g * LANES, (g + 1) * LANES)
        hit = match[:, cut].astype(F32) > 0.0
        mixed, own_coef = None, None
        for m, ref in enumerate((first_a, first_b)):
            top = tops[2 * g + m]
            weight = jnp.exp2(ref[:, cut] - top)
            new = jnp.exp2(selfs[2 * g + m] - top)
            total = (
                new
                + jnp.sum(weight, axis=0, keepdims=True)
                + jnp.sum(jnp.where(hit, page_sum[m], 0.0), axis=0, keepdims=True)
            )
            coef = 1.0 / total if m == 0 else -lam / total
            page_coef[m] = page_coef[m] + jnp.where(hit, coef, 0.0)
            mixed = weight * coef if m == 0 else mixed + weight * coef
            own_coef = new * coef if m == 0 else own_coef + new * coef
        mixed = jnp.transpose(mixed).astype(BF16)
        for p in range(SHARED):
            wide[cut, p * PAGE : (p + 1) * PAGE] = mixed * page0[p, cut]
        own_rows.append(stack_rows(split(own_coef, 2), TILE))
    tiles(jnp.concatenate(own_rows, axis=1), TILE, send_c)
    coef_in = exchange(send_c, recv_c, c_sem)

    priv_a[...] = priv_a[...] * jnp.sum(page_coef[0], axis=1, keepdims=True) + priv_b[
        ...
    ] * jnp.sum(page_coef[1], axis=1, keepdims=True)

    row = iota((GROUP, LANES), 0)
    for g in range(pages // GROUP):
        mine = slice(g * GROUP, (g + 1) * GROUP)
        values = pool_v[mine].reshape(GROUP * PAGE, WIDE)[:, 2 * QK :]
        weight = priv_a[mine]
        spread = jnp.concatenate(
            [jnp.where(row == i, weight, 0.0) for i in range(GROUP)], axis=1
        ).astype(BF16)
        page_out[mine] = dot(spread, values)
    high, low = split(page_out[...], 2)
    pair = jnp.concatenate([high, low], axis=0).astype(BF16)
    values = pool_v[0:SHARED].reshape(SHARED * PAGE, WIDE)[:, 2 * QK :]
    result = dot(wide[...], values) + dot(match_t[...], pair)
    send_r[...] = result.astype(BF16).reshape(n_tok, CAP, VDIM)

    mixed_in = exchange(send_r, recv_r, r_sem)
    own_w.wait()
    coef_in.wait_recv()
    rows = jnp.concatenate([gather_tiles(recv_c, g) for g in range(blocks)], axis=1)
    coefs = dot_nt(place_t[...], rows.astype(BF16))
    addend = (coefs[:, 0:1] + coefs[:, 1:2]) * v_new[...].astype(F32)
    mixed_in.wait_recv()
    mixed = dot(place_t[...], recv_r[...].reshape(slots, VDIM)) + addend
    scale = lax.rsqrt(jnp.mean(mixed * mixed, axis=1, keepdims=True) + norm_eps)
    heads[me_h] = (mixed * scale * gain[...] * (1.0 - lambda_init)).astype(BF16)

    started = gather_start(heads, h_send, h_recv)
    weights_in.wait_recv()
    proj[...] = jnp.zeros(proj.shape, F32)

    def add_out(source):
        proj[...] = proj[...] + dot(heads[source], wcol_v[source])

    gather_rest(started, add_out)
    out[...] = proj[...].astype(BF16)
    for copy in sent:
        copy.wait_send()


def on_device(sizes, tokens, w_in, w_out, gain, lq1, lk1, lq2, lk2, pool, table, length, owner):
    n_tok, n_head, count, features = sizes
    slots = n_tok * CAP
    pages = pool.shape[0]
    vmem = pl.BlockSpec(memory_space=pltpu.VMEM)
    hbm = pl.BlockSpec(memory_space=pltpu.HBM)
    dma = pltpu.SemaphoreType.DMA
    return pl.pallas_call(
        functools.partial(step_kernel, sizes),
        out_shape=pltpu.VMEM((count, features), BF16),
        in_specs=[hbm] * 12,
        out_specs=vmem,
        scratch_shapes=[
            pltpu.VMEM((1, VDIM), F32),
            pltpu.VMEM((1, QK), F32),
            pltpu.VMEM((1, QK), F32),
            pltpu.VMEM((1, QK), F32),
            pltpu.VMEM((1, QK), F32),
            pltpu.VMEM((MAXP, count), jnp.int32),
            pltpu.VMEM((1, count), jnp.int32),
            pltpu.VMEM((1, count), jnp.int32),
            pltpu.VMEM((n_head, count, features), BF16),
            pltpu.VMEM(w_in.shape, BF16),
            pltpu.VMEM((n_head, VDIM, features), BF16),
            pltpu.VMEM((pages, PAGE, WIDE), BF16),
            pltpu.VMEM((n_head, count, VDIM), BF16),
            pltpu.VMEM((slots, count), BF16),
            pltpu.VMEM((count, slots), BF16),
            pltpu.VMEM((PER, LANES, LANES), BF16),
            pltpu.VMEM((count, 2 * QK), F32),
            pltpu.VMEM((count, VDIM), BF16),
            pltpu.VMEM((n_tok, FIELDS, LANES), BF16),
            pltpu.VMEM((n_tok, FIELDS, LANES), BF16),
            pltpu.VMEM((n_tok, CAP, 2 * QK), BF16),
            pltpu.VMEM((n_tok, CAP, 2 * QK), BF16),
            pltpu.VMEM((n_tok, TILE, LANES), BF16),
            pltpu.VMEM((n_tok, TILE, LANES), BF16),
            pltpu.VMEM((n_tok, CAP, VDIM), BF16),
            pltpu.VMEM((n_tok, CAP, VDIM), BF16),
            pltpu.VMEM((n_tok, TILE, LANES), BF16),
            pltpu.VMEM((n_tok, TILE, LANES), BF16),
            pltpu.VMEM((8, slots), F32),
            pltpu.VMEM((pages, slots), BF16),
            pltpu.VMEM((slots, 2 * pages), BF16),
            pltpu.VMEM((pages, PAGE), F32),
            pltpu.VMEM((SHARED, slots, PAGE), BF16),
            pltpu.VMEM((PAGE, slots), F32),
            pltpu.VMEM((PAGE, slots), F32),
            pltpu.VMEM((2 * pages, 2 * QK), BF16),
            pltpu.VMEM((pages, PAGE), F32),
            pltpu.VMEM((pages, PAGE), F32),
            pltpu.VMEM((pages, VDIM), F32),
            pltpu.VMEM((slots, SHARED * PAGE), BF16),
            dma((12,)),
        ]
        + [dma((number,)) for number in (1, 19, 2, 2, 2, 2, 2, 2, 1, 19)],
        compiler_params=pltpu.CompilerParams(
            collective_id=0, has_side_effects=True, vmem_limit_bytes=60 * 1024 * 1024
        ),
        name="decode_step",
    )(
        tokens,
        w_in,
        w_out,
        pool.reshape(pages, PAGE, WIDE),
        gain.reshape(1, VDIM),
        lq1.reshape(1, QK),
        lk1.reshape(1, QK),
        lq2.reshape(1, QK),
        lk2.reshape(1, QK),
        jnp.transpose(table),
        length.reshape(1, count),
        owner.reshape(1, count),
    )


def solution(mesh):
    n_tok, n_head = mesh.shape["tok"], mesh.shape["head"]

    def run(
        tokens,
        input_weight,
        output_weight,
        head_gain,
        query_lambda_one,
        key_lambda_one,
        query_lambda_two,
        key_lambda_two,
        cache_pool,
        page_table,
        cache_length,
        cache_owner,
    ):
        sizes = (n_tok, n_head, tokens.shape[0] // n_tok, tokens.shape[1] // n_head)
        placed = (
            P("tok", "head"),
            P(None, "head"),
            P("head", None),
            P("head"),
            P(),
            P(),
            P(),
            P(),
            P("tok", "head", None, None),
            P("tok", None),
            P("tok"),
            P("tok", None),
        )
        return jax.shard_map(
            functools.partial(on_device, sizes),
            mesh=mesh,
            in_specs=placed,
            out_specs=P("tok", "head"),
            check_vma=False,
        )(
            tokens,
            input_weight,
            output_weight,
            head_gain,
            query_lambda_one,
            key_lambda_one,
            query_lambda_two,
            key_lambda_two,
            cache_pool,
            page_table,
            cache_length,
            cache_owner,
        )

    return run
```

```python
import functools
import math

import jax
import jax.numpy as jnp
from jax import lax
from jax.experimental import pallas as pl
from jax.experimental.pallas import tpu as pltpu
from jax.sharding import PartitionSpec as P

QK = 128
VDIM = 256
PAGE = 128
CAP = 32
SHARED = 8
MAXP = 8
GROUP = 16
LANES = 128
FIELDS = 16
TILE = 8
PER = LANES // CAP
WIDE = 2 * QK + VDIM

lambda_init = 0.8
norm_eps = 1e-05
NEG = -1e30
SCALE = math.log2(math.e) / math.sqrt(QK)
MESH = pl.DeviceIdType.MESH
F32 = jnp.float32
BF16 = jnp.bfloat16


def iota(shape, dim):
    return lax.broadcasted_iota(jnp.int32, shape, dim)


def one_hot(condition):
    return condition.astype(F32).astype(BF16)


def dot(a, b):
    return jnp.dot(a, b, preferred_element_type=F32)


def dot_nt(a, b):
    return lax.dot_general(a, b, (((1,), (1,)), ((), ())), preferred_element_type=F32)


def split(value, terms):
    parts = []
    for _ in range(terms - 1):
        high = value.astype(BF16).astype(F32)
        parts.append(high)
        value = value - high
    return parts + [value]


def stack_rows(rows, height):
    row = iota((height, rows[0].shape[1]), 0)
    stacked = jnp.where(row == 0, rows[0], 0.0)
    for index in range(1, len(rows)):
        stacked = jnp.where(row == index, rows[index], stacked)
    return stacked


def step_kernel(
    sizes,
    tokens,
    w_in,
    w_out,
    pool,
    gain_h,
    lq1_h,
    lk1_h,
    lq2_h,
    lk2_h,
    table_h,
    length_h,
    owner_h,
    out,
    gain,
    lq1,
    lk1,
    lq2,
    lk2,
    table,
    length,
    owner,
    x,
    win_v,
    wcol_v,
    pool_v,
    heads,
    place,
    place_t,
    turn,
    proj,
    v_new,
    send_m,
    recv_m,
    send_q,
    recv_q,
    send_s,
    recv_s,
    send_r,
    recv_r,
    send_c,
    recv_c,
    info,
    match,
    match_t,
    times,
    page0,
    first_a,
    first_b,
    page_q,
    priv_a,
    priv_b,
    page_out,
    wide,
    greet_sem,
    local_sem,
    x_send,
    x_recv,
    m_sem,
    q_sem,
    s_sem,
    w_sem,
    c_sem,
    r_sem,
    h_send,
    h_recv,
):
    n_tok, n_head, count, features = sizes
    slots = n_tok * CAP
    blocks = slots // LANES
    pages = pool.shape[0]
    ny = n_head // 2
    nx = 4
    nz = n_tok // nx
    me_t = lax.axis_index("tok")
    me_h = lax.axis_index("head")
    y, core = me_h // 2, me_h % 2
    z_at, x_at = me_t // nx, me_t % nx
    up, down, far = (y + 1) % ny, (y + ny - 1) % ny, (y + 2) % ny
    sib = y * 2 + 1 - core
    h_up, h_down, h_far = up * 2 + core, down * 2 + core, far * 2 + core
    a_up, a_down, a_far = up * 2 + 1 - core, down * 2 + 1 - core, far * 2 + 1 - core

    offsets = [(dz, dx) for dz in range(nz) for dx in range(nx) if dz + dx > 0]
    offsets.sort(key=lambda o: -(min(o[0], nz - o[0]) + min(o[1], nx - o[1])))
    peers = [((z_at + dz) % nz) * nx + (x_at + dx) % nx for dz, dx in offsets]

    barrier = pltpu.get_barrier_semaphore()
    x_near = [z_at * nx + (x_at + d) % nx for d in (1, nx - 1)]
    z_near = [(z_at + d) % nz * nx + x_at for d in (1, nz - 1)]
    for peer in (sib, h_up, h_down):
        pl.semaphore_signal(barrier, inc=1, device_id=(me_t, peer), device_id_type=MESH)
    for peer in x_near + z_near:
        pl.semaphore_signal(barrier, inc=1, device_id=(peer, me_h), device_id_type=MESH)

    def greet(step):
        if step > 0:
            pl.semaphore_wait(greet_sem.at[step - 1], 2)
        if step < 3:
            for peer in (x_near, z_near, z_near)[step]:
                pl.semaphore_signal(
                    greet_sem.at[step], inc=1, device_id=(peer, me_h), device_id_type=MESH
                )

    sent = []

    def remote(source, target, send_sem, recv_sem, device):
        copy = pltpu.make_async_remote_copy(
            src_ref=source,
            dst_ref=target,
            send_sem=send_sem,
            recv_sem=recv_sem,
            device_id=device,
            device_id_type=MESH,
        )
        copy.start()
        return copy

    def bulk(source, target, blocks_of, send_sem, recv_sem):
        some = pl.ds(0, blocks_of)
        copy = pltpu.make_async_remote_copy(
            src_ref=source.at[some],
            dst_ref=target.at[some],
            send_sem=send_sem,
            recv_sem=recv_sem,
            device_id=(me_t, sib),
            device_id_type=MESH,
        )
        sent.append(copy)
        return copy

    def exchange(source, target, sems):
        for p in peers:
            remote(source.at[p], target.at[me_t], sems.at[0], sems.at[1], (p, me_h))
        target[me_t] = source[me_t]
        return bulk(source, target, len(peers), sems.at[0], sems.at[1])

    local_x = pltpu.make_async_copy(tokens, x.at[me_h], local_sem.at[0])
    local_x.start()
    load_win = pltpu.make_async_copy(w_in, win_v, local_sem.at[1])
    load_win.start()

    small = [
        pltpu.make_async_copy(source, target, local_sem.at[4 + k])
        for k, (source, target) in enumerate(
            (
                (owner_h, owner),
                (table_h, table),
                (length_h, length),
                (gain_h, gain),
                (lq1_h, lq1),
                (lk1_h, lk1),
                (lq2_h, lq2),
                (lk2_h, lk2),
            )
        )
    ]
    for load in small:
        load.start()
    for load in small:
        load.wait()

    own = owner[...]
    named = own == iota((n_tok, count), 0)
    earlier = one_hot(iota((count, count), 0) < iota((count, count), 1))
    before = dot(one_hot(named), earlier)
    rank = jnp.sum(jnp.where(named, before, 0.0), axis=0, keepdims=True)
    slot = own * CAP + rank.astype(jnp.int32)
    eye = iota((count, count), 0) == iota((count, count), 1)
    slot_c = jnp.sum(jnp.where(eye, slot, 0), axis=1, keepdims=True)
    place[...] = one_hot(iota((slots, count), 0) == slot)
    place_t[...] = one_hot(iota((count, slots), 1) == slot_c)
    shift = (me_t % PER) * CAP
    for b in range(PER):
        source_lane = iota((LANES, LANES), 0)
        moved = source_lane - b * CAP + shift == iota((LANES, LANES), 1)
        turn[b] = one_hot(moved & (source_lane // CAP == b))

    def tiles(rows, height, target):
        groups = jnp.concatenate(
            [rows[:, g * LANES : (g + 1) * LANES] for g in range(blocks)], axis=0
        ).astype(BF16)
        for b in range(PER):
            moved = dot(groups, turn[b]).astype(BF16)
            for g in range(blocks):
                target[g * PER + b] = moved[g * height : (g + 1) * height]

    def gather_tiles(source, g):
        total = source[g * PER].astype(F32)
        for b in range(1, PER):
            total = total + source[g * PER + b].astype(F32)
        return total

    lengths = length[...]
    ends = stack_rows([(lengths // 8).astype(F32), (lengths % 8).astype(F32)], 8)
    fields = jnp.concatenate([table[...].astype(F32), ends], axis=0).astype(BF16)
    tiles(dot(fields, place_t[...]), FIELDS, send_m)

    pl.semaphore_wait(barrier, 3 + len(x_near) + len(z_near))

    quarter = count // 4

    def gather_start(buffer, send_sem, recv_sem):
        def go(index, source, start, quarters, target):
            part = buffer.at[source, pl.ds(start * quarter, quarters * quarter)]
            return remote(part, part, send_sem.at[0], recv_sem.at[index], (me_t, target))

        copies = [
            go(0, me_h, 0, 1, h_up),
            go(1, me_h, 3, 1, h_down),
            go(2, me_h, 1, 1, h_up),
            go(3, me_h, 2, 1, h_down),
            go(4, me_h, 2, 2, h_up),
            go(5, me_h, 0, 2, h_down),
            go(6, me_h, 0, 4, sib),
        ]
        bulk(buffer, buffer, n_head - 1, send_sem.at[0], recv_sem.at[0])
        return go, copies

    def gather_rest(started, add, beside):
        go, copies = started
        add(me_h)
        for k, (source, start, target) in enumerate(
            ((h_down, 0, h_up), (h_up, 3, h_down), (h_down, 1, h_up), (h_up, 2, h_down))
        ):
            copies[k].wait_recv()
            copies.append(go(7 + k, source, start, 1, target))
        copies.append(go(11, h_down, 0, 2, sib))
        copies.append(go(12, h_up, 2, 2, sib))
        beside(1)
        copies[6].wait_recv()
        add(sib)
        copies[4].wait_recv()
        copies.append(go(13, h_down, 2, 2, sib))
        add(h_down)
        copies[5].wait_recv()
        copies.append(go(14, h_up, 0, 2, sib))
        add(h_up)
        beside(2)
        copies[11].wait_recv()
        copies[13].wait_recv()
        add(a_down)
        copies[12].wait_recv()
        copies[14].wait_recv()
        add(a_up)
        for k, start in enumerate((0, 3, 1, 2)):
            copies[7 + k].wait_recv()
            copies.append(go(15 + k, h_far, start, 1, sib))
        beside(3)
        add(h_far)
        for k in range(4):
            copies[15 + k].wait_recv()
        add(a_far)

    local_x.wait()
    started = gather_start(x, x_send, x_recv)
    greet(0)
    load_win.wait()
    load_pool = pltpu.make_async_copy(pool, pool_v, local_sem.at[2])
    load_pool.start()

    def add_query(source):
        rows = pl.ds(pl.multiple_of(source * features, features), features)
        proj[...] = proj[...] + dot(x[source], win_v[rows, 0 : 2 * QK])

    proj[...] = jnp.zeros(proj.shape, F32)
    arriving = []

    def beside_gather(step):
        greet(step)
        if step == 3:
            arriving.append(exchange(send_m, recv_m, m_sem))

    gather_rest(started, add_query, beside_gather)

    query = proj[...].astype(BF16)
    send_q[...] = dot(place[...], query).astype(BF16).reshape(n_tok, CAP, 2 * QK)
    query_in = exchange(send_q, recv_q, q_sem)

    fresh = jnp.zeros((count, 2 * QK + VDIM), F32)
    for h in range(n_head):
        fresh = fresh + dot(x[h], win_v[h * features : (h + 1) * features, 2 * QK :])
    fresh = fresh.astype(BF16)
    v_new[...] = fresh[:, 2 * QK :]
    product = query.astype(F32) * fresh[:, 0 : 2 * QK].astype(F32)
    high, low = split(product, 2)
    ones = jnp.ones((8, QK), F32).astype(BF16)
    terms = []
    for m in range(2):
        part = slice(m * QK, (m + 1) * QK)
        total = dot_nt(ones, high[:, part].astype(BF16)) + dot_nt(ones, low[:, part].astype(BF16))
        terms += split(total[0:1] * SCALE, 3)
    tiles(dot(stack_rows(terms, TILE).astype(BF16), place_t[...]), TILE, send_s)
    self_in = exchange(send_s, recv_s, s_sem)

    def columns(h):
        return w_out.at[:, pl.ds(pl.multiple_of(h * features, features), features)]

    own_w = pltpu.make_async_copy(columns(me_h), wcol_v.at[me_h], local_sem.at[3])
    own_w.start()
    for h in (h_up, h_down, h_far, a_up, a_down, a_far, sib):
        remote(columns(h), wcol_v.at[me_h], w_sem.at[0], w_sem.at[1], (me_t, h))
    weights_in = bulk(wcol_v, wcol_v, n_head - 1, w_sem.at[0], w_sem.at[1])
    lam = (
        jnp.exp(jnp.sum(lq1[...] * lk1[...], axis=1, keepdims=True))
        - jnp.exp(jnp.sum(lq2[...] * lk2[...], axis=1, keepdims=True))
        + lambda_init
    )

    arriving[0].wait_recv()
    whole = jnp.zeros((pages, LANES), F32)
    rest = jnp.zeros((pages, LANES), F32)
    page = iota((pages, LANES), 0).astype(F32)
    for g in range(blocks):
        cut = slice(g * LANES, (g + 1) * LANES)
        got = gather_tiles(recv_m, g)
        cached = got[8:9] * 8.0 + got[9:10]
        info[0:1, cut] = got[0:1]
        info[1:2, cut] = cached
        hit_any = jnp.zeros((pages, LANES), F32)
        for j in range(1, MAXP):
            left = cached - float(PAGE * j)
            number = jnp.where(left > 0.0, got[j : j + 1], -1.0)
            hit = number == page
            hit_any = jnp.where(hit, 1.0, hit_any)
            whole = whole + jnp.where(hit, jnp.where(left >= float(PAGE), 1.0, 0.0), 0.0)
            rest = rest + jnp.where(hit, jnp.where(left >= float(PAGE), 0.0, left), 0.0)
        match[:, cut] = hit_any.astype(BF16)
        match_t[cut] = jnp.transpose(jnp.concatenate([hit_any, hit_any], axis=0)).astype(BF16)
        chosen = jnp.transpose(jnp.broadcast_to(got[0:1], (LANES, LANES)))
        for p in range(SHARED):
            page0[p, cut] = one_hot(chosen == float(p))
    whole = jnp.sum(whole, axis=1, keepdims=True)
    rest = jnp.sum(rest, axis=1, keepdims=True)
    position = iota((pages, PAGE), 1).astype(F32)
    times[...] = whole + jnp.where(position < rest, 1.0, 0.0)
    load_pool.wait()
    query_in.wait_recv()

    queries = recv_q[...].reshape(slots, 2 * QK)
    found = dot(match[...], queries)
    side = iota((GROUP, 2 * QK), 1) < QK
    for g in range(pages // GROUP):
        mine = found[g * GROUP : (g + 1) * GROUP]
        both = [jnp.where(side, mine, 0.0), jnp.where(side, 0.0, mine)]
        page_q[2 * g * GROUP : 2 * (g + 1) * GROUP] = jnp.concatenate(both, axis=0).astype(BF16)
    half = slots // 2
    for h in range(2):
        cut = slice(h * half, (h + 1) * half)
        at = info[0:1, cut]
        for ref, lo in ((first_a, 0), (first_b, QK)):
            kept = None
            for p in range(0, SHARED, 2):
                keys = pool_v[p : p + 2].reshape(2 * PAGE, WIDE)[:, lo : lo + QK]
                score = dot_nt(keys, queries[cut, lo : lo + QK])
                chosen = jnp.where(at == float(p), score[0:PAGE], score[PAGE:])
                kept = chosen if p == 0 else jnp.where(at >= float(p), chosen, kept)
            ref[:, cut] = kept

    row = iota((2 * GROUP, LANES), 0) % GROUP
    for g in range(pages // GROUP):
        mine = slice(g * GROUP, (g + 1) * GROUP)
        keys = pool_v[mine].reshape(GROUP * PAGE, WIDE)[:, 0 : 2 * QK]
        score = dot_nt(page_q[2 * g * GROUP : 2 * (g + 1) * GROUP], keys)
        chosen = score[:, 0:PAGE]
        for i in range(1, GROUP):
            chosen = jnp.where(row == i, score[:, i * PAGE : (i + 1) * PAGE], chosen)
        priv_a[mine] = chosen[0:GROUP]
        priv_b[mine] = chosen[GROUP:]

    self_in.wait_recv()
    page_best = []
    for ref in (priv_a, priv_b):
        score = jnp.where(times[...] > 0.0, ref[...] * SCALE, NEG)
        ref[...] = score
        page_best.append(jnp.max(score, axis=1, keepdims=True))
    tops, selfs = [], []
    page_top = [jnp.zeros((pages, LANES), F32) for _ in range(2)]
    depth = iota((PAGE, LANES), 0).astype(F32)
    for g in range(blocks):
        cut = slice(g * LANES, (g + 1) * LANES)
        hit = match[:, cut].astype(F32) > 0.0
        got = gather_tiles(recv_s, g)
        valid = depth < info[1:2, cut]
        for m, ref in enumerate((first_a, first_b)):
            score = jnp.where(valid, ref[:, cut] * SCALE, NEG)
            ref[:, cut] = score
            mine = got[3 * m : 3 * m + 1] + got[3 * m + 1 : 3 * m + 2] + got[3 * m + 2 : 3 * m + 3]
            best = jnp.max(jnp.where(hit, page_best[m], NEG), axis=0, keepdims=True)
            top = jnp.maximum(jnp.maximum(jnp.max(score, axis=0, keepdims=True), best), mine)
            page_top[m] = page_top[m] + jnp.where(hit, top, 0.0)
            tops.append(top)
            selfs.append(mine)

    page_sum = []
    for m, ref in enumerate((priv_a, priv_b)):
        top = jnp.sum(page_top[m], axis=1, keepdims=True)
        weight = jnp.where(times[...] > 0.0, jnp.exp2(ref[...] - top) * times[...], 0.0)
        ref[...] = weight
        page_sum.append(jnp.sum(weight, axis=1, keepdims=True))
    page_coef = [jnp.zeros((pages, LANES), F32) for _ in range(2)]
    own_rows = []
    for g in range(blocks):
        cut = slice(g * LANES, (g + 1) * LANES)
        hit = match[:, cut].astype(F32) > 0.0
        mixed, own_coef = None, None
        for m, ref in enumerate((first_a, first_b)):
            top = tops[2 * g + m]
            weight = jnp.exp2(ref[:, cut] - top)
            new = jnp.exp2(selfs[2 * g + m] - top)
            total = (
                new
                + jnp.sum(weight, axis=0, keepdims=True)
                + jnp.sum(jnp.where(hit, page_sum[m], 0.0), axis=0, keepdims=True)
            )
            coef = 1.0 / total if m == 0 else -lam / total
            page_coef[m] = page_coef[m] + jnp.where(hit, coef, 0.0)
            mixed = weight * coef if m == 0 else mixed + weight * coef
            own_coef = new * coef if m == 0 else own_coef + new * coef
        mixed = jnp.transpose(mixed).astype(BF16)
        for p in range(SHARED):
            wide[cut, p * PAGE : (p + 1) * PAGE] = mixed * page0[p, cut]
        own_rows.append(stack_rows(split(own_coef, 2), TILE))
    tiles(jnp.concatenate(own_rows, axis=1), TILE, send_c)
    coef_in = exchange(send_c, recv_c, c_sem)

    priv_a[...] = priv_a[...] * jnp.sum(page_coef[0], axis=1, keepdims=True) + priv_b[
        ...
    ] * jnp.sum(page_coef[1], axis=1, keepdims=True)

    row = iota((GROUP, LANES), 0)
    for g in range(pages // GROUP):
        mine = slice(g * GROUP, (g + 1) * GROUP)
        values = pool_v[mine].reshape(GROUP * PAGE, WIDE)[:, 2 * QK :]
        weight = priv_a[mine]
        spread = jnp.concatenate(
            [jnp.where(row == i, weight, 0.0) for i in range(GROUP)], axis=1
        ).astype(BF16)
        page_out[mine] = dot(spread, values)
    high, low = split(page_out[...], 2)
    pair = jnp.concatenate([high, low], axis=0).astype(BF16)
    values = pool_v[0:SHARED].reshape(SHARED * PAGE, WIDE)[:, 2 * QK :]
    result = dot(wide[...], values) + dot(match_t[...], pair)
    send_r[...] = result.astype(BF16).reshape(n_tok, CAP, VDIM)

    mixed_in = exchange(send_r, recv_r, r_sem)
    own_w.wait()
    coef_in.wait_recv()
    rows = jnp.concatenate([gather_tiles(recv_c, g) for g in range(blocks)], axis=1)
    coefs = dot_nt(place_t[...], rows.astype(BF16))
    addend = (coefs[:, 0:1] + coefs[:, 1:2]) * v_new[...].astype(F32)
    mixed_in.wait_recv()
    mixed = dot(place_t[...], recv_r[...].reshape(slots, VDIM)) + addend
    scale = lax.rsqrt(jnp.mean(mixed * mixed, axis=1, keepdims=True) + norm_eps)
    heads[me_h] = (mixed * scale * gain[...] * (1.0 - lambda_init)).astype(BF16)

    started = gather_start(heads, h_send, h_recv)
    weights_in.wait_recv()
    proj[...] = jnp.zeros(proj.shape, F32)

    def add_out(source):
        proj[...] = proj[...] + dot(heads[source], wcol_v[source])

    gather_rest(started, add_out, lambda step: None)
    out[...] = proj[...].astype(BF16)
    for copy in sent:
        copy.wait_send()


def on_device(sizes, tokens, w_in, w_out, gain, lq1, lk1, lq2, lk2, pool, table, length, owner):
    n_tok, n_head, count, features = sizes
    slots = n_tok * CAP
    pages = pool.shape[0]
    vmem = pl.BlockSpec(memory_space=pltpu.VMEM)
    hbm = pl.BlockSpec(memory_space=pltpu.HBM)
    dma = pltpu.SemaphoreType.DMA
    return pl.pallas_call(
        functools.partial(step_kernel, sizes),
        out_shape=pltpu.VMEM((count, features), BF16),
        in_specs=[hbm] * 12,
        out_specs=vmem,
        scratch_shapes=[
            pltpu.VMEM((1, VDIM), F32),
            pltpu.VMEM((1, QK), F32),
            pltpu.VMEM((1, QK), F32),
            pltpu.VMEM((1, QK), F32),
            pltpu.VMEM((1, QK), F32),
            pltpu.VMEM((MAXP, count), jnp.int32),
            pltpu.VMEM((1, count), jnp.int32),
            pltpu.VMEM((1, count), jnp.int32),
            pltpu.VMEM((n_head, count, features), BF16),
            pltpu.VMEM(w_in.shape, BF16),
            pltpu.VMEM((n_head, VDIM, features), BF16),
            pltpu.VMEM((pages, PAGE, WIDE), BF16),
            pltpu.VMEM((n_head, count, VDIM), BF16),
            pltpu.VMEM((slots, count), BF16),
            pltpu.VMEM((count, slots), BF16),
            pltpu.VMEM((PER, LANES, LANES), BF16),
            pltpu.VMEM((count, 2 * QK), F32),
            pltpu.VMEM((count, VDIM), BF16),
            pltpu.VMEM((n_tok, FIELDS, LANES), BF16),
            pltpu.VMEM((n_tok, FIELDS, LANES), BF16),
            pltpu.VMEM((n_tok, CAP, 2 * QK), BF16),
            pltpu.VMEM((n_tok, CAP, 2 * QK), BF16),
            pltpu.VMEM((n_tok, TILE, LANES), BF16),
            pltpu.VMEM((n_tok, TILE, LANES), BF16),
            pltpu.VMEM((n_tok, CAP, VDIM), BF16),
            pltpu.VMEM((n_tok, CAP, VDIM), BF16),
            pltpu.VMEM((n_tok, TILE, LANES), BF16),
            pltpu.VMEM((n_tok, TILE, LANES), BF16),
            pltpu.VMEM((8, slots), F32),
            pltpu.VMEM((pages, slots), BF16),
            pltpu.VMEM((slots, 2 * pages), BF16),
            pltpu.VMEM((pages, PAGE), F32),
            pltpu.VMEM((SHARED, slots, PAGE), BF16),
            pltpu.VMEM((PAGE, slots), F32),
            pltpu.VMEM((PAGE, slots), F32),
            pltpu.VMEM((2 * pages, 2 * QK), BF16),
            pltpu.VMEM((pages, PAGE), F32),
            pltpu.VMEM((pages, PAGE), F32),
            pltpu.VMEM((pages, VDIM), F32),
            pltpu.VMEM((slots, SHARED * PAGE), BF16),
            pltpu.SemaphoreType.REGULAR((3,)),
            dma((12,)),
        ]
        + [dma((number,)) for number in (1, 19, 2, 2, 2, 2, 2, 2, 1, 19)],
        compiler_params=pltpu.CompilerParams(
            collective_id=0, has_side_effects=True, vmem_limit_bytes=60 * 1024 * 1024
        ),
        name="decode_step",
    )(
        tokens,
        w_in,
        w_out,
        pool.reshape(pages, PAGE, WIDE),
        gain.reshape(1, VDIM),
        lq1.reshape(1, QK),
        lk1.reshape(1, QK),
        lq2.reshape(1, QK),
        lk2.reshape(1, QK),
        jnp.transpose(table),
        length.reshape(1, count),
        owner.reshape(1, count),
    )


def solution(mesh):
    n_tok, n_head = mesh.shape["tok"], mesh.shape["head"]

    def run(
        tokens,
        input_weight,
        output_weight,
        head_gain,
        query_lambda_one,
        key_lambda_one,
        query_lambda_two,
        key_lambda_two,
        cache_pool,
        page_table,
        cache_length,
        cache_owner,
    ):
        sizes = (n_tok, n_head, tokens.shape[0] // n_tok, tokens.shape[1] // n_head)
        placed = (
            P("tok", "head"),
            P(None, "head"),
            P("head", None),
            P("head"),
            P(),
            P(),
            P(),
            P(),
            P("tok", "head", None, None),
            P("tok", None),
            P("tok"),
            P("tok", None),
        )
        return jax.shard_map(
            functools.partial(on_device, sizes),
            mesh=mesh,
            in_specs=placed,
            out_specs=P("tok", "head"),
            check_vma=False,
        )(
            tokens,
            input_weight,
            output_weight,
            head_gain,
            query_lambda_one,
            key_lambda_one,
            query_lambda_two,
            key_lambda_two,
            cache_pool,
            page_table,
            cache_length,
            cache_owner,
        )

    return run
```

```python
import functools
import math

import jax
import jax.numpy as jnp
from jax import lax
from jax.experimental import pallas as pl
from jax.experimental.pallas import tpu as pltpu
from jax.sharding import PartitionSpec as P

QK = 128
VDIM = 256
PAGE = 128
CAP = 32
SHARED = 8
MAXP = 8
GROUP = 16
LANES = 128
FIELDS = 16
TILE = 8
PER = LANES // CAP
WIDE = 2 * QK + VDIM

lambda_init = 0.8
norm_eps = 1e-05
NEG = -1e30
SCALE = math.log2(math.e) / math.sqrt(QK)
MESH = pl.DeviceIdType.MESH
F32 = jnp.float32
BF16 = jnp.bfloat16


def iota(shape, dim):
    return lax.broadcasted_iota(jnp.int32, shape, dim)


def one_hot(condition):
    return condition.astype(F32).astype(BF16)


def dot(a, b):
    return jnp.dot(a, b, preferred_element_type=F32)


def dot_nt(a, b):
    return lax.dot_general(a, b, (((1,), (1,)), ((), ())), preferred_element_type=F32)


def split(value, terms):
    parts = []
    for _ in range(terms - 1):
        high = value.astype(BF16).astype(F32)
        parts.append(high)
        value = value - high
    return parts + [value]


def stack_rows(rows, height):
    row = iota((height, rows[0].shape[1]), 0)
    stacked = jnp.where(row == 0, rows[0], 0.0)
    for index in range(1, len(rows)):
        stacked = jnp.where(row == index, rows[index], stacked)
    return stacked


def step_kernel(
    sizes,
    tokens,
    w_in,
    w_out,
    pool,
    gain_h,
    lq1_h,
    lk1_h,
    lq2_h,
    lk2_h,
    table_h,
    length_h,
    owner_h,
    out,
    gain,
    lq1,
    lk1,
    lq2,
    lk2,
    table,
    length,
    owner,
    x,
    win_v,
    wcol_v,
    pool_v,
    heads,
    place,
    place_t,
    turn,
    proj,
    v_new,
    send_m,
    recv_m,
    send_q,
    recv_q,
    send_s,
    recv_s,
    send_r,
    recv_r,
    send_c,
    recv_c,
    info,
    match,
    match_t,
    times,
    page0,
    first_a,
    first_b,
    page_q,
    priv_a,
    priv_b,
    page_out,
    wide,
    greet_sem,
    local_sem,
    x_send,
    x_recv,
    m_sem,
    q_sem,
    s_sem,
    w_sem,
    c_sem,
    r_sem,
    h_send,
    h_recv,
):
    n_tok, n_head, count, features = sizes
    slots = n_tok * CAP
    blocks = slots // LANES
    pages = pool.shape[0]
    ny = n_head // 2
    nx = 4
    nz = n_tok // nx
    me_t = lax.axis_index("tok")
    me_h = lax.axis_index("head")
    y, core = me_h // 2, me_h % 2
    z_at, x_at = me_t // nx, me_t % nx
    up, down, far = (y + 1) % ny, (y + ny - 1) % ny, (y + 2) % ny
    sib = y * 2 + 1 - core
    h_up, h_down, h_far = up * 2 + core, down * 2 + core, far * 2 + core
    a_up, a_down, a_far = up * 2 + 1 - core, down * 2 + 1 - core, far * 2 + 1 - core

    offsets = [(dz, dx) for dz in range(nz) for dx in range(nx) if dz + dx > 0]
    offsets.sort(key=lambda o: -(min(o[0], nz - o[0]) + min(o[1], nx - o[1])))
    peers = [((z_at + dz) % nz) * nx + (x_at + dx) % nx for dz, dx in offsets]

    barrier = pltpu.get_barrier_semaphore()
    x_near = [z_at * nx + (x_at + d) % nx for d in (1, nx - 1)]
    z_near = [(z_at + d) % nz * nx + x_at for d in (1, nz - 1)]
    for peer in (sib, h_up, h_down):
        pl.semaphore_signal(barrier, inc=1, device_id=(me_t, peer), device_id_type=MESH)
    for peer in x_near + z_near:
        pl.semaphore_signal(barrier, inc=1, device_id=(peer, me_h), device_id_type=MESH)

    def greet(step):
        if step > 0:
            pl.semaphore_wait(greet_sem.at[step - 1], 2)
        if step < 3:
            for peer in (x_near, z_near, z_near)[step]:
                pl.semaphore_signal(
                    greet_sem.at[step], inc=1, device_id=(peer, me_h), device_id_type=MESH
                )

    sent = []

    def remote(source, target, send_sem, recv_sem, device):
        copy = pltpu.make_async_remote_copy(
            src_ref=source,
            dst_ref=target,
            send_sem=send_sem,
            recv_sem=recv_sem,
            device_id=device,
            device_id_type=MESH,
        )
        copy.start()
        return copy

    def bulk(source, target, blocks_of, send_sem, recv_sem):
        some = pl.ds(0, blocks_of)
        copy = pltpu.make_async_remote_copy(
            src_ref=source.at[some],
            dst_ref=target.at[some],
            send_sem=send_sem,
            recv_sem=recv_sem,
            device_id=(me_t, sib),
            device_id_type=MESH,
        )
        sent.append(copy)
        return copy

    def exchange(source, target, sems):
        for p in peers:
            remote(source.at[p], target.at[me_t], sems.at[0], sems.at[1], (p, me_h))
        target[me_t] = source[me_t]
        return bulk(source, target, len(peers), sems.at[0], sems.at[1])

    def exchange_rows(make, source, target, sems):
        for dz in sorted(range(nz), key=lambda d: -min(d, nz - d)):
            zz = (z_at + dz) % nz
            rows = pl.ds(pl.multiple_of(zz * nx * CAP, nx * CAP), nx * CAP)
            source[pl.ds(zz * nx, nx)] = make(rows).astype(BF16).reshape((nx,) + source.shape[1:])
            for dx in sorted(range(nx), key=lambda d: -min(d, nx - d)):
                if dz + dx > 0:
                    p = zz * nx + (x_at + dx) % nx
                    remote(source.at[p], target.at[me_t], sems.at[0], sems.at[1], (p, me_h))
        target[me_t] = source[me_t]
        return bulk(source, target, len(peers), sems.at[0], sems.at[1])

    local_x = pltpu.make_async_copy(tokens, x.at[me_h], local_sem.at[0])
    local_x.start()
    load_win = pltpu.make_async_copy(w_in, win_v, local_sem.at[1])
    load_win.start()

    small = [
        pltpu.make_async_copy(source, target, local_sem.at[4 + k])
        for k, (source, target) in enumerate(
            (
                (owner_h, owner),
                (table_h, table),
                (length_h, length),
                (gain_h, gain),
                (lq1_h, lq1),
                (lk1_h, lk1),
                (lq2_h, lq2),
                (lk2_h, lk2),
            )
        )
    ]
    for load in small:
        load.start()
    pl.semaphore_wait(barrier, 3 + len(x_near) + len(z_near))

    quarter = count // 4

    def gather_start(buffer, mine, send_sem, recv_sem):
        def go(index, source, start, quarters, target):
            rows = pl.ds(start * quarter, quarters * quarter)
            part = buffer.at[source, rows]
            origin = mine.at[rows] if source is me_h else part
            return remote(origin, part, send_sem.at[0], recv_sem.at[index], (me_t, target))

        copies = [
            go(0, me_h, 0, 1, h_up),
            go(1, me_h, 3, 1, h_down),
            go(2, me_h, 1, 1, h_up),
            go(3, me_h, 2, 1, h_down),
            go(4, me_h, 2, 2, h_up),
            go(5, me_h, 0, 2, h_down),
            go(6, me_h, 0, 4, sib),
        ]
        bulk(buffer, buffer, n_head - 1, send_sem.at[0], recv_sem.at[0])
        return go, copies

    def gather_rest(started, add, beside):
        go, copies = started
        for k, (source, start, target) in enumerate(
            ((h_down, 0, h_up), (h_up, 3, h_down), (h_down, 1, h_up), (h_up, 2, h_down))
        ):
            copies[k].wait_recv()
            copies.append(go(7 + k, source, start, 1, target))
        copies.append(go(11, h_down, 0, 2, sib))
        copies.append(go(12, h_up, 2, 2, sib))
        beside(1)
        add(me_h)
        copies[6].wait_recv()
        add(sib)
        copies[4].wait_recv()
        copies.append(go(13, h_down, 2, 2, sib))
        add(h_down)
        copies[5].wait_recv()
        copies.append(go(14, h_up, 0, 2, sib))
        add(h_up)
        beside(2)
        copies[11].wait_recv()
        copies[13].wait_recv()
        add(a_down)
        copies[12].wait_recv()
        copies[14].wait_recv()
        add(a_up)
        for k, start in enumerate((0, 3, 1, 2)):
            copies[7 + k].wait_recv()
            copies.append(go(15 + k, h_far, start, 1, sib))
        beside(3)
        add(h_far)
        for k in range(4):
            copies[15 + k].wait_recv()
        add(a_far)

    def tiles(rows, height, target):
        groups = jnp.concatenate(
            [rows[:, g * LANES : (g + 1) * LANES] for g in range(blocks)], axis=0
        ).astype(BF16)
        for b in range(PER):
            moved = dot(groups, turn[b]).astype(BF16)
            for g in range(blocks):
                target[g * PER + b] = moved[g * height : (g + 1) * height]

    def gather_tiles(source, g):
        total = source[g * PER].astype(F32)
        for b in range(1, PER):
            total = total + source[g * PER + b].astype(F32)
        return total

    started = gather_start(x, tokens, x_send, x_recv)
    greet(0)

    def prepare():
        for load in small:
            load.wait()
        own = owner[...]
        named = own == iota((n_tok, count), 0)
        earlier = one_hot(iota((count, count), 0) < iota((count, count), 1))
        before = dot(one_hot(named), earlier)
        rank = jnp.sum(jnp.where(named, before, 0.0), axis=0, keepdims=True)
        slot = own * CAP + rank.astype(jnp.int32)
        eye = iota((count, count), 0) == iota((count, count), 1)
        slot_c = jnp.sum(jnp.where(eye, slot, 0), axis=1, keepdims=True)
        place[...] = one_hot(iota((slots, count), 0) == slot)
        place_t[...] = one_hot(iota((count, slots), 1) == slot_c)
        shift = (me_t % PER) * CAP
        for b in range(PER):
            source_lane = iota((LANES, LANES), 0)
            moved = source_lane - b * CAP + shift == iota((LANES, LANES), 1)
            turn[b] = one_hot(moved & (source_lane // CAP == b))

        lengths = length[...]
        ends = stack_rows([(lengths // 8).astype(F32), (lengths % 8).astype(F32)], 8)
        fields = jnp.concatenate([table[...].astype(F32), ends], axis=0).astype(BF16)
        tiles(dot(fields, place_t[...]), FIELDS, send_m)

    def add_query(source):
        rows = pl.ds(pl.multiple_of(source * features, features), features)
        proj[...] = proj[...] + dot(x[source], win_v[rows, 0 : 2 * QK])

    proj[...] = jnp.zeros(proj.shape, F32)
    load_pool = pltpu.make_async_copy(pool, pool_v, local_sem.at[2])
    arriving = []

    def beside_gather(step):
        greet(step)
        if step == 1:
            prepare()
            local_x.wait()
            load_win.wait()
            load_pool.start()
        elif step == 3:
            arriving.append(exchange(send_m, recv_m, m_sem))

    gather_rest(started, add_query, beside_gather)

    query = proj[...].astype(BF16)
    query_in = exchange_rows(lambda rows: dot(place[rows], query), send_q, recv_q, q_sem)

    fresh = jnp.zeros((count, 2 * QK + VDIM), F32)
    for h in range(n_head):
        fresh = fresh + dot(x[h], win_v[h * features : (h + 1) * features, 2 * QK :])
    fresh = fresh.astype(BF16)
    v_new[...] = fresh[:, 2 * QK :]
    product = query.astype(F32) * fresh[:, 0 : 2 * QK].astype(F32)
    high, low = split(product, 2)
    ones = jnp.ones((8, QK), F32).astype(BF16)
    terms = []
    for m in range(2):
        part = slice(m * QK, (m + 1) * QK)
        total = dot_nt(ones, high[:, part].astype(BF16)) + dot_nt(ones, low[:, part].astype(BF16))
        terms += split(total[0:1] * SCALE, 3)
    tiles(dot(stack_rows(terms, TILE).astype(BF16), place_t[...]), TILE, send_s)
    self_in = exchange(send_s, recv_s, s_sem)

    def columns(h):
        return w_out.at[:, pl.ds(pl.multiple_of(h * features, features), features)]

    own_w = pltpu.make_async_copy(columns(me_h), wcol_v.at[me_h], local_sem.at[3])
    own_w.start()
    for h in (h_up, h_down, h_far, a_up, a_down, a_far, sib):
        remote(columns(h), wcol_v.at[me_h], w_sem.at[0], w_sem.at[1], (me_t, h))
    weights_in = bulk(wcol_v, wcol_v, n_head - 1, w_sem.at[0], w_sem.at[1])
    lam = (
        jnp.exp(jnp.sum(lq1[...] * lk1[...], axis=1, keepdims=True))
        - jnp.exp(jnp.sum(lq2[...] * lk2[...], axis=1, keepdims=True))
        + lambda_init
    )

    arriving[0].wait_recv()
    whole = jnp.zeros((pages, LANES), F32)
    rest = jnp.zeros((pages, LANES), F32)
    page = iota((pages, LANES), 0).astype(F32)
    for g in range(blocks):
        cut = slice(g * LANES, (g + 1) * LANES)
        got = gather_tiles(recv_m, g)
        cached = got[8:9] * 8.0 + got[9:10]
        info[0:1, cut] = got[0:1]
        info[1:2, cut] = cached
        hit_any = jnp.zeros((pages, LANES), F32)
        for j in range(1, MAXP):
            left = cached - float(PAGE * j)
            number = jnp.where(left > 0.0, got[j : j + 1], -1.0)
            hit = number == page
            hit_any = jnp.where(hit, 1.0, hit_any)
            whole = whole + jnp.where(hit, jnp.where(left >= float(PAGE), 1.0, 0.0), 0.0)
            rest = rest + jnp.where(hit, jnp.where(left >= float(PAGE), 0.0, left), 0.0)
        match[:, cut] = hit_any.astype(BF16)
        match_t[cut] = jnp.transpose(jnp.concatenate([hit_any, hit_any], axis=0)).astype(BF16)
        chosen = jnp.transpose(jnp.broadcast_to(got[0:1], (LANES, LANES)))
        for p in range(SHARED):
            page0[p, cut] = one_hot(chosen == float(p))
    whole = jnp.sum(whole, axis=1, keepdims=True)
    rest = jnp.sum(rest, axis=1, keepdims=True)
    position = iota((pages, PAGE), 1).astype(F32)
    times[...] = whole + jnp.where(position < rest, 1.0, 0.0)
    load_pool.wait()
    query_in.wait_recv()

    queries = recv_q[...].reshape(slots, 2 * QK)
    found = dot(match[...], queries)
    side = iota((GROUP, 2 * QK), 1) < QK
    for g in range(pages // GROUP):
        mine = found[g * GROUP : (g + 1) * GROUP]
        both = [jnp.where(side, mine, 0.0), jnp.where(side, 0.0, mine)]
        page_q[2 * g * GROUP : 2 * (g + 1) * GROUP] = jnp.concatenate(both, axis=0).astype(BF16)
    half = slots // 2
    for h in range(2):
        cut = slice(h * half, (h + 1) * half)
        at = info[0:1, cut]
        for ref, lo in ((first_a, 0), (first_b, QK)):
            kept = None
            for p in range(0, SHARED, 2):
                keys = pool_v[p : p + 2].reshape(2 * PAGE, WIDE)[:, lo : lo + QK]
                score = dot_nt(keys, queries[cut, lo : lo + QK])
                chosen = jnp.where(at == float(p), score[0:PAGE], score[PAGE:])
                kept = chosen if p == 0 else jnp.where(at >= float(p), chosen, kept)
            ref[:, cut] = kept

    row = iota((2 * GROUP, LANES), 0) % GROUP
    for g in range(pages // GROUP):
        mine = slice(g * GROUP, (g + 1) * GROUP)
        keys = pool_v[mine].reshape(GROUP * PAGE, WIDE)[:, 0 : 2 * QK]
        score = dot_nt(page_q[2 * g * GROUP : 2 * (g + 1) * GROUP], keys)
        chosen = score[:, 0:PAGE]
        for i in range(1, GROUP):
            chosen = jnp.where(row == i, score[:, i * PAGE : (i + 1) * PAGE], chosen)
        priv_a[mine] = chosen[0:GROUP]
        priv_b[mine] = chosen[GROUP:]

    self_in.wait_recv()
    page_best = []
    for ref in (priv_a, priv_b):
        score = jnp.where(times[...] > 0.0, ref[...] * SCALE, NEG)
        ref[...] = score
        page_best.append(jnp.max(score, axis=1, keepdims=True))
    tops, selfs = [], []
    page_top = [jnp.zeros((pages, LANES), F32) for _ in range(2)]
    depth = iota((PAGE, LANES), 0).astype(F32)
    for g in range(blocks):
        cut = slice(g * LANES, (g + 1) * LANES)
        hit = match[:, cut].astype(F32) > 0.0
        got = gather_tiles(recv_s, g)
        valid = depth < info[1:2, cut]
        for m, ref in enumerate((first_a, first_b)):
            score = jnp.where(valid, ref[:, cut] * SCALE, NEG)
            ref[:, cut] = score
            mine = got[3 * m : 3 * m + 1] + got[3 * m + 1 : 3 * m + 2] + got[3 * m + 2 : 3 * m + 3]
            best = jnp.max(jnp.where(hit, page_best[m], NEG), axis=0, keepdims=True)
            top = jnp.maximum(jnp.maximum(jnp.max(score, axis=0, keepdims=True), best), mine)
            page_top[m] = page_top[m] + jnp.where(hit, top, 0.0)
            tops.append(top)
            selfs.append(mine)

    page_sum = []
    for m, ref in enumerate((priv_a, priv_b)):
        top = jnp.sum(page_top[m], axis=1, keepdims=True)
        weight = jnp.where(times[...] > 0.0, jnp.exp2(ref[...] - top) * times[...], 0.0)
        ref[...] = weight
        page_sum.append(jnp.sum(weight, axis=1, keepdims=True))
    page_coef = [jnp.zeros((pages, LANES), F32) for _ in range(2)]
    own_rows = []
    for g in range(blocks):
        cut = slice(g * LANES, (g + 1) * LANES)
        hit = match[:, cut].astype(F32) > 0.0
        mixed, own_coef = None, None
        for m, ref in enumerate((first_a, first_b)):
            top = tops[2 * g + m]
            weight = jnp.exp2(ref[:, cut] - top)
            new = jnp.exp2(selfs[2 * g + m] - top)
            total = (
                new
                + jnp.sum(weight, axis=0, keepdims=True)
                + jnp.sum(jnp.where(hit, page_sum[m], 0.0), axis=0, keepdims=True)
            )
            coef = 1.0 / total if m == 0 else -lam / total
            page_coef[m] = page_coef[m] + jnp.where(hit, coef, 0.0)
            mixed = weight * coef if m == 0 else mixed + weight * coef
            own_coef = new * coef if m == 0 else own_coef + new * coef
        mixed = jnp.transpose(mixed).astype(BF16)
        for p in range(SHARED):
            wide[cut, p * PAGE : (p + 1) * PAGE] = mixed * page0[p, cut]
        own_rows.append(stack_rows(split(own_coef, 2), TILE))
    tiles(jnp.concatenate(own_rows, axis=1), TILE, send_c)
    coef_in = exchange(send_c, recv_c, c_sem)

    priv_a[...] = priv_a[...] * jnp.sum(page_coef[0], axis=1, keepdims=True) + priv_b[
        ...
    ] * jnp.sum(page_coef[1], axis=1, keepdims=True)

    row = iota((GROUP, LANES), 0)
    for g in range(pages // GROUP):
        mine = slice(g * GROUP, (g + 1) * GROUP)
        values = pool_v[mine].reshape(GROUP * PAGE, WIDE)[:, 2 * QK :]
        weight = priv_a[mine]
        spread = jnp.concatenate(
            [jnp.where(row == i, weight, 0.0) for i in range(GROUP)], axis=1
        ).astype(BF16)
        page_out[mine] = dot(spread, values)
    high, low = split(page_out[...], 2)
    pair = jnp.concatenate([high, low], axis=0).astype(BF16)
    values = pool_v[0:SHARED].reshape(SHARED * PAGE, WIDE)[:, 2 * QK :]

    mixed_in = exchange_rows(
        lambda rows: dot(wide[rows], values) + dot(match_t[rows], pair), send_r, recv_r, r_sem
    )
    own_w.wait()
    coef_in.wait_recv()
    rows = jnp.concatenate([gather_tiles(recv_c, g) for g in range(blocks)], axis=1)
    coefs = dot_nt(place_t[...], rows.astype(BF16))
    addend = (coefs[:, 0:1] + coefs[:, 1:2]) * v_new[...].astype(F32)
    mixed_in.wait_recv()
    mixed = dot(place_t[...], recv_r[...].reshape(slots, VDIM)) + addend
    scale = lax.rsqrt(jnp.mean(mixed * mixed, axis=1, keepdims=True) + norm_eps)
    heads[me_h] = (mixed * scale * gain[...] * (1.0 - lambda_init)).astype(BF16)

    started = gather_start(heads, heads.at[me_h], h_send, h_recv)
    weights_in.wait_recv()
    proj[...] = jnp.zeros(proj.shape, F32)

    def add_out(source):
        proj[...] = proj[...] + dot(heads[source], wcol_v[source])

    gather_rest(started, add_out, lambda step: None)
    out[...] = proj[...].astype(BF16)
    for copy in sent:
        copy.wait_send()


def on_device(sizes, tokens, w_in, w_out, gain, lq1, lk1, lq2, lk2, pool, table, length, owner):
    n_tok, n_head, count, features = sizes
    slots = n_tok * CAP
    pages = pool.shape[0]
    vmem = pl.BlockSpec(memory_space=pltpu.VMEM)
    hbm = pl.BlockSpec(memory_space=pltpu.HBM)
    dma = pltpu.SemaphoreType.DMA
    return pl.pallas_call(
        functools.partial(step_kernel, sizes),
        out_shape=pltpu.VMEM((count, features), BF16),
        in_specs=[hbm] * 12,
        out_specs=vmem,
        scratch_shapes=[
            pltpu.VMEM((1, VDIM), F32),
            pltpu.VMEM((1, QK), F32),
            pltpu.VMEM((1, QK), F32),
            pltpu.VMEM((1, QK), F32),
            pltpu.VMEM((1, QK), F32),
            pltpu.VMEM((MAXP, count), jnp.int32),
            pltpu.VMEM((1, count), jnp.int32),
            pltpu.VMEM((1, count), jnp.int32),
            pltpu.VMEM((n_head, count, features), BF16),
            pltpu.VMEM(w_in.shape, BF16),
            pltpu.VMEM((n_head, VDIM, features), BF16),
            pltpu.VMEM((pages, PAGE, WIDE), BF16),
            pltpu.VMEM((n_head, count, VDIM), BF16),
            pltpu.VMEM((slots, count), BF16),
            pltpu.VMEM((count, slots), BF16),
            pltpu.VMEM((PER, LANES, LANES), BF16),
            pltpu.VMEM((count, 2 * QK), F32),
            pltpu.VMEM((count, VDIM), BF16),
            pltpu.VMEM((n_tok, FIELDS, LANES), BF16),
            pltpu.VMEM((n_tok, FIELDS, LANES), BF16),
            pltpu.VMEM((n_tok, CAP, 2 * QK), BF16),
            pltpu.VMEM((n_tok, CAP, 2 * QK), BF16),
            pltpu.VMEM((n_tok, TILE, LANES), BF16),
            pltpu.VMEM((n_tok, TILE, LANES), BF16),
            pltpu.VMEM((n_tok, CAP, VDIM), BF16),
            pltpu.VMEM((n_tok, CAP, VDIM), BF16),
            pltpu.VMEM((n_tok, TILE, LANES), BF16),
            pltpu.VMEM((n_tok, TILE, LANES), BF16),
            pltpu.VMEM((8, slots), F32),
            pltpu.VMEM((pages, slots), BF16),
            pltpu.VMEM((slots, 2 * pages), BF16),
            pltpu.VMEM((pages, PAGE), F32),
            pltpu.VMEM((SHARED, slots, PAGE), BF16),
            pltpu.VMEM((PAGE, slots), F32),
            pltpu.VMEM((PAGE, slots), F32),
            pltpu.VMEM((2 * pages, 2 * QK), BF16),
            pltpu.VMEM((pages, PAGE), F32),
            pltpu.VMEM((pages, PAGE), F32),
            pltpu.VMEM((pages, VDIM), F32),
            pltpu.VMEM((slots, SHARED * PAGE), BF16),
            pltpu.SemaphoreType.REGULAR((3,)),
            dma((12,)),
        ]
        + [dma((number,)) for number in (1, 19, 2, 2, 2, 2, 2, 2, 1, 19)],
        compiler_params=pltpu.CompilerParams(
            collective_id=0, has_side_effects=True, vmem_limit_bytes=60 * 1024 * 1024
        ),
        name="decode_step",
    )(
        tokens,
        w_in,
        w_out,
        pool.reshape(pages, PAGE, WIDE),
        gain.reshape(1, VDIM),
        lq1.reshape(1, QK),
        lk1.reshape(1, QK),
        lq2.reshape(1, QK),
        lk2.reshape(1, QK),
        jnp.transpose(table),
        length.reshape(1, count),
        owner.reshape(1, count),
    )


def solution(mesh):
    n_tok, n_head = mesh.shape["tok"], mesh.shape["head"]

    def run(
        tokens,
        input_weight,
        output_weight,
        head_gain,
        query_lambda_one,
        key_lambda_one,
        query_lambda_two,
        key_lambda_two,
        cache_pool,
        page_table,
        cache_length,
        cache_owner,
    ):
        sizes = (n_tok, n_head, tokens.shape[0] // n_tok, tokens.shape[1] // n_head)
        placed = (
            P("tok", "head"),
            P(None, "head"),
            P("head", None),
            P("head"),
            P(),
            P(),
            P(),
            P(),
            P("tok", "head", None, None),
            P("tok", None),
            P("tok"),
            P("tok", None),
        )
        return jax.shard_map(
            functools.partial(on_device, sizes),
            mesh=mesh,
            in_specs=placed,
            out_specs=P("tok", "head"),
            check_vma=False,
        )(
            tokens,
            input_weight,
            output_weight,
            head_gain,
            query_lambda_one,
            key_lambda_one,
            query_lambda_two,
            key_lambda_two,
            cache_pool,
            page_table,
            cache_length,
            cache_owner,
        )

    return run
```

```python
import functools
import math

import jax
import jax.numpy as jnp
from jax import lax
from jax.experimental import pallas as pl
from jax.experimental.pallas import tpu as pltpu
from jax.sharding import PartitionSpec as P

QK = 128
VDIM = 256
PAGE = 128
CAP = 32
SHARED = 8
MAXP = 8
GROUP = 8
LANES = 128
FIELDS = 16
TILE = 8
PER = LANES // CAP
WIDE = 2 * QK + VDIM

lambda_init = 0.8
norm_eps = 1e-05
NEG = -1e30
SCALE = math.log2(math.e) / math.sqrt(QK)
MESH = pl.DeviceIdType.MESH
F32 = jnp.float32
BF16 = jnp.bfloat16


def iota(shape, dim):
    return lax.broadcasted_iota(jnp.int32, shape, dim)


def one_hot(condition):
    return condition.astype(F32).astype(BF16)


def dot(a, b):
    return jnp.dot(a, b, preferred_element_type=F32)


def dot_nt(a, b):
    return lax.dot_general(a, b, (((1,), (1,)), ((), ())), preferred_element_type=F32)


def split(value, terms):
    parts = []
    for _ in range(terms - 1):
        high = value.astype(BF16).astype(F32)
        parts.append(high)
        value = value - high
    return parts + [value]


def stack_rows(rows, height):
    row = iota((height, rows[0].shape[1]), 0)
    stacked = jnp.where(row == 0, rows[0], 0.0)
    for index in range(1, len(rows)):
        stacked = jnp.where(row == index, rows[index], stacked)
    return stacked


def step_kernel(
    sizes,
    tokens,
    w_in,
    w_out,
    pool,
    gain_h,
    lq1_h,
    lk1_h,
    lq2_h,
    lk2_h,
    table_h,
    length_h,
    owner_h,
    out,
    gain,
    lq1,
    lk1,
    lq2,
    lk2,
    table,
    length,
    owner,
    x,
    win_v,
    wcol_v,
    pool_v,
    heads,
    place,
    place_t,
    turn,
    proj,
    v_new,
    send_m,
    recv_m,
    send_q,
    recv_q,
    send_s,
    recv_s,
    send_r,
    recv_r,
    send_c,
    recv_c,
    info,
    match,
    match_t,
    times,
    page0,
    first_a,
    first_b,
    page_q,
    priv_a,
    priv_b,
    page_out,
    wide,
    greet_sem,
    local_sem,
    x_send,
    x_recv,
    m_sem,
    q_sem,
    s_sem,
    w_sem,
    c_sem,
    r_sem,
    h_send,
    h_recv,
):
    n_tok, n_head, count, features = sizes
    slots = n_tok * CAP
    blocks = slots // LANES
    pages = pool.shape[0]
    ny = n_head // 2
    nx = 4
    nz = n_tok // nx
    me_t = lax.axis_index("tok")
    me_h = lax.axis_index("head")
    y, core = me_h // 2, me_h % 2
    z_at, x_at = me_t // nx, me_t % nx
    up, down, far = (y + 1) % ny, (y + ny - 1) % ny, (y + 2) % ny
    sib = y * 2 + 1 - core
    h_up, h_down, h_far = up * 2 + core, down * 2 + core, far * 2 + core
    a_up, a_down, a_far = up * 2 + 1 - core, down * 2 + 1 - core, far * 2 + 1 - core

    offsets = [(dz, dx) for dz in range(nz) for dx in range(nx) if dz + dx > 0]
    offsets.sort(key=lambda o: -(min(o[0], nz - o[0]) + min(o[1], nx - o[1])))
    peers = [((z_at + dz) % nz) * nx + (x_at + dx) % nx for dz, dx in offsets]

    barrier = pltpu.get_barrier_semaphore()
    x_near = [z_at * nx + (x_at + d) % nx for d in (1, nx - 1)]
    z_near = [(z_at + d) % nz * nx + x_at for d in (1, nz - 1)]
    for peer in (sib, h_up, h_down):
        pl.semaphore_signal(barrier, inc=1, device_id=(me_t, peer), device_id_type=MESH)
    for peer in x_near + z_near:
        pl.semaphore_signal(barrier, inc=1, device_id=(peer, me_h), device_id_type=MESH)

    def greet(step):
        if step > 0:
            pl.semaphore_wait(greet_sem.at[step - 1], 2)
        if step < 3:
            for peer in (x_near, z_near, z_near)[step]:
                pl.semaphore_signal(
                    greet_sem.at[step], inc=1, device_id=(peer, me_h), device_id_type=MESH
                )

    sent = []

    def remote(source, target, send_sem, recv_sem, device):
        copy = pltpu.make_async_remote_copy(
            src_ref=source,
            dst_ref=target,
            send_sem=send_sem,
            recv_sem=recv_sem,
            device_id=device,
            device_id_type=MESH,
        )
        copy.start()
        return copy

    def bulk(source, target, blocks_of, send_sem, recv_sem):
        some = pl.ds(0, blocks_of)
        copy = pltpu.make_async_remote_copy(
            src_ref=source.at[some],
            dst_ref=target.at[some],
            send_sem=send_sem,
            recv_sem=recv_sem,
            device_id=(me_t, sib),
            device_id_type=MESH,
        )
        sent.append(copy)
        return copy

    def exchange(source, target, sems):
        for p in peers:
            remote(source.at[p], target.at[me_t], sems.at[0], sems.at[1], (p, me_h))
        target[me_t] = source[me_t]
        return bulk(source, target, len(peers), sems.at[0], sems.at[1])

    def exchange_rows(make, source, target, sems):
        for dz in sorted(range(nz), key=lambda d: -min(d, nz - d)):
            zz = (z_at + dz) % nz
            rows = pl.ds(pl.multiple_of(zz * nx * CAP, nx * CAP), nx * CAP)
            source[pl.ds(zz * nx, nx)] = make(rows).astype(BF16).reshape((nx,) + source.shape[1:])
            for dx in sorted(range(nx), key=lambda d: -min(d, nx - d)):
                if dz + dx > 0:
                    p = zz * nx + (x_at + dx) % nx
                    remote(source.at[p], target.at[me_t], sems.at[0], sems.at[1], (p, me_h))
        target[me_t] = source[me_t]
        return bulk(source, target, len(peers), sems.at[0], sems.at[1])

    pl.semaphore_wait(barrier, 3 + len(x_near) + len(z_near))

    quarter = count // 4

    def gather_start(buffer, mine, send_sem, recv_sem):
        def go(index, source, start, quarters, target):
            rows = pl.ds(start * quarter, quarters * quarter)
            part = buffer.at[source, rows]
            origin = mine.at[rows] if source is me_h else part
            return remote(origin, part, send_sem.at[0], recv_sem.at[index], (me_t, target))

        copies = [
            go(0, me_h, 0, 1, h_up),
            go(1, me_h, 3, 1, h_down),
            go(2, me_h, 1, 1, h_up),
            go(3, me_h, 2, 1, h_down),
            go(4, me_h, 2, 2, h_up),
            go(5, me_h, 0, 2, h_down),
            go(6, me_h, 0, 4, sib),
        ]
        bulk(buffer, buffer, n_head - 1, send_sem.at[0], recv_sem.at[0])
        return go, copies

    def gather_rest(started, add, beside):
        go, copies = started
        for k, (source, start, target) in enumerate(
            ((h_down, 0, h_up), (h_up, 3, h_down), (h_down, 1, h_up), (h_up, 2, h_down))
        ):
            copies[k].wait_recv()
            copies.append(go(7 + k, source, start, 1, target))
        copies.append(go(11, h_down, 0, 2, sib))
        copies.append(go(12, h_up, 2, 2, sib))
        beside(1)
        add(me_h)
        copies[6].wait_recv()
        add(sib)
        copies[4].wait_recv()
        copies.append(go(13, h_down, 2, 2, sib))
        add(h_down)
        copies[5].wait_recv()
        copies.append(go(14, h_up, 0, 2, sib))
        add(h_up)
        beside(2)
        copies[11].wait_recv()
        copies[13].wait_recv()
        add(a_down)
        copies[12].wait_recv()
        copies[14].wait_recv()
        add(a_up)
        for k, start in enumerate((0, 3, 1, 2)):
            copies[7 + k].wait_recv()
            copies.append(go(15 + k, h_far, start, 1, sib))
        beside(3)
        add(h_far)
        for k in range(4):
            copies[15 + k].wait_recv()
        add(a_far)

    def tiles(rows, height, target):
        groups = jnp.concatenate(
            [rows[:, g * LANES : (g + 1) * LANES] for g in range(blocks)], axis=0
        ).astype(BF16)
        for b in range(PER):
            moved = dot(groups, turn[b]).astype(BF16)
            for g in range(blocks):
                target[g * PER + b] = moved[g * height : (g + 1) * height]

    def gather_tiles(source, g):
        total = source[g * PER].astype(F32)
        for b in range(1, PER):
            total = total + source[g * PER + b].astype(F32)
        return total

    started = gather_start(x, tokens, x_send, x_recv)
    greet(0)
    local_x = pltpu.make_async_copy(tokens, x.at[me_h], local_sem.at[0])
    local_x.start()
    load_win = pltpu.make_async_copy(w_in, win_v, local_sem.at[1])
    load_win.start()

    small = [
        pltpu.make_async_copy(source, target, local_sem.at[4 + k])
        for k, (source, target) in enumerate(
            (
                (owner_h, owner),
                (table_h, table),
                (length_h, length),
                (gain_h, gain),
                (lq1_h, lq1),
                (lk1_h, lk1),
                (lq2_h, lq2),
                (lk2_h, lk2),
            )
        )
    ]
    for load in small:
        load.start()

    def prepare():
        for load in small:
            load.wait()
        own = owner[...]
        named = own == iota((n_tok, count), 0)
        earlier = one_hot(iota((count, count), 0) < iota((count, count), 1))
        before = dot(one_hot(named), earlier)
        rank = jnp.sum(jnp.where(named, before, 0.0), axis=0, keepdims=True)
        slot = own * CAP + rank.astype(jnp.int32)
        eye = iota((count, count), 0) == iota((count, count), 1)
        slot_c = jnp.sum(jnp.where(eye, slot, 0), axis=1, keepdims=True)
        place[...] = one_hot(iota((slots, count), 0) == slot)
        place_t[...] = one_hot(iota((count, slots), 1) == slot_c)
        shift = (me_t % PER) * CAP
        for b in range(PER):
            source_lane = iota((LANES, LANES), 0)
            moved = source_lane - b * CAP + shift == iota((LANES, LANES), 1)
            turn[b] = one_hot(moved & (source_lane // CAP == b))

        lengths = length[...]
        ends = stack_rows([(lengths // 8).astype(F32), (lengths % 8).astype(F32)], 8)
        fields = jnp.concatenate([table[...].astype(F32), ends], axis=0).astype(BF16)
        tiles(dot(fields, place_t[...]), FIELDS, send_m)

    def add_query(source):
        rows = pl.ds(pl.multiple_of(source * features, features), features)
        proj[...] = proj[...] + dot(x[source], win_v[rows, 0 : 2 * QK])

    proj[...] = jnp.zeros(proj.shape, F32)
    load_pool = pltpu.make_async_copy(pool, pool_v, local_sem.at[2])
    arriving = []

    def beside_gather(step):
        greet(step)
        if step == 1:
            prepare()
            local_x.wait()
            load_win.wait()
            load_pool.start()
        elif step == 3:
            arriving.append(exchange(send_m, recv_m, m_sem))

    gather_rest(started, add_query, beside_gather)

    query = proj[...].astype(BF16)
    query_in = exchange_rows(lambda rows: dot(place[rows], query), send_q, recv_q, q_sem)

    fresh = jnp.zeros((count, 2 * QK + VDIM), F32)
    for h in range(n_head):
        fresh = fresh + dot(x[h], win_v[h * features : (h + 1) * features, 2 * QK :])
    fresh = fresh.astype(BF16)
    v_new[...] = fresh[:, 2 * QK :]
    product = query.astype(F32) * fresh[:, 0 : 2 * QK].astype(F32)
    high, low = split(product, 2)
    ones = jnp.ones((8, QK), F32).astype(BF16)
    terms = []
    for m in range(2):
        part = slice(m * QK, (m + 1) * QK)
        total = dot_nt(ones, high[:, part].astype(BF16)) + dot_nt(ones, low[:, part].astype(BF16))
        terms += split(total[0:1] * SCALE, 3)
    tiles(dot(stack_rows(terms, TILE).astype(BF16), place_t[...]), TILE, send_s)
    self_in = exchange(send_s, recv_s, s_sem)

    def columns(h):
        return w_out.at[:, pl.ds(pl.multiple_of(h * features, features), features)]

    own_w = pltpu.make_async_copy(columns(me_h), wcol_v.at[me_h], local_sem.at[3])
    own_w.start()
    for h in (h_up, h_down, h_far, a_up, a_down, a_far, sib):
        remote(columns(h), wcol_v.at[me_h], w_sem.at[0], w_sem.at[1], (me_t, h))
    weights_in = bulk(wcol_v, wcol_v, n_head - 1, w_sem.at[0], w_sem.at[1])
    lam = (
        jnp.exp(jnp.sum(lq1[...] * lk1[...], axis=1, keepdims=True))
        - jnp.exp(jnp.sum(lq2[...] * lk2[...], axis=1, keepdims=True))
        + lambda_init
    )

    arriving[0].wait_recv()
    whole = jnp.zeros((pages, LANES), F32)
    rest = jnp.zeros((pages, LANES), F32)
    page = iota((pages, LANES), 0).astype(F32)
    for g in range(blocks):
        cut = slice(g * LANES, (g + 1) * LANES)
        got = gather_tiles(recv_m, g)
        cached = got[8:9] * 8.0 + got[9:10]
        info[0:1, cut] = got[0:1]
        info[1:2, cut] = cached
        hit_any = jnp.zeros((pages, LANES), F32)
        for j in range(1, MAXP):
            left = cached - float(PAGE * j)
            number = jnp.where(left > 0.0, got[j : j + 1], -1.0)
            hit = number == page
            hit_any = jnp.where(hit, 1.0, hit_any)
            whole = whole + jnp.where(hit, jnp.where(left >= float(PAGE), 1.0, 0.0), 0.0)
            rest = rest + jnp.where(hit, jnp.where(left >= float(PAGE), 0.0, left), 0.0)
        match[:, cut] = hit_any.astype(BF16)
        match_t[cut] = jnp.transpose(jnp.concatenate([hit_any, hit_any], axis=0)).astype(BF16)
        chosen = jnp.transpose(jnp.broadcast_to(got[0:1], (LANES, LANES)))
        for p in range(SHARED):
            page0[p, cut] = one_hot(chosen == float(p))
    whole = jnp.sum(whole, axis=1, keepdims=True)
    rest = jnp.sum(rest, axis=1, keepdims=True)
    position = iota((pages, PAGE), 1).astype(F32)
    times[...] = whole + jnp.where(position < rest, 1.0, 0.0)
    load_pool.wait()
    query_in.wait_recv()

    queries = recv_q[...].reshape(slots, 2 * QK)
    found = dot(match[...], queries)
    side = iota((GROUP, 2 * QK), 1) < QK
    for g in range(pages // GROUP):
        mine = found[g * GROUP : (g + 1) * GROUP]
        both = [jnp.where(side, mine, 0.0), jnp.where(side, 0.0, mine)]
        page_q[2 * g * GROUP : 2 * (g + 1) * GROUP] = jnp.concatenate(both, axis=0).astype(BF16)
    half = slots // 2
    for h in range(2):
        cut = slice(h * half, (h + 1) * half)
        at = info[0:1, cut]
        for ref, lo in ((first_a, 0), (first_b, QK)):
            keys = pool_v[0:SHARED].reshape(SHARED * PAGE, WIDE)[:, lo : lo + QK]
            score = dot_nt(keys, queries[cut, lo : lo + QK])
            kept = score[0:PAGE]
            for p in range(1, SHARED):
                kept = jnp.where(at == float(p), score[p * PAGE : (p + 1) * PAGE], kept)
            ref[:, cut] = kept

    row = iota((2 * GROUP, LANES), 0) % GROUP
    for g in range(pages // GROUP):
        mine = slice(g * GROUP, (g + 1) * GROUP)
        keys = pool_v[mine].reshape(GROUP * PAGE, WIDE)[:, 0 : 2 * QK]
        score = dot_nt(page_q[2 * g * GROUP : 2 * (g + 1) * GROUP], keys)
        chosen = score[:, 0:PAGE]
        for i in range(1, GROUP):
            chosen = jnp.where(row == i, score[:, i * PAGE : (i + 1) * PAGE], chosen)
        priv_a[mine] = chosen[0:GROUP]
        priv_b[mine] = chosen[GROUP:]

    self_in.wait_recv()
    page_best = []
    for ref in (priv_a, priv_b):
        score = jnp.where(times[...] > 0.0, ref[...] * SCALE, NEG)
        ref[...] = score
        page_best.append(jnp.max(score, axis=1, keepdims=True))
    tops, selfs = [], []
    page_top = [jnp.zeros((pages, LANES), F32) for _ in range(2)]
    depth = iota((PAGE, LANES), 0).astype(F32)
    for g in range(blocks):
        cut = slice(g * LANES, (g + 1) * LANES)
        hit = match[:, cut].astype(F32) > 0.0
        got = gather_tiles(recv_s, g)
        valid = depth < info[1:2, cut]
        for m, ref in enumerate((first_a, first_b)):
            score = jnp.where(valid, ref[:, cut] * SCALE, NEG)
            ref[:, cut] = score
            mine = got[3 * m : 3 * m + 1] + got[3 * m + 1 : 3 * m + 2] + got[3 * m + 2 : 3 * m + 3]
            best = jnp.max(jnp.where(hit, page_best[m], NEG), axis=0, keepdims=True)
            top = jnp.maximum(jnp.maximum(jnp.max(score, axis=0, keepdims=True), best), mine)
            page_top[m] = page_top[m] + jnp.where(hit, top, 0.0)
            tops.append(top)
            selfs.append(mine)

    page_sum = []
    for m, ref in enumerate((priv_a, priv_b)):
        top = jnp.sum(page_top[m], axis=1, keepdims=True)
        weight = jnp.where(times[...] > 0.0, jnp.exp2(ref[...] - top) * times[...], 0.0)
        ref[...] = weight
        page_sum.append(jnp.sum(weight, axis=1, keepdims=True))
    page_coef = [jnp.zeros((pages, LANES), F32) for _ in range(2)]
    own_rows = []
    for g in range(blocks):
        cut = slice(g * LANES, (g + 1) * LANES)
        hit = match[:, cut].astype(F32) > 0.0
        mixed, own_coef = None, None
        for m, ref in enumerate((first_a, first_b)):
            top = tops[2 * g + m]
            weight = jnp.exp2(ref[:, cut] - top)
            new = jnp.exp2(selfs[2 * g + m] - top)
            total = (
                new
                + jnp.sum(weight, axis=0, keepdims=True)
                + jnp.sum(jnp.where(hit, page_sum[m], 0.0), axis=0, keepdims=True)
            )
            coef = 1.0 / total if m == 0 else -lam / total
            page_coef[m] = page_coef[m] + jnp.where(hit, coef, 0.0)
            mixed = weight * coef if m == 0 else mixed + weight * coef
            own_coef = new * coef if m == 0 else own_coef + new * coef
        mixed = jnp.transpose(mixed).astype(BF16)
        for p in range(SHARED):
            wide[cut, p * PAGE : (p + 1) * PAGE] = mixed * page0[p, cut]
        own_rows.append(stack_rows(split(own_coef, 2), TILE))
    tiles(jnp.concatenate(own_rows, axis=1), TILE, send_c)
    coef_in = exchange(send_c, recv_c, c_sem)

    priv_a[...] = priv_a[...] * jnp.sum(page_coef[0], axis=1, keepdims=True) + priv_b[
        ...
    ] * jnp.sum(page_coef[1], axis=1, keepdims=True)

    row = iota((GROUP, LANES), 0)
    for g in range(pages // GROUP):
        mine = slice(g * GROUP, (g + 1) * GROUP)
        values = pool_v[mine].reshape(GROUP * PAGE, WIDE)[:, 2 * QK :]
        weight = priv_a[mine]
        spread = jnp.concatenate(
            [jnp.where(row == i, weight, 0.0) for i in range(GROUP)], axis=1
        ).astype(BF16)
        page_out[mine] = dot(spread, values)
    high, low = split(page_out[...], 2)
    pair = jnp.concatenate([high, low], axis=0).astype(BF16)
    values = pool_v[0:SHARED].reshape(SHARED * PAGE, WIDE)[:, 2 * QK :]

    mixed_in = exchange_rows(
        lambda rows: dot(wide[rows], values) + dot(match_t[rows], pair), send_r, recv_r, r_sem
    )
    own_w.wait()
    coef_in.wait_recv()
    rows = jnp.concatenate([gather_tiles(recv_c, g) for g in range(blocks)], axis=1)
    coefs = dot_nt(place_t[...], rows.astype(BF16))
    addend = (coefs[:, 0:1] + coefs[:, 1:2]) * v_new[...].astype(F32)
    mixed_in.wait_recv()
    mixed = dot(place_t[...], recv_r[...].reshape(slots, VDIM)) + addend
    scale = lax.rsqrt(jnp.mean(mixed * mixed, axis=1, keepdims=True) + norm_eps)
    heads[me_h] = (mixed * scale * gain[...] * (1.0 - lambda_init)).astype(BF16)

    started = gather_start(heads, heads.at[me_h], h_send, h_recv)
    weights_in.wait_recv()
    proj[...] = jnp.zeros(proj.shape, F32)

    def add_out(source):
        proj[...] = proj[...] + dot(heads[source], wcol_v[source])

    gather_rest(started, add_out, lambda step: None)
    out[...] = proj[...].astype(BF16)
    for copy in sent:
        copy.wait_send()


def on_device(sizes, tokens, w_in, w_out, gain, lq1, lk1, lq2, lk2, pool, table, length, owner):
    n_tok, n_head, count, features = sizes
    slots = n_tok * CAP
    pages = pool.shape[0]
    vmem = pl.BlockSpec(memory_space=pltpu.VMEM)
    hbm = pl.BlockSpec(memory_space=pltpu.HBM)
    dma = pltpu.SemaphoreType.DMA
    return pl.pallas_call(
        functools.partial(step_kernel, sizes),
        out_shape=pltpu.VMEM((count, features), BF16),
        in_specs=[hbm] * 12,
        out_specs=vmem,
        scratch_shapes=[
            pltpu.VMEM((1, VDIM), F32),
            pltpu.VMEM((1, QK), F32),
            pltpu.VMEM((1, QK), F32),
            pltpu.VMEM((1, QK), F32),
            pltpu.VMEM((1, QK), F32),
            pltpu.VMEM((MAXP, count), jnp.int32),
            pltpu.VMEM((1, count), jnp.int32),
            pltpu.VMEM((1, count), jnp.int32),
            pltpu.VMEM((n_head, count, features), BF16),
            pltpu.VMEM(w_in.shape, BF16),
            pltpu.VMEM((n_head, VDIM, features), BF16),
            pltpu.VMEM((pages, PAGE, WIDE), BF16),
            pltpu.VMEM((n_head, count, VDIM), BF16),
            pltpu.VMEM((slots, count), BF16),
            pltpu.VMEM((count, slots), BF16),
            pltpu.VMEM((PER, LANES, LANES), BF16),
            pltpu.VMEM((count, 2 * QK), F32),
            pltpu.VMEM((count, VDIM), BF16),
            pltpu.VMEM((n_tok, FIELDS, LANES), BF16),
            pltpu.VMEM((n_tok, FIELDS, LANES), BF16),
            pltpu.VMEM((n_tok, CAP, 2 * QK), BF16),
            pltpu.VMEM((n_tok, CAP, 2 * QK), BF16),
            pltpu.VMEM((n_tok, TILE, LANES), BF16),
            pltpu.VMEM((n_tok, TILE, LANES), BF16),
            pltpu.VMEM((n_tok, CAP, VDIM), BF16),
            pltpu.VMEM((n_tok, CAP, VDIM), BF16),
            pltpu.VMEM((n_tok, TILE, LANES), BF16),
            pltpu.VMEM((n_tok, TILE, LANES), BF16),
            pltpu.VMEM((8, slots), F32),
            pltpu.VMEM((pages, slots), BF16),
            pltpu.VMEM((slots, 2 * pages), BF16),
            pltpu.VMEM((pages, PAGE), F32),
            pltpu.VMEM((SHARED, slots, PAGE), BF16),
            pltpu.VMEM((PAGE, slots), F32),
            pltpu.VMEM((PAGE, slots), F32),
            pltpu.VMEM((2 * pages, 2 * QK), BF16),
            pltpu.VMEM((pages, PAGE), F32),
            pltpu.VMEM((pages, PAGE), F32),
            pltpu.VMEM((pages, VDIM), F32),
            pltpu.VMEM((slots, SHARED * PAGE), BF16),
            pltpu.SemaphoreType.REGULAR((3,)),
            dma((12,)),
        ]
        + [dma((number,)) for number in (1, 19, 2, 2, 2, 2, 2, 2, 1, 19)],
        compiler_params=pltpu.CompilerParams(
            collective_id=0, has_side_effects=True, vmem_limit_bytes=60 * 1024 * 1024
        ),
        name="decode_step",
    )(
        tokens,
        w_in,
        w_out,
        pool.reshape(pages, PAGE, WIDE),
        gain.reshape(1, VDIM),
        lq1.reshape(1, QK),
        lk1.reshape(1, QK),
        lq2.reshape(1, QK),
        lk2.reshape(1, QK),
        jnp.transpose(table),
        length.reshape(1, count),
        owner.reshape(1, count),
    )


def solution(mesh):
    n_tok, n_head = mesh.shape["tok"], mesh.shape["head"]

    def run(
        tokens,
        input_weight,
        output_weight,
        head_gain,
        query_lambda_one,
        key_lambda_one,
        query_lambda_two,
        key_lambda_two,
        cache_pool,
        page_table,
        cache_length,
        cache_owner,
    ):
        sizes = (n_tok, n_head, tokens.shape[0] // n_tok, tokens.shape[1] // n_head)
        placed = (
            P("tok", "head"),
            P(None, "head"),
            P("head", None),
            P("head"),
            P(),
            P(),
            P(),
            P(),
            P("tok", "head", None, None),
            P("tok", None),
            P("tok"),
            P("tok", None),
        )
        return jax.shard_map(
            functools.partial(on_device, sizes),
            mesh=mesh,
            in_specs=placed,
            out_specs=P("tok", "head"),
            check_vma=False,
        )(
            tokens,
            input_weight,
            output_weight,
            head_gain,
            query_lambda_one,
            key_lambda_one,
            query_lambda_two,
            key_lambda_two,
            cache_pool,
            page_table,
            cache_length,
            cache_owner,
        )

    return run
```

```python
import functools
import math

import jax
import jax.numpy as jnp
from jax import lax
from jax.experimental import pallas as pl
from jax.experimental.pallas import tpu as pltpu
from jax.sharding import PartitionSpec as P

QK = 128
VDIM = 256
PAGE = 128
CAP = 32
SHARED = 8
MAXP = 8
GROUP = 8
LANES = 128
FIELDS = 16
TILE = 8
PER = LANES // CAP
WIDE = 2 * QK + VDIM

lambda_init = 0.8
norm_eps = 1e-05
NEG = -1e30
SCALE = math.log2(math.e) / math.sqrt(QK)
MESH = pl.DeviceIdType.MESH
F32 = jnp.float32
BF16 = jnp.bfloat16


def iota(shape, dim):
    return lax.broadcasted_iota(jnp.int32, shape, dim)


def one_hot(condition):
    return condition.astype(F32).astype(BF16)


def dot(a, b):
    return jnp.dot(a, b, preferred_element_type=F32)


def dot_nt(a, b):
    return lax.dot_general(a, b, (((1,), (1,)), ((), ())), preferred_element_type=F32)


def split(value, terms):
    parts = []
    for _ in range(terms - 1):
        high = value.astype(BF16).astype(F32)
        parts.append(high)
        value = value - high
    return parts + [value]


def stack_rows(rows, height):
    row = iota((height, rows[0].shape[1]), 0)
    stacked = jnp.where(row == 0, rows[0], 0.0)
    for index in range(1, len(rows)):
        stacked = jnp.where(row == index, rows[index], stacked)
    return stacked


def step_kernel(
    sizes,
    tokens,
    w_in,
    w_out,
    pool,
    gain_h,
    lq1_h,
    lk1_h,
    lq2_h,
    lk2_h,
    table_h,
    length_h,
    owner_h,
    out,
    gain,
    lq1,
    lk1,
    lq2,
    lk2,
    table,
    length,
    owner,
    x,
    win_v,
    wcol_v,
    pool_v,
    heads,
    place,
    place_t,
    turn,
    proj,
    v_new,
    send_m,
    recv_m,
    send_q,
    recv_q,
    send_s,
    recv_s,
    send_r,
    recv_r,
    send_c,
    recv_c,
    info,
    match,
    match_t,
    times,
    page0,
    first_a,
    first_b,
    page_q,
    priv_a,
    priv_b,
    page_out,
    wide,
    greet_sem,
    local_sem,
    x_send,
    x_recv,
    m_sem,
    q_sem,
    s_sem,
    w_sem,
    c_sem,
    r_sem,
    h_send,
    h_recv,
):
    n_tok, n_head, count, features = sizes
    slots = n_tok * CAP
    blocks = slots // LANES
    pages = pool.shape[0]
    ny = n_head // 2
    nx = 4
    nz = n_tok // nx
    me_t = lax.axis_index("tok")
    me_h = lax.axis_index("head")
    y, core = me_h // 2, me_h % 2
    z_at, x_at = me_t // nx, me_t % nx
    up, down, far = (y + 1) % ny, (y + ny - 1) % ny, (y + 2) % ny
    sib = y * 2 + 1 - core
    h_up, h_down, h_far = up * 2 + core, down * 2 + core, far * 2 + core
    a_up, a_down, a_far = up * 2 + 1 - core, down * 2 + 1 - core, far * 2 + 1 - core

    offsets = [(dz, dx) for dz in range(nz) for dx in range(nx) if dz + dx > 0]
    offsets.sort(key=lambda o: -(min(o[0], nz - o[0]) + min(o[1], nx - o[1])))
    peers = [((z_at + dz) % nz) * nx + (x_at + dx) % nx for dz, dx in offsets]

    barrier = pltpu.get_barrier_semaphore()
    x_near = [z_at * nx + (x_at + d) % nx for d in (1, nx - 1)]
    z_near = [(z_at + d) % nz * nx + x_at for d in (1, nz - 1)]
    for peer in (sib, h_up, h_down):
        pl.semaphore_signal(barrier, inc=1, device_id=(me_t, peer), device_id_type=MESH)
    for peer in x_near + z_near:
        pl.semaphore_signal(barrier, inc=1, device_id=(peer, me_h), device_id_type=MESH)

    def greet(step):
        if step > 0:
            pl.semaphore_wait(greet_sem.at[step - 1], 2)
        if step < 3:
            for peer in (x_near, z_near, z_near)[step]:
                pl.semaphore_signal(
                    greet_sem.at[step], inc=1, device_id=(peer, me_h), device_id_type=MESH
                )

    sent = []

    def remote(source, target, send_sem, recv_sem, device):
        copy = pltpu.make_async_remote_copy(
            src_ref=source,
            dst_ref=target,
            send_sem=send_sem,
            recv_sem=recv_sem,
            device_id=device,
            device_id_type=MESH,
        )
        copy.start()
        return copy

    def bulk(source, target, blocks_of, send_sem, recv_sem):
        some = pl.ds(0, blocks_of)
        copy = pltpu.make_async_remote_copy(
            src_ref=source.at[some],
            dst_ref=target.at[some],
            send_sem=send_sem,
            recv_sem=recv_sem,
            device_id=(me_t, sib),
            device_id_type=MESH,
        )
        sent.append(copy)
        return copy

    def exchange(source, target, sems):
        for p in peers:
            remote(source.at[p], target.at[me_t], sems.at[0], sems.at[1], (p, me_h))
        target[me_t] = source[me_t]
        return bulk(source, target, len(peers), sems.at[0], sems.at[1])

    def exchange_rows(make, source, target, sems):
        for dz in sorted(range(nz), key=lambda d: -min(d, nz - d)):
            zz = (z_at + dz) % nz
            rows = pl.ds(pl.multiple_of(zz * nx * CAP, nx * CAP), nx * CAP)
            source[pl.ds(zz * nx, nx)] = make(rows).astype(BF16).reshape((nx,) + source.shape[1:])
            for dx in sorted(range(nx), key=lambda d: -min(d, nx - d)):
                if dz + dx > 0:
                    p = zz * nx + (x_at + dx) % nx
                    remote(source.at[p], target.at[me_t], sems.at[0], sems.at[1], (p, me_h))
        target[me_t] = source[me_t]
        return bulk(source, target, len(peers), sems.at[0], sems.at[1])

    pl.semaphore_wait(barrier, 3 + len(x_near) + len(z_near))

    quarter = count // 4

    def gather_start(buffer, mine, send_sem, recv_sem):
        def go(index, source, start, quarters, target):
            rows = pl.ds(start * quarter, quarters * quarter)
            part = buffer.at[source, rows]
            origin = mine.at[rows] if source is me_h else part
            return remote(origin, part, send_sem.at[0], recv_sem.at[index], (me_t, target))

        copies = [
            go(0, me_h, 0, 1, h_up),
            go(1, me_h, 3, 1, h_down),
            go(2, me_h, 1, 1, h_up),
            go(3, me_h, 2, 1, h_down),
            go(4, me_h, 2, 2, h_up),
            go(5, me_h, 0, 2, h_down),
            go(6, me_h, 0, 4, sib),
        ]
        bulk(buffer, buffer, n_head - 1, send_sem.at[0], recv_sem.at[0])
        return go, copies

    def gather_rest(started, add, beside):
        go, copies = started
        crossed = []
        for k, (source, start, target) in enumerate(
            ((h_down, 0, h_up), (h_up, 3, h_down), (h_down, 1, h_up), (h_up, 2, h_down))
        ):
            copies[k].wait_recv()
            copies.append(go(7 + k, source, start, 1, target))
            if k >= 2:
                crossed.append(go(15 + k, source, start, 1, (a_up, a_down)[k - 2]))
        copies.append(go(11, h_down, 0, 2, sib))
        copies.append(go(12, h_up, 2, 2, sib))
        beside(1)
        add(me_h)
        copies[6].wait_recv()
        add(sib)
        copies[4].wait_recv()
        copies.append(go(13, h_down, 2, 2, sib))
        add(h_down)
        copies[5].wait_recv()
        copies.append(go(14, h_up, 0, 2, sib))
        add(h_up)
        beside(2)
        copies[11].wait_recv()
        copies[13].wait_recv()
        add(a_down)
        copies[12].wait_recv()
        copies[14].wait_recv()
        add(a_up)
        for k, start in enumerate((0, 3)):
            copies[7 + k].wait_recv()
            copies.append(go(15 + k, h_far, start, 1, sib))
        beside(3)
        copies[9].wait_recv()
        copies[10].wait_recv()
        add(h_far)
        for copy in copies[15:] + crossed:
            copy.wait_recv()
        add(a_far)

    def tiles(rows, height, target):
        groups = jnp.concatenate(
            [rows[:, g * LANES : (g + 1) * LANES] for g in range(blocks)], axis=0
        ).astype(BF16)
        for b in range(PER):
            moved = dot(groups, turn[b]).astype(BF16)
            for g in range(blocks):
                target[g * PER + b] = moved[g * height : (g + 1) * height]

    def gather_tiles(source, g):
        total = source[g * PER].astype(F32)
        for b in range(1, PER):
            total = total + source[g * PER + b].astype(F32)
        return total

    started = gather_start(x, tokens, x_send, x_recv)
    greet(0)
    local_x = pltpu.make_async_copy(tokens, x.at[me_h], local_sem.at[0])
    local_x.start()
    load_win = pltpu.make_async_copy(w_in, win_v, local_sem.at[1])
    load_win.start()

    small = [
        pltpu.make_async_copy(source, target, local_sem.at[4 + k])
        for k, (source, target) in enumerate(
            (
                (owner_h, owner),
                (table_h, table),
                (length_h, length),
                (gain_h, gain),
                (lq1_h, lq1),
                (lk1_h, lk1),
                (lq2_h, lq2),
                (lk2_h, lk2),
            )
        )
    ]
    for load in small:
        load.start()

    def prepare():
        for load in small:
            load.wait()
        own = owner[...]
        named = own == iota((n_tok, count), 0)
        earlier = one_hot(iota((count, count), 0) < iota((count, count), 1))
        before = dot(one_hot(named), earlier)
        rank = jnp.sum(jnp.where(named, before, 0.0), axis=0, keepdims=True)
        slot = own * CAP + rank.astype(jnp.int32)
        eye = iota((count, count), 0) == iota((count, count), 1)
        slot_c = jnp.sum(jnp.where(eye, slot, 0), axis=1, keepdims=True)
        place[...] = one_hot(iota((slots, count), 0) == slot)
        place_t[...] = one_hot(iota((count, slots), 1) == slot_c)
        shift = (me_t % PER) * CAP
        for b in range(PER):
            source_lane = iota((LANES, LANES), 0)
            moved = source_lane - b * CAP + shift == iota((LANES, LANES), 1)
            turn[b] = one_hot(moved & (source_lane // CAP == b))

        lengths = length[...]
        ends = stack_rows([(lengths // 8).astype(F32), (lengths % 8).astype(F32)], 8)
        fields = jnp.concatenate([table[...].astype(F32), ends], axis=0).astype(BF16)
        tiles(dot(fields, place_t[...]), FIELDS, send_m)

    def add_query(source):
        rows = pl.ds(pl.multiple_of(source * features, features), features)
        proj[...] = proj[...] + dot(x[source], win_v[rows, 0 : 2 * QK])

    proj[...] = jnp.zeros(proj.shape, F32)
    load_pool = pltpu.make_async_copy(pool, pool_v, local_sem.at[2])
    arriving = []

    def beside_gather(step):
        greet(step)
        if step == 1:
            prepare()
            local_x.wait()
            load_win.wait()
            load_pool.start()
        elif step == 3:
            arriving.append(exchange(send_m, recv_m, m_sem))

    gather_rest(started, add_query, beside_gather)

    query = proj[...].astype(BF16)
    query_in = exchange_rows(lambda rows: dot(place[rows], query), send_q, recv_q, q_sem)

    fresh = jnp.zeros((count, 2 * QK + VDIM), F32)
    for h in range(n_head):
        fresh = fresh + dot(x[h], win_v[h * features : (h + 1) * features, 2 * QK :])
    fresh = fresh.astype(BF16)
    v_new[...] = fresh[:, 2 * QK :]
    product = query.astype(F32) * fresh[:, 0 : 2 * QK].astype(F32)
    high, low = split(product, 2)
    ones = jnp.ones((8, QK), F32).astype(BF16)
    terms = []
    for m in range(2):
        part = slice(m * QK, (m + 1) * QK)
        total = dot_nt(ones, high[:, part].astype(BF16)) + dot_nt(ones, low[:, part].astype(BF16))
        terms += split(total[0:1] * SCALE, 3)
    tiles(dot(stack_rows(terms, TILE).astype(BF16), place_t[...]), TILE, send_s)
    self_in = exchange(send_s, recv_s, s_sem)

    def columns(h):
        return w_out.at[:, pl.ds(pl.multiple_of(h * features, features), features)]

    own_w = pltpu.make_async_copy(columns(me_h), wcol_v.at[me_h], local_sem.at[3])
    own_w.start()
    for h in (h_up, h_down, h_far, a_up, a_down, a_far, sib):
        remote(columns(h), wcol_v.at[me_h], w_sem.at[0], w_sem.at[1], (me_t, h))
    weights_in = bulk(wcol_v, wcol_v, n_head - 1, w_sem.at[0], w_sem.at[1])
    lam = (
        jnp.exp(jnp.sum(lq1[...] * lk1[...], axis=1, keepdims=True))
        - jnp.exp(jnp.sum(lq2[...] * lk2[...], axis=1, keepdims=True))
        + lambda_init
    )

    arriving[0].wait_recv()
    whole = jnp.zeros((pages, LANES), F32)
    rest = jnp.zeros((pages, LANES), F32)
    page = iota((pages, LANES), 0).astype(F32)
    for g in range(blocks):
        cut = slice(g * LANES, (g + 1) * LANES)
        got = gather_tiles(recv_m, g)
        cached = got[8:9] * 8.0 + got[9:10]
        info[0:1, cut] = got[0:1]
        info[1:2, cut] = cached
        hit_any = jnp.zeros((pages, LANES), F32)
        for j in range(1, MAXP):
            left = cached - float(PAGE * j)
            number = jnp.where(left > 0.0, got[j : j + 1], -1.0)
            hit = number == page
            hit_any = jnp.where(hit, 1.0, hit_any)
            whole = whole + jnp.where(hit, jnp.where(left >= float(PAGE), 1.0, 0.0), 0.0)
            rest = rest + jnp.where(hit, jnp.where(left >= float(PAGE), 0.0, left), 0.0)
        match[:, cut] = hit_any.astype(BF16)
        match_t[cut] = jnp.transpose(jnp.concatenate([hit_any, hit_any], axis=0)).astype(BF16)
        chosen = jnp.transpose(jnp.broadcast_to(got[0:1], (LANES, LANES)))
        for p in range(SHARED):
            page0[p, cut] = one_hot(chosen == float(p))
    whole = jnp.sum(whole, axis=1, keepdims=True)
    rest = jnp.sum(rest, axis=1, keepdims=True)
    position = iota((pages, PAGE), 1).astype(F32)
    times[...] = whole + jnp.where(position < rest, 1.0, 0.0)
    load_pool.wait()
    query_in.wait_recv()

    queries = recv_q[...].reshape(slots, 2 * QK)
    found = dot(match[...], queries)
    side = iota((GROUP, 2 * QK), 1) < QK
    for g in range(pages // GROUP):
        mine = found[g * GROUP : (g + 1) * GROUP]
        both = [jnp.where(side, mine, 0.0), jnp.where(side, 0.0, mine)]
        page_q[2 * g * GROUP : 2 * (g + 1) * GROUP] = jnp.concatenate(both, axis=0).astype(BF16)
    half = slots // 2
    for h in range(2):
        cut = slice(h * half, (h + 1) * half)
        at = info[0:1, cut]
        for ref, lo in ((first_a, 0), (first_b, QK)):
            keys = pool_v[0:SHARED].reshape(SHARED * PAGE, WIDE)[:, lo : lo + QK]
            score = dot_nt(keys, queries[cut, lo : lo + QK])
            kept = score[0:PAGE]
            for p in range(1, SHARED):
                kept = jnp.where(at == float(p), score[p * PAGE : (p + 1) * PAGE], kept)
            ref[:, cut] = kept

    row = iota((2 * GROUP, LANES), 0) % GROUP
    for g in range(pages // GROUP):
        mine = slice(g * GROUP, (g + 1) * GROUP)
        keys = pool_v[mine].reshape(GROUP * PAGE, WIDE)[:, 0 : 2 * QK]
        score = dot_nt(page_q[2 * g * GROUP : 2 * (g + 1) * GROUP], keys)
        chosen = score[:, 0:PAGE]
        for i in range(1, GROUP):
            chosen = jnp.where(row == i, score[:, i * PAGE : (i + 1) * PAGE], chosen)
        priv_a[mine] = chosen[0:GROUP]
        priv_b[mine] = chosen[GROUP:]

    self_in.wait_recv()
    page_best = []
    for ref in (priv_a, priv_b):
        score = jnp.where(times[...] > 0.0, ref[...] * SCALE, NEG)
        ref[...] = score
        page_best.append(jnp.max(score, axis=1, keepdims=True))
    tops, selfs = [], []
    page_top = [jnp.zeros((pages, LANES), F32) for _ in range(2)]
    depth = iota((PAGE, LANES), 0).astype(F32)
    for g in range(blocks):
        cut = slice(g * LANES, (g + 1) * LANES)
        hit = match[:, cut].astype(F32) > 0.0
        got = gather_tiles(recv_s, g)
        valid = depth < info[1:2, cut]
        for m, ref in enumerate((first_a, first_b)):
            score = jnp.where(valid, ref[:, cut] * SCALE, NEG)
            ref[:, cut] = score
            mine = got[3 * m : 3 * m + 1] + got[3 * m + 1 : 3 * m + 2] + got[3 * m + 2 : 3 * m + 3]
            best = jnp.max(jnp.where(hit, page_best[m], NEG), axis=0, keepdims=True)
            top = jnp.maximum(jnp.maximum(jnp.max(score, axis=0, keepdims=True), best), mine)
            page_top[m] = page_top[m] + jnp.where(hit, top, 0.0)
            tops.append(top)
            selfs.append(mine)

    page_sum = []
    for m, ref in enumerate((priv_a, priv_b)):
        top = jnp.sum(page_top[m], axis=1, keepdims=True)
        weight = jnp.where(times[...] > 0.0, jnp.exp2(ref[...] - top) * times[...], 0.0)
        ref[...] = weight
        page_sum.append(jnp.sum(weight, axis=1, keepdims=True))
    page_coef = [jnp.zeros((pages, LANES), F32) for _ in range(2)]
    own_rows = []
    for g in range(blocks):
        cut = slice(g * LANES, (g + 1) * LANES)
        hit = match[:, cut].astype(F32) > 0.0
        mixed, own_coef = None, None
        for m, ref in enumerate((first_a, first_b)):
            top = tops[2 * g + m]
            weight = jnp.exp2(ref[:, cut] - top)
            new = jnp.exp2(selfs[2 * g + m] - top)
            total = (
                new
                + jnp.sum(weight, axis=0, keepdims=True)
                + jnp.sum(jnp.where(hit, page_sum[m], 0.0), axis=0, keepdims=True)
            )
            coef = 1.0 / total if m == 0 else -lam / total
            page_coef[m] = page_coef[m] + jnp.where(hit, coef, 0.0)
            mixed = weight * coef if m == 0 else mixed + weight * coef
            own_coef = new * coef if m == 0 else own_coef + new * coef
        mixed = jnp.transpose(mixed).astype(BF16)
        for p in range(SHARED):
            wide[cut, p * PAGE : (p + 1) * PAGE] = mixed * page0[p, cut]
        own_rows.append(stack_rows(split(own_coef, 2), TILE))
    tiles(jnp.concatenate(own_rows, axis=1), TILE, send_c)
    coef_in = exchange(send_c, recv_c, c_sem)

    priv_a[...] = priv_a[...] * jnp.sum(page_coef[0], axis=1, keepdims=True) + priv_b[
        ...
    ] * jnp.sum(page_coef[1], axis=1, keepdims=True)

    row = iota((GROUP, LANES), 0)
    for g in range(pages // GROUP):
        mine = slice(g * GROUP, (g + 1) * GROUP)
        values = pool_v[mine].reshape(GROUP * PAGE, WIDE)[:, 2 * QK :]
        weight = priv_a[mine]
        spread = jnp.concatenate(
            [jnp.where(row == i, weight, 0.0) for i in range(GROUP)], axis=1
        ).astype(BF16)
        page_out[mine] = dot(spread, values)
    high, low = split(page_out[...], 2)
    pair = jnp.concatenate([high, low], axis=0).astype(BF16)
    values = pool_v[0:SHARED].reshape(SHARED * PAGE, WIDE)[:, 2 * QK :]

    mixed_in = exchange_rows(
        lambda rows: dot(wide[rows], values) + dot(match_t[rows], pair), send_r, recv_r, r_sem
    )
    own_w.wait()
    coef_in.wait_recv()
    rows = jnp.concatenate([gather_tiles(recv_c, g) for g in range(blocks)], axis=1)
    coefs = dot_nt(place_t[...], rows.astype(BF16))
    addend = (coefs[:, 0:1] + coefs[:, 1:2]) * v_new[...].astype(F32)
    mixed_in.wait_recv()
    mixed = dot(place_t[...], recv_r[...].reshape(slots, VDIM)) + addend
    scale = lax.rsqrt(jnp.mean(mixed * mixed, axis=1, keepdims=True) + norm_eps)
    heads[me_h] = (mixed * scale * gain[...] * (1.0 - lambda_init)).astype(BF16)

    started = gather_start(heads, heads.at[me_h], h_send, h_recv)
    weights_in.wait_recv()
    proj[...] = jnp.zeros(proj.shape, F32)

    def add_out(source):
        proj[...] = proj[...] + dot(heads[source], wcol_v[source])

    gather_rest(started, add_out, lambda step: None)
    out[...] = proj[...].astype(BF16)
    for copy in sent:
        copy.wait_send()


def on_device(sizes, tokens, w_in, w_out, gain, lq1, lk1, lq2, lk2, pool, table, length, owner):
    n_tok, n_head, count, features = sizes
    slots = n_tok * CAP
    pages = pool.shape[0]
    vmem = pl.BlockSpec(memory_space=pltpu.VMEM)
    hbm = pl.BlockSpec(memory_space=pltpu.HBM)
    dma = pltpu.SemaphoreType.DMA
    return pl.pallas_call(
        functools.partial(step_kernel, sizes),
        out_shape=pltpu.VMEM((count, features), BF16),
        in_specs=[hbm] * 12,
        out_specs=vmem,
        scratch_shapes=[
            pltpu.VMEM((1, VDIM), F32),
            pltpu.VMEM((1, QK), F32),
            pltpu.VMEM((1, QK), F32),
            pltpu.VMEM((1, QK), F32),
            pltpu.VMEM((1, QK), F32),
            pltpu.VMEM((MAXP, count), jnp.int32),
            pltpu.VMEM((1, count), jnp.int32),
            pltpu.VMEM((1, count), jnp.int32),
            pltpu.VMEM((n_head, count, features), BF16),
            pltpu.VMEM(w_in.shape, BF16),
            pltpu.VMEM((n_head, VDIM, features), BF16),
            pltpu.VMEM((pages, PAGE, WIDE), BF16),
            pltpu.VMEM((n_head, count, VDIM), BF16),
            pltpu.VMEM((slots, count), BF16),
            pltpu.VMEM((count, slots), BF16),
            pltpu.VMEM((PER, LANES, LANES), BF16),
            pltpu.VMEM((count, 2 * QK), F32),
            pltpu.VMEM((count, VDIM), BF16),
            pltpu.VMEM((n_tok, FIELDS, LANES), BF16),
            pltpu.VMEM((n_tok, FIELDS, LANES), BF16),
            pltpu.VMEM((n_tok, CAP, 2 * QK), BF16),
            pltpu.VMEM((n_tok, CAP, 2 * QK), BF16),
            pltpu.VMEM((n_tok, TILE, LANES), BF16),
            pltpu.VMEM((n_tok, TILE, LANES), BF16),
            pltpu.VMEM((n_tok, CAP, VDIM), BF16),
            pltpu.VMEM((n_tok, CAP, VDIM), BF16),
            pltpu.VMEM((n_tok, TILE, LANES), BF16),
            pltpu.VMEM((n_tok, TILE, LANES), BF16),
            pltpu.VMEM((8, slots), F32),
            pltpu.VMEM((pages, slots), BF16),
            pltpu.VMEM((slots, 2 * pages), BF16),
            pltpu.VMEM((pages, PAGE), F32),
            pltpu.VMEM((SHARED, slots, PAGE), BF16),
            pltpu.VMEM((PAGE, slots), F32),
            pltpu.VMEM((PAGE, slots), F32),
            pltpu.VMEM((2 * pages, 2 * QK), BF16),
            pltpu.VMEM((pages, PAGE), F32),
            pltpu.VMEM((pages, PAGE), F32),
            pltpu.VMEM((pages, VDIM), F32),
            pltpu.VMEM((slots, SHARED * PAGE), BF16),
            pltpu.SemaphoreType.REGULAR((3,)),
            dma((12,)),
        ]
        + [dma((number,)) for number in (1, 19, 2, 2, 2, 2, 2, 2, 1, 19)],
        compiler_params=pltpu.CompilerParams(
            collective_id=0, has_side_effects=True, vmem_limit_bytes=60 * 1024 * 1024
        ),
        name="decode_step",
    )(
        tokens,
        w_in,
        w_out,
        pool.reshape(pages, PAGE, WIDE),
        gain.reshape(1, VDIM),
        lq1.reshape(1, QK),
        lk1.reshape(1, QK),
        lq2.reshape(1, QK),
        lk2.reshape(1, QK),
        jnp.transpose(table),
        length.reshape(1, count),
        owner.reshape(1, count),
    )


def solution(mesh):
    n_tok, n_head = mesh.shape["tok"], mesh.shape["head"]

    def run(
        tokens,
        input_weight,
        output_weight,
        head_gain,
        query_lambda_one,
        key_lambda_one,
        query_lambda_two,
        key_lambda_two,
        cache_pool,
        page_table,
        cache_length,
        cache_owner,
    ):
        sizes = (n_tok, n_head, tokens.shape[0] // n_tok, tokens.shape[1] // n_head)
        placed = (
            P("tok", "head"),
            P(None, "head"),
            P("head", None),
            P("head"),
            P(),
            P(),
            P(),
            P(),
            P("tok", "head", None, None),
            P("tok", None),
            P("tok"),
            P("tok", None),
        )
        return jax.shard_map(
            functools.partial(on_device, sizes),
            mesh=mesh,
            in_specs=placed,
            out_specs=P("tok", "head"),
            check_vma=False,
        )(
            tokens,
            input_weight,
            output_weight,
            head_gain,
            query_lambda_one,
            key_lambda_one,
            query_lambda_two,
            key_lambda_two,
            cache_pool,
            page_table,
            cache_length,
            cache_owner,
        )

    return run
```
